256 devices in a mesh: row: 32 (over y, x, core), col: 8 (over z).
Axes of the slice: x: 4, y: 4, z: 8, core: 2. Of those that a mesh axis runs over, the one named last changes fastest.
Arguments:
- queries: bfloat16 [4096, 32, 128], P('row', 'col'), may hold values from -96 to 96
- keys: bfloat16 [4096, 32, 128], P('row', 'col'), may hold values from -6 to 6
- values: bfloat16 [4096, 32, 128], P('row', 'col'), may hold values from -6 to 6
- out_grad: bfloat16 [4096, 32, 128], P('row', 'col'), may hold values from -24 to 24
- row_keep: int32 [4096], P('row'), may hold values 0 or 1
- row_lengths: int32 [4096], P('row'), may hold values from 8 to 32, as said below
Outputs:
- dq: bfloat16 [4096, 32, 128], P('row', 'col')
- dk: bfloat16 [4096, 32, 128], P('row', 'col')
- dv: bfloat16 [4096, 32, 128], P('row', 'col')
The draws below stay inside these ranges and needn't reach their ends.
Inputs may be any that keep to these rules, and one draw needn't show every extreme that they name: Row r's cells in columns below row_lengths[r] are valid.
All inputs are finite; a program needn't handle non-finite values. No bound on the sum of `row_keep` on one device may be relied on, other than what follows from the above.
Results may differ from the reference program's by a relative error of at most 0.035.
Values may be sent and summed in bfloat16 or wider, within the bound.
No kernel may reach another device: no remote copies, remote signals or barrier semaphores. Data moves between devices by JAX's collectives and lax.ppermute only.
A program may use at most 64 MiB of HBM per device.

```python
import math
import jax
import jax.numpy as jnp
from jax import lax

WIDTH = 128
SUMMARIES = 256
ROWS = 4096
COLS = 32
GROUP_ROWS = 16


def draw_queries(key, part):
    drawn = jax.random.normal(jax.random.fold_in(key, 21), (ROWS, COLS, WIDTH), jnp.float32)
    result_table = 2.0 * jnp.clip(drawn, -6.0, 6.0)
    return result_table.astype(jnp.bfloat16)


def draw_keys(key, part):
    drawn = jax.random.normal(jax.random.fold_in(key, 41), (ROWS, COLS, WIDTH), jnp.float32)
    result_table = jnp.clip(drawn, -6.0, 6.0)
    return result_table.astype(jnp.bfloat16)


def draw_row_lengths(key, part):
    lengths_drawn = jax.random.randint(jax.random.fold_in(key, 31), (ROWS,), COLS // 4, COLS + 1)
    chosen = jax.random.randint(jax.random.fold_in(key, 32), (), 0, ROWS)
    row_ids = jnp.arange(ROWS, dtype=jnp.int32)
    return jnp.where(row_ids == chosen, COLS, lengths_drawn).astype(jnp.int32)


def plant(entries, key, smallest, largest):
    longest = entries.shape.index(max(entries.shape))
    spots = []
    for shift in (0, 1):
        where = [jax.random.randint(jax.random.fold_in(key, axis), (), 0, length) for axis, length in enumerate(entries.shape)]
        where[longest] = (where[longest] + shift) % entries.shape[longest]
        spots.append(tuple(where))
    return entries.at[spots[0]].set(smallest).at[spots[1]].set(largest)


def level_of(stream_key, dims, split, least, largest):
    level, own = 1.0, jax.random.fold_in(stream_key, 6)
    for dim, blocks in split:
        steps = jnp.exp(jax.random.uniform(jax.random.fold_in(own, dim), (blocks,), jnp.float32, least / len(split), largest / len(split)))
        level = level * jnp.repeat(steps, dims[dim] // blocks).reshape([-1 if axis == dim else 1 for axis in range(len(dims))])
    return level


def scatter_about(stream_key, shape, width, limit, split=(), kind=jnp.bfloat16):
    values = jax.random.normal(stream_key, shape, jnp.float32) * width
    if len(split) > 0:
        values = level_of(stream_key, shape, split, -0.22, 0.18) * values
    return jnp.clip(values, min=-limit, max=limit).astype(kind)


def setup_inputs(seed: int = 0) -> dict:
    streams_of = jax.random.split(jax.random.key(seed), 7)
    queries = draw_queries(jax.random.fold_in(streams_of[6], 71), 0)
    keys = draw_keys(jax.random.fold_in(streams_of[6], 71), 0)
    values = scatter_about(streams_of[2], (ROWS, COLS, WIDTH), 1.0, 6.0, ((0, 32), (1, 8)))
    out_grad = scatter_about(streams_of[3], (ROWS, COLS, WIDTH), 4.0, 24.0, ((0, 32), (1, 8)))
    row_keep = plant((jax.random.randint(streams_of[4], (ROWS,), 0, 8) < 7).astype(jnp.int32), jax.random.fold_in(streams_of[4], 1), 0, 1)
    row_lengths = draw_row_lengths(jax.random.fold_in(streams_of[6], 71), 0)
    return dict(queries=queries, keys=keys, values=values, out_grad=out_grad, row_keep=row_keep, row_lengths=row_lengths)


def blank_cells(table, cell_keep):
    return jnp.where(cell_keep, table, jnp.zeros((), table.dtype))

def softmax_rows(logits):
    row_peak = lax.optimization_barrier(jnp.max(logits, axis=-1, keepdims=True))
    lifted = jnp.exp(logits - row_peak)
    return lifted / lax.optimization_barrier(jnp.sum(lifted, axis=-1, keepdims=True))

def reference(queries, keys, values, out_grad, row_keep, row_lengths):
    column_ids = jnp.arange(COLS, dtype=jnp.int32)
    cell_keep = ((row_keep[:, None] == 1) & (column_ids[None, :] < row_lengths[:, None]))[:, :, None]
    q_masked = blank_cells(queries, cell_keep)
    k_masked = blank_cells(keys, cell_keep)
    v_masked = blank_cells(values, cell_keep)
    g_masked = blank_cells(out_grad, cell_keep)
    flat_width = COLS * WIDTH
    q_flat = q_masked.reshape(ROWS, flat_width)
    k_flat = k_masked.reshape(ROWS, flat_width)
    v_flat = v_masked.reshape(ROWS, flat_width)
    g_flat = g_masked.reshape(ROWS, flat_width)
    logit_scale = 1.0 / math.sqrt(COLS * WIDTH)
    logits = jnp.dot(q_flat, k_flat.T, preferred_element_type=jnp.float32) * logit_scale
    logits = jnp.where(row_keep[None, :] == 1, logits, -1e+30)
    probs = softmax_rows(logits)
    prob_bf = probs.astype(jnp.bfloat16)
    dprobs = jnp.dot(g_flat, v_flat.T, preferred_element_type=jnp.float32)
    row_delta = lax.optimization_barrier(jnp.sum(prob_bf.astype(jnp.float32) * dprobs, axis=1, keepdims=True))
    dlogit_bf = (logit_scale * probs * (dprobs - row_delta)).astype(jnp.bfloat16)
    dq_rows = jnp.dot(dlogit_bf, k_flat, preferred_element_type=jnp.float32)
    dk_rows = jnp.dot(dlogit_bf.T, q_flat, preferred_element_type=jnp.float32)
    dv_rows = jnp.dot(prob_bf.T, g_flat, preferred_element_type=jnp.float32)
    key_sums = lax.optimization_barrier(jnp.sum(k_masked.astype(jnp.float32).reshape(SUMMARIES, GROUP_ROWS, COLS, WIDTH), axis=1))
    value_sums = lax.optimization_barrier(jnp.sum(v_masked.astype(jnp.float32).reshape(SUMMARIES, GROUP_ROWS, COLS, WIDTH), axis=1))
    summary_keys = (key_sums / GROUP_ROWS).astype(jnp.bfloat16)
    summary_values = (value_sums / GROUP_ROWS).astype(jnp.bfloat16)
    inv_root = 1.0 / math.sqrt(WIDTH)
    q_float = q_masked.astype(jnp.float32)
    g_float = g_masked.astype(jnp.float32)
    sk_float = summary_keys.astype(jnp.float32)
    sv_float = summary_values.astype(jnp.float32)
    cross_logits = jnp.einsum('rcd,scd->crs', q_float, sk_float) * inv_root
    cross_probs = softmax_rows(cross_logits)
    cross_bf = cross_probs.astype(jnp.bfloat16)
    cross_dprobs = jnp.einsum('rcd,scd->crs', g_float, sv_float)
    cross_delta = lax.optimization_barrier(jnp.sum(cross_bf.astype(jnp.float32) * cross_dprobs, axis=-1, keepdims=True))
    cross_dlogit = (inv_root * cross_probs * (cross_dprobs - cross_delta)).astype(jnp.bfloat16)
    dlogit_float = cross_dlogit.astype(jnp.float32)
    dq_cross = jnp.einsum('crs,scd->rcd', dlogit_float, sk_float)
    dsum_keys = jnp.einsum('crs,rcd->scd', dlogit_float, q_float)
    dsum_values = jnp.einsum('crs,rcd->scd', cross_bf.astype(jnp.float32), g_float)
    spread_keys = jnp.repeat(dsum_keys, GROUP_ROWS, axis=0) / GROUP_ROWS
    spread_values = jnp.repeat(dsum_values, GROUP_ROWS, axis=0) / GROUP_ROWS
    grad_q = jnp.where(cell_keep, dq_rows.reshape(ROWS, COLS, WIDTH) + dq_cross, 0.0).astype(jnp.bfloat16)
    grad_k = jnp.where(cell_keep, dk_rows.reshape(ROWS, COLS, WIDTH) + spread_keys, 0.0).astype(jnp.bfloat16)
    grad_v = jnp.where(cell_keep, dv_rows.reshape(ROWS, COLS, WIDTH) + spread_values, 0.0).astype(jnp.bfloat16)
    return (grad_q, grad_k, grad_v)
```

```python
import math

import jax
import jax.numpy as jnp
from jax import lax
from jax.sharding import PartitionSpec as P

SUMMARIES = 256
BLOCKS = 8

ROW_PAIR = (((1,), (1,)), ((), ()))
LEAD_PAIR = (((0,), (0,)), ((), ()))


def dot_f32(left, right, dims=(((1,), (0,)), ((), ()))):
    return lax.dot_general(left, right, dims, preferred_element_type=jnp.float32)


def merge_stats(stats):
    peak = jnp.max(stats[:, 0], axis=0)
    weight = jnp.exp(stats[:, 0] - peak)
    total = jnp.sum(weight * stats[:, 1], axis=0)
    delta = jnp.sum(weight * stats[:, 2], axis=0) / total
    return peak, total, delta


def shards(queries, keys, values, out_grad, row_keep, row_lengths):
    rows_dev, cols_dev, feature = queries.shape
    row_axis = lax.axis_size("row")
    total_rows = rows_dev * row_axis
    total_cols = cols_dev * lax.axis_size("col")
    group_rows = total_rows // SUMMARIES
    flat_width = cols_dev * feature
    near = [[y * BLOCKS + i for i in range(BLOCKS)] for y in range(row_axis // BLOCKS)]
    far = [[y * BLOCKS + i for y in range(row_axis // BLOCKS)] for i in range(BLOCKS)]
    bands = row_axis // BLOCKS
    block_keys = bands * rows_dev
    column_ids = lax.axis_index("col") * cols_dev + jnp.arange(cols_dev, dtype=jnp.int32)
    cell_keep = (row_keep[:, None] == 1) & (column_ids[None, :] < row_lengths[:, None])
    keep_flat = jnp.broadcast_to(cell_keep[:, :, None], queries.shape).reshape(
        rows_dev, flat_width
    )
    zero = jnp.zeros((), queries.dtype)

    def masked(table):
        return jnp.where(keep_flat, table.reshape(rows_dev, flat_width), zero)

    q_flat, k_flat, v_flat, g_flat = (
        masked(queries),
        masked(keys),
        masked(values),
        masked(out_grad),
    )
    logit_scale = 1.0 / math.sqrt(total_cols * feature)
    inv_root = 1.0 / math.sqrt(feature)

    k_blk = lax.all_gather(k_flat, "row", axis=0, tiled=True, axis_index_groups=far)
    q_blk = lax.all_gather(q_flat, "row", axis=0, tiled=True, axis_index_groups=near)
    logit_piece = dot_f32(q_blk, k_blk, ROW_PAIR)
    logit_sum = lax.psum_scatter(logit_piece, "col", scatter_dimension=0, tiled=True)

    flag_row = jnp.pad(
        row_keep.astype(jnp.bfloat16)[None, :], ((0, 15), (0, flat_width - rows_dev))
    )
    v_pay = jnp.concatenate([v_flat, flag_row], axis=0)
    v_all = lax.all_gather(v_pay, "row", axis=0, tiled=False, axis_index_groups=far)
    v_blk = v_all[:, :rows_dev].reshape(block_keys, flat_width)
    key_flags = v_all[:, rows_dev, :rows_dev].reshape(block_keys)
    g_blk = lax.all_gather(g_flat, "row", axis=0, tiled=True, axis_index_groups=near)
    dprob_piece = dot_f32(g_blk, v_blk, ROW_PAIR)
    dprob_sum = lax.psum_scatter(dprob_piece, "col", scatter_dimension=0, tiled=True)

    tokens = block_keys // group_rows

    def pooled(blk):
        summed = jnp.sum(
            blk.reshape(tokens, group_rows, flat_width), axis=1, dtype=jnp.float32
        )
        return (summed / group_rows).astype(jnp.bfloat16)

    sum_k, sum_v = pooled(k_blk), pooled(v_blk)
    cross_exp, cross_dp, cross_stats = [], [], []
    for c in range(cols_dev):
        lanes = slice(c * feature, (c + 1) * feature)
        cl = dot_f32(sum_k[:, lanes], q_blk[:, lanes], ROW_PAIR) * inv_root
        dp = dot_f32(sum_v[:, lanes], g_blk[:, lanes], ROW_PAIR)
        peak = jnp.max(cl, axis=0)
        lifted = jnp.exp(cl - peak[None, :])
        cross_exp.append(lifted)
        cross_dp.append(dp)
        cross_stats.append(
            jnp.stack([peak, jnp.sum(lifted, axis=0), jnp.sum(lifted * dp, axis=0)])
        )
    own_stats = jnp.stack(cross_stats, axis=1)
    all_stats = lax.all_gather(own_stats, "row", axis=0, tiled=False, axis_index_groups=near)
    c_peak, c_total, c_delta = merge_stats(all_stats)
    dq_cross, dk_sum, dv_sum = [], [], []
    for c in range(cols_dev):
        lanes = slice(c * feature, (c + 1) * feature)
        weight = jnp.exp(own_stats[0, c] - c_peak[c]) / c_total[c]
        probs = cross_exp[c] * weight[None, :]
        prob_bf = probs.astype(jnp.bfloat16)
        dl_bf = (inv_root * probs * (cross_dp[c] - c_delta[c][None, :])).astype(jnp.bfloat16)
        dq_cross.append(dot_f32(dl_bf, sum_k[:, lanes], LEAD_PAIR))
        dk_sum.append(dot_f32(dl_bf, q_blk[:, lanes]))
        dv_sum.append(dot_f32(prob_bf, g_blk[:, lanes]))

    def spread(pieces):
        wide = jnp.concatenate(pieces, axis=1) / group_rows
        return jnp.broadcast_to(wide[:, None, :], (tokens, group_rows, flat_width)).reshape(
            block_keys, flat_width
        )

    logits = jnp.where(key_flags[None, :] > 0, logit_sum * logit_scale, -1e30)
    r_peak = jnp.max(logits, axis=1)
    lifted = jnp.exp(logits - r_peak[:, None])
    r_stats = jnp.stack(
        [r_peak, jnp.sum(lifted, axis=1), jnp.sum(lifted * dprob_sum, axis=1)]
    )
    m_peak, m_total, m_delta = merge_stats(
        lax.all_gather(r_stats, "row", axis=0, tiled=False, axis_index_groups=near)
    )
    probs = lifted * (jnp.exp(r_peak - m_peak) / m_total)[:, None]
    dlogit = logit_scale * probs * (dprob_sum - m_delta[:, None])
    both = jnp.concatenate([probs.astype(jnp.bfloat16), dlogit.astype(jnp.bfloat16)], axis=1)
    both_blk = lax.all_gather(both, "col", axis=0, tiled=True)
    prob_blk, dlogit_blk = both_blk[:, :block_keys], both_blk[:, block_keys:]

    dq_part = dot_f32(dlogit_blk, k_blk) + jnp.concatenate(dq_cross, axis=1)
    dk_part = dot_f32(dlogit_blk, q_blk, LEAD_PAIR) + spread(dk_sum)
    dv_part = dot_f32(prob_blk, g_blk, LEAD_PAIR) + spread(dv_sum)

    def reduce_parts(parts, groups):
        moved = lax.all_to_all(
            parts, "row", split_axis=0, concat_axis=0, tiled=True, axis_index_groups=groups
        )
        return jnp.sum(
            moved.reshape(len(groups[0]), -1, moved.shape[-1]), axis=0, dtype=jnp.float32
        )

    def finished(total):
        return (
            jnp.where(keep_flat, total, 0.0)
            .astype(jnp.bfloat16)
            .reshape(rows_dev, cols_dev, feature)
        )

    grad_q = finished(reduce_parts(dq_part.astype(jnp.bfloat16), near))
    kv = reduce_parts(jnp.concatenate([dk_part, dv_part], axis=1).astype(jnp.bfloat16), far)
    return (grad_q, finished(kv[:, :flat_width]), finished(kv[:, flat_width:]))


def solution(mesh):
    return jax.shard_map(
        shards,
        mesh=mesh,
        in_specs=(
            P("row", "col", None),
            P("row", "col", None),
            P("row", "col", None),
            P("row", "col", None),
            P("row"),
            P("row"),
        ),
        out_specs=(P("row", "col", None), P("row", "col", None), P("row", "col", None)),
        check_vma=False,
    )
```

```python
import math

import jax
import jax.numpy as jnp
from jax import lax
from jax.experimental.layout import Layout, with_layout_constraint
from jax.sharding import PartitionSpec as P

SUMMARIES = 256
XS = 4

ROW_PAIR = (((1,), (1,)), ((), ()))
LEAD_PAIR = (((0,), (0,)), ((), ()))
PLAIN = (((1,), (0,)), ((), ()))


def dot_f32(left, right, dims=PLAIN):
    return lax.dot_general(left, right, dims, preferred_element_type=jnp.float32)


def merge_stats(stats):
    peak = jnp.max(stats[:, 0], axis=0)
    weight = jnp.exp(stats[:, 0] - peak)
    total = jnp.sum(weight * stats[:, 1], axis=0)
    delta = jnp.sum(weight * stats[:, 2], axis=0) / total
    return peak, total, delta


def shards(queries, keys, values, out_grad, row_keep, row_lengths):
    rows_dev, cols_dev, feature = queries.shape
    row_axis = lax.axis_size("row")
    ys = row_axis // (2 * XS)
    near_size = 2 * XS
    total_rows = rows_dev * row_axis
    total_cols = cols_dev * lax.axis_size("col")
    group_rows = total_rows // SUMMARIES
    flat_width = cols_dev * feature
    block_rows = near_size * rows_dev
    block_keys = ys * rows_dev
    near = [[y * near_size + i for i in range(near_size)] for y in range(ys)]
    place = lax.axis_index("row")
    own_x = (place // 2) % XS
    own_core = place % 2

    def at(y, x, core):
        return ((y % ys) * XS + x % XS) * 2 + core

    cells = [(y, x, c) for y in range(ys) for x in range(XS) for c in range(2)]

    def shift_y(table, step):
        return lax.ppermute(table, "row", [(at(y, x, c), at(y + step, x, c)) for y, x, c in cells])

    def shift_x(table, step):
        return lax.ppermute(table, "row", [(at(y, x, c), at(y, x + step, c)) for y, x, c in cells])

    def swap_core(table):
        return lax.ppermute(table, "row", [(at(y, x, c), at(y, x, 1 - c)) for y, x, c in cells])

    def by_core(own, other):
        first = jnp.where(own_core == 0, own, other)
        second = jnp.where(own_core == 0, other, own)
        return first, second

    column_ids = lax.axis_index("col") * cols_dev + jnp.arange(cols_dev, dtype=jnp.int32)
    cell_keep = (row_keep[:, None] == 1) & (column_ids[None, :] < row_lengths[:, None])
    keep_flat = jnp.broadcast_to(cell_keep[:, :, None], queries.shape).reshape(
        rows_dev, flat_width
    )
    zero = jnp.zeros((), queries.dtype)

    def masked(table):
        flat = jnp.where(keep_flat, table.reshape(rows_dev, flat_width), zero)
        return with_layout_constraint(flat, Layout((0, 1)))

    def key_block(table):
        return [table] + [shift_y(table, s) for s in range(1, ys)]

    def query_block(table):
        pieces = [table] + [shift_x(table, s) for s in range(1, XS)]
        line = jnp.zeros((XS,) + table.shape, table.dtype)
        for s, piece in enumerate(pieces):
            line = lax.dynamic_update_slice(line, piece[None], ((own_x - s) % XS, 0, 0))
        pair = jnp.stack(by_core(line, swap_core(line)), axis=1)
        return pair.reshape(block_rows, flat_width)

    logit_scale = 1.0 / math.sqrt(total_cols * feature)
    inv_root = 1.0 / math.sqrt(feature)

    q_flat, k_flat = masked(queries), masked(keys)
    k_blk = jnp.concatenate(key_block(k_flat), axis=0)
    q_blk = query_block(q_flat)
    logit_piece = dot_f32(q_blk, k_blk, ROW_PAIR)
    keep_flat, _ = lax.optimization_barrier((keep_flat, logit_piece))
    logit_sum = lax.psum_scatter(logit_piece, "col", scatter_dimension=0, tiled=True)

    v_flat, g_flat = masked(values), masked(out_grad)
    flag_row = jnp.pad(
        row_keep.astype(jnp.bfloat16)[None, :], ((0, 15), (0, flat_width - rows_dev))
    )
    v_pieces = key_block(jnp.concatenate([v_flat, flag_row], axis=0))
    v_blk = jnp.concatenate([p[:rows_dev] for p in v_pieces], axis=0)
    key_flags = jnp.concatenate([p[rows_dev, :rows_dev] for p in v_pieces])
    g_blk = query_block(g_flat)
    dprob_piece = dot_f32(g_blk, v_blk, ROW_PAIR).astype(jnp.bfloat16)
    dprob_parts = lax.all_to_all(dprob_piece, "col", split_axis=0, concat_axis=0, tiled=True)

    tokens = block_keys // group_rows

    def pooled(blk):
        summed = jnp.sum(
            blk.reshape(tokens, group_rows, flat_width), axis=1, dtype=jnp.float32
        )
        return (summed / group_rows).astype(jnp.bfloat16)

    sum_k, sum_v = pooled(k_blk), pooled(v_blk)
    cross_exp, cross_dp, cross_stats = [], [], []
    for c in range(cols_dev):
        lanes = slice(c * feature, (c + 1) * feature)
        cl = dot_f32(sum_k[:, lanes], q_blk[:, lanes], ROW_PAIR) * inv_root
        dp = dot_f32(sum_v[:, lanes], g_blk[:, lanes], ROW_PAIR)
        peak = jnp.max(cl, axis=0)
        lifted = jnp.exp(cl - peak[None, :])
        cross_exp.append(lifted)
        cross_dp.append(dp)
        cross_stats.append(
            jnp.stack([peak, jnp.sum(lifted, axis=0), jnp.sum(lifted * dp, axis=0)])
        )
    own_stats = jnp.stack(cross_stats, axis=1)
    all_stats = lax.all_gather(own_stats, "row", axis=0, tiled=False, axis_index_groups=near)
    c_peak, c_total, c_delta = merge_stats(all_stats)
    dq_cross, dk_sum, dv_sum = [], [], []
    for c in range(cols_dev):
        lanes = slice(c * feature, (c + 1) * feature)
        weight = jnp.exp(own_stats[0, c] - c_peak[c]) / c_total[c]
        probs = cross_exp[c] * weight[None, :]
        prob_bf = probs.astype(jnp.bfloat16)
        dl_bf = (inv_root * probs * (cross_dp[c] - c_delta[c][None, :])).astype(jnp.bfloat16)
        dq_cross.append(dot_f32(dl_bf, sum_k[:, lanes], LEAD_PAIR))
        dk_sum.append(dot_f32(dl_bf, q_blk[:, lanes]))
        dv_sum.append(dot_f32(prob_bf, g_blk[:, lanes]))
    dq_cross = jnp.concatenate(dq_cross, axis=1)
    dk_sum = jnp.concatenate(dk_sum, axis=1) / group_rows
    dv_sum = jnp.concatenate(dv_sum, axis=1) / group_rows
    logit_sum, dq_cross, dk_sum, dv_sum = lax.optimization_barrier(
        (logit_sum, dq_cross, dk_sum, dv_sum)
    )

    def spread(wide):
        return jnp.broadcast_to(wide[:, None, :], (tokens, group_rows, flat_width)).reshape(
            block_keys, flat_width
        )

    dprob_sum = jnp.sum(
        dprob_parts.reshape(-1, block_rows // lax.axis_size("col"), block_keys),
        axis=0,
        dtype=jnp.float32,
    )
    logits = jnp.where(key_flags[None, :] > 0, logit_sum * logit_scale, -1e30)
    peak = jnp.max(logits, axis=1)
    lifted = jnp.exp(logits - peak[:, None])
    total = jnp.sum(lifted, axis=1)
    weighted = jnp.sum(lifted * dprob_sum, axis=1)
    delta = weighted / total
    lift_bf = lifted.astype(jnp.bfloat16)
    tilt_bf = (lifted * (dprob_sum - delta[:, None])).astype(jnp.bfloat16)
    lift_blk = lax.all_gather(lift_bf, "col", axis=0, tiled=True).astype(jnp.float32)
    tilt_blk = lax.all_gather(tilt_bf, "col", axis=0, tiled=True).astype(jnp.float32)
    m_peak, m_total, m_delta = merge_stats(
        lax.all_gather(
            jnp.stack([peak, total, weighted]),
            "row",
            axis=0,
            tiled=False,
            axis_index_groups=near,
        )
    )
    scaling = jnp.stack([jnp.exp(peak - m_peak) / m_total, m_delta - delta])
    scaling = lax.all_gather(scaling, "col", axis=1, tiled=True)
    weight, offset = scaling[0][:, None], scaling[1][:, None]
    prob_blk = (lift_blk * weight).astype(jnp.bfloat16)
    dlogit_blk = (logit_scale * weight * (tilt_blk - lift_blk * offset)).astype(jnp.bfloat16)

    def reduce_keys(part):
        part = part.astype(jnp.bfloat16).reshape(ys, rows_dev, flat_width)
        moved = [part[0]] + [shift_y(part[s], -s) for s in range(1, ys)]
        return sum(m.astype(jnp.float32) for m in moved)

    def reduce_queries(part):
        part = part.astype(jnp.bfloat16).reshape(XS, 2, rows_dev, flat_width)
        own, other = by_core(part[:, 0], part[:, 1])
        line = (own.astype(jnp.float32) + swap_core(other).astype(jnp.float32)).astype(
            jnp.bfloat16
        )

        def piece(s):
            return lax.dynamic_index_in_dim(line, (own_x - s) % XS, axis=0, keepdims=False)

        moved = [piece(0)] + [shift_x(piece(s), -s) for s in range(1, XS)]
        return sum(m.astype(jnp.float32) for m in moved)

    def finished(rows):
        return (
            jnp.where(keep_flat, rows, 0.0)
            .astype(jnp.bfloat16)
            .reshape(rows_dev, cols_dev, feature)
        )

    grad_v = finished(reduce_keys(dot_f32(prob_blk, g_blk, LEAD_PAIR) + spread(dv_sum)))
    grad_q = finished(reduce_queries(dot_f32(dlogit_blk, k_blk) + dq_cross))
    grad_k = finished(reduce_keys(dot_f32(dlogit_blk, q_blk, LEAD_PAIR) + spread(dk_sum)))
    return (grad_q, grad_k, grad_v)


def solution(mesh):
    return jax.shard_map(
        shards,
        mesh=mesh,
        in_specs=(
            P("row", "col", None),
            P("row", "col", None),
            P("row", "col", None),
            P("row", "col", None),
            P("row"),
            P("row"),
        ),
        out_specs=(P("row", "col", None), P("row", "col", None), P("row", "col", None)),
        check_vma=False,
    )
```

```python
import math

import jax
import jax.numpy as jnp
from jax import lax
from jax.experimental.layout import Layout, with_layout_constraint
from jax.sharding import PartitionSpec as P

SUMMARIES = 256
XS = 4

ROW_PAIR = (((1,), (1,)), ((), ()))
LEAD_PAIR = (((0,), (0,)), ((), ()))
PLAIN = (((1,), (0,)), ((), ()))


def dot_f32(left, right, dims=PLAIN):
    return lax.dot_general(left, right, dims, preferred_element_type=jnp.float32)


def merge_stats(stats):
    peak = jnp.max(stats[:, 0], axis=0)
    weight = jnp.exp(stats[:, 0] - peak)
    total = jnp.sum(weight * stats[:, 1], axis=0)
    delta = jnp.sum(weight * stats[:, 2], axis=0) / total
    return peak, total, delta


def shards(queries, keys, values, out_grad, row_keep, row_lengths):
    rows_dev, cols_dev, feature = queries.shape
    row_axis = lax.axis_size("row")
    ys = row_axis // (2 * XS)
    near_size = 2 * XS
    total_rows = rows_dev * row_axis
    total_cols = cols_dev * lax.axis_size("col")
    group_rows = total_rows // SUMMARIES
    flat_width = cols_dev * feature
    block_rows = near_size * rows_dev
    block_keys = ys * rows_dev
    near = [[y * near_size + i for i in range(near_size)] for y in range(ys)]
    place = lax.axis_index("row")
    own_x = (place // 2) % XS
    own_core = place % 2

    def at(y, x, core):
        return ((y % ys) * XS + x % XS) * 2 + core

    cells = [(y, x, c) for y in range(ys) for x in range(XS) for c in range(2)]

    def shift_y(table, step):
        return lax.ppermute(table, "row", [(at(y, x, c), at(y + step, x, c)) for y, x, c in cells])

    def shift_x(table, step):
        return lax.ppermute(table, "row", [(at(y, x, c), at(y, x + step, c)) for y, x, c in cells])

    def swap_core(table):
        return lax.ppermute(table, "row", [(at(y, x, c), at(y, x, 1 - c)) for y, x, c in cells])

    def share(table, axis, groups=None):
        count = lax.axis_size(axis) if groups is None else len(groups[0])
        copies = jnp.broadcast_to(table[None], (count,) + table.shape)
        return lax.all_to_all(
            copies, axis, split_axis=0, concat_axis=0, tiled=True, axis_index_groups=groups
        )

    def by_core(own, other):
        first = jnp.where(own_core == 0, own, other)
        second = jnp.where(own_core == 0, other, own)
        return first, second

    column_ids = lax.axis_index("col") * cols_dev + jnp.arange(cols_dev, dtype=jnp.int32)
    cell_keep = (row_keep[:, None] == 1) & (column_ids[None, :] < row_lengths[:, None])
    keep_flat = jnp.broadcast_to(cell_keep[:, :, None], queries.shape).reshape(
        rows_dev, flat_width
    )
    zero = jnp.zeros((), queries.dtype)

    def masked(table):
        flat = jnp.where(keep_flat, table.reshape(rows_dev, flat_width), zero)
        return with_layout_constraint(flat, Layout((0, 1)))

    def key_block(table):
        return [table] + [shift_y(table, s) for s in range(1, ys)]

    def query_block(table):
        pieces = [table] + [shift_x(table, s) for s in range(1, XS)]
        line = jnp.zeros((XS,) + table.shape, table.dtype)
        for s, piece in enumerate(pieces):
            line = lax.dynamic_update_slice(line, piece[None], ((own_x - s) % XS, 0, 0))
        pair = jnp.stack(by_core(line, swap_core(line)), axis=1)
        return pair.reshape(block_rows, flat_width)

    logit_scale = 1.0 / math.sqrt(total_cols * feature)
    inv_root = 1.0 / math.sqrt(feature)

    q_flat, k_flat = lax.optimization_barrier((masked(queries), masked(keys)))
    k_blk = jnp.concatenate(key_block(k_flat), axis=0)
    q_blk = query_block(q_flat)
    logit_piece = dot_f32(q_blk, k_blk, ROW_PAIR)
    keep_flat, _ = lax.optimization_barrier((keep_flat, logit_piece))
    logit_sum = lax.psum_scatter(logit_piece, "col", scatter_dimension=0, tiled=True)

    v_flat, g_flat = masked(values), masked(out_grad)
    flag_row = jnp.pad(
        row_keep.astype(jnp.bfloat16)[None, :], ((0, 15), (0, flat_width - rows_dev))
    )
    v_pieces = key_block(jnp.concatenate([v_flat, flag_row], axis=0))
    v_blk = jnp.concatenate([p[:rows_dev] for p in v_pieces], axis=0)
    key_flags = jnp.concatenate([p[rows_dev, :rows_dev] for p in v_pieces])
    g_blk = query_block(g_flat)
    dprob_piece = dot_f32(g_blk, v_blk, ROW_PAIR).astype(jnp.bfloat16)
    dprob_parts = lax.all_to_all(dprob_piece, "col", split_axis=0, concat_axis=0, tiled=True)

    k_tok, _ = lax.optimization_barrier((k_blk, dprob_piece))
    tokens = block_keys // group_rows

    def pooled(blk):
        summed = jnp.sum(
            blk.reshape(tokens, group_rows, flat_width), axis=1, dtype=jnp.float32
        )
        return (summed / group_rows).astype(jnp.bfloat16)

    sum_k, sum_v = pooled(k_tok), pooled(v_blk)
    cross_exp, cross_dp, cross_stats = [], [], []
    for c in range(cols_dev):
        lanes = slice(c * feature, (c + 1) * feature)
        cl = dot_f32(sum_k[:, lanes], q_blk[:, lanes], ROW_PAIR) * inv_root
        dp = dot_f32(sum_v[:, lanes], g_blk[:, lanes], ROW_PAIR)
        peak = jnp.max(cl, axis=0)
        lifted = jnp.exp(cl - peak[None, :])
        cross_exp.append(lifted)
        cross_dp.append(dp)
        cross_stats.append(
            jnp.stack([peak, jnp.sum(lifted, axis=0), jnp.sum(lifted * dp, axis=0)])
        )
    own_stats = jnp.stack(cross_stats, axis=1)
    logit_sum, own_stats, cross_exp, cross_dp = lax.optimization_barrier(
        (logit_sum, own_stats, cross_exp, cross_dp)
    )

    def spread(wide):
        return jnp.broadcast_to(wide[:, None, :], (tokens, group_rows, flat_width)).reshape(
            block_keys, flat_width
        )

    dprob_sum = jnp.sum(
        dprob_parts.reshape(-1, block_rows // lax.axis_size("col"), block_keys),
        axis=0,
        dtype=jnp.float32,
    )
    logits = jnp.where(key_flags[None, :] > 0, logit_sum * logit_scale, -1e30)
    peak = jnp.max(logits, axis=1)
    lifted = jnp.exp(logits - peak[:, None])
    total = jnp.sum(lifted, axis=1)
    weighted = jnp.sum(lifted * dprob_sum, axis=1)
    delta = weighted / total
    lift_bf = lifted.astype(jnp.bfloat16)
    tilt_bf = (lifted * (dprob_sum - delta[:, None])).astype(jnp.bfloat16)
    both = jnp.concatenate([lift_bf, tilt_bf], axis=1)
    peak, total, weighted, both_sent = lax.optimization_barrier((peak, total, weighted, both))
    both = lax.all_gather(both_sent, "col", axis=0, tiled=True)
    row_stats = jnp.stack([peak, total, weighted]).reshape(1, 3 * rows_dev)
    packed = jnp.concatenate(
        [
            own_stats.reshape(3 * cols_dev, block_rows),
            jnp.pad(row_stats, ((0, 0), (0, block_rows - 3 * rows_dev))),
        ],
        axis=0,
    )
    packed = share(packed, "row", near)
    m_peak, m_total, m_delta = merge_stats(
        packed[:, -1, : 3 * rows_dev].reshape(near_size, 3, rows_dev)
    )
    scaling = jnp.stack([jnp.exp(peak - m_peak) / m_total, m_delta - delta])
    scaling = share(scaling, "col")
    scaling = jnp.swapaxes(scaling, 0, 1).reshape(2, block_rows)
    c_peak, c_total, c_delta = merge_stats(
        packed[:, :-1].reshape(near_size, 3, cols_dev, block_rows)
    )
    dq_cross, dk_sum, dv_sum = [], [], []
    for c in range(cols_dev):
        lanes = slice(c * feature, (c + 1) * feature)
        weight = jnp.exp(own_stats[0, c] - c_peak[c]) / c_total[c]
        probs = cross_exp[c] * weight[None, :]
        prob_bf = probs.astype(jnp.bfloat16)
        dl_bf = (inv_root * probs * (cross_dp[c] - c_delta[c][None, :])).astype(jnp.bfloat16)
        dq_cross.append(dot_f32(dl_bf, sum_k[:, lanes], LEAD_PAIR))
        dk_sum.append(dot_f32(dl_bf, q_blk[:, lanes]))
        dv_sum.append(dot_f32(prob_bf, g_blk[:, lanes]))
    dq_cross = jnp.concatenate(dq_cross, axis=1)
    dk_sum = jnp.concatenate(dk_sum, axis=1) / group_rows
    dv_sum = jnp.concatenate(dv_sum, axis=1) / group_rows
    both, scaling, dq_cross, dk_sum, dv_sum = lax.optimization_barrier(
        (both, scaling, dq_cross, dk_sum, dv_sum)
    )
    lift_blk = both[:, :block_keys].astype(jnp.float32)
    tilt_blk = both[:, block_keys:].astype(jnp.float32)
    weight, offset = scaling[0][:, None], scaling[1][:, None]
    prob_blk = (lift_blk * weight).astype(jnp.bfloat16)
    dlogit_blk = (logit_scale * weight * (tilt_blk - lift_blk * offset)).astype(jnp.bfloat16)

    def reduce_keys(part):
        part = part.astype(jnp.bfloat16).reshape(ys, rows_dev, flat_width)
        moved = [part[0]] + [shift_y(part[s], -s) for s in range(1, ys)]
        return sum(m.astype(jnp.float32) for m in moved)

    def reduce_queries(part):
        part = part.astype(jnp.bfloat16).reshape(XS, 2, rows_dev, flat_width)
        own, other = by_core(part[:, 0], part[:, 1])
        line = (own.astype(jnp.float32) + swap_core(other).astype(jnp.float32)).astype(
            jnp.bfloat16
        )

        def piece(s):
            return lax.dynamic_index_in_dim(line, (own_x - s) % XS, axis=0, keepdims=False)

        moved = [piece(0)] + [shift_x(piece(s), -s) for s in range(1, XS)]
        return sum(m.astype(jnp.float32) for m in moved)

    def finished(rows):
        return (
            jnp.where(keep_flat, rows, 0.0)
            .astype(jnp.bfloat16)
            .reshape(rows_dev, cols_dev, feature)
        )

    grad_v = finished(reduce_keys(dot_f32(prob_blk, g_blk, LEAD_PAIR) + spread(dv_sum)))
    grad_q = finished(reduce_queries(dot_f32(dlogit_blk, k_blk) + dq_cross))
    grad_k = finished(reduce_keys(dot_f32(dlogit_blk, q_blk, LEAD_PAIR) + spread(dk_sum)))
    return (grad_q, grad_k, grad_v)


def solution(mesh):
    return jax.shard_map(
        shards,
        mesh=mesh,
        in_specs=(
            P("row", "col", None),
            P("row", "col", None),
            P("row", "col", None),
            P("row", "col", None),
            P("row"),
            P("row"),
        ),
        out_specs=(P("row", "col", None), P("row", "col", None), P("row", "col", None)),
        check_vma=False,
    )
```

```python
import math

import jax
import jax.numpy as jnp
from jax import lax
from jax.experimental import pallas as pl
from jax.experimental.pallas import tpu as pltpu
from jax.experimental.layout import Layout, with_layout_constraint
from jax.sharding import PartitionSpec as P

SUMMARIES = 256
XS = 4

ROW_PAIR = (((1,), (1,)), ((), ()))
LEAD_PAIR = (((0,), (0,)), ((), ()))
PLAIN = (((1,), (0,)), ((), ()))


def dot_f32(left, right, dims=PLAIN):
    return lax.dot_general(left, right, dims, preferred_element_type=jnp.float32)


def across(column):
    n = column.shape[0]
    eye = lax.broadcasted_iota(jnp.int32, (n, n), 0) == lax.broadcasted_iota(jnp.int32, (n, n), 1)
    return jnp.sum(jnp.where(eye, column, 0.0), axis=0, keepdims=True)


def upright(row):
    n = row.shape[1]
    eye = lax.broadcasted_iota(jnp.int32, (n, n), 0) == lax.broadcasted_iota(jnp.int32, (n, n), 1)
    return jnp.sum(jnp.where(eye, row, 0.0), axis=1, keepdims=True)


def block_softmax(logit_scale, logit_sum, own, forward, back, key_flags):
    rows, width = logit_sum.shape

    def kernel(logit_ref, own_ref, forward_ref, back_ref, flag_ref, both_ref, stat_ref):
        dprob = (
            own_ref[...].astype(jnp.float32)
            + forward_ref[...].astype(jnp.float32)
            + back_ref[...].astype(jnp.float32)
        )
        logits = jnp.where(flag_ref[...] > 0, logit_ref[...] * logit_scale, -1e30)
        peak = jnp.max(logits, axis=1, keepdims=True)
        lifted = jnp.exp(logits - peak)
        total = jnp.sum(lifted, axis=1, keepdims=True)
        weighted = jnp.sum(lifted * dprob, axis=1, keepdims=True)
        delta = weighted / total
        both_ref[:, :width] = lifted.astype(jnp.bfloat16)
        both_ref[:, width:] = (lifted * (dprob - delta)).astype(jnp.bfloat16)
        for i, column in enumerate((peak, total, weighted, delta)):
            stat_ref[i : i + 1, :] = across(column)
        stat_ref[4:8, :] = jnp.zeros((4, rows), jnp.float32)

    return pl.pallas_call(
        kernel,
        out_shape=(
            jax.ShapeDtypeStruct((rows, 2 * width), jnp.bfloat16),
            jax.ShapeDtypeStruct((8, rows), jnp.float32),
        ),
        name="block_softmax",
    )(logit_sum, own, forward, back, key_flags)


def query_grads(logit_scale, core, both, scaling, k_blk, cross_dl, sum_k, rows_dev):
    block_rows, width = both.shape[0], both.shape[1] // 2
    flat_width = k_blk.shape[1]
    chunks = block_rows // rows_dev
    tokens = sum_k.shape[0]
    columns = cross_dl.shape[0] // tokens
    feature = flat_width // columns

    def kernel(core_ref, both_ref, scale_ref, k_ref, dl_ref, sk_ref, p_ref, ds_ref, own_ref, other_ref, dq_ref):
        for i in range(chunks):
            rows = slice(i * rows_dev, (i + 1) * rows_dev)
            weight = upright(scale_ref[i, 0:1, :])
            offset = upright(scale_ref[i, 1:2, :])
            lifted = both_ref[rows, :width].astype(jnp.float32)
            tilted = both_ref[rows, width:].astype(jnp.float32)
            p_ref[rows, :] = (lifted * weight).astype(jnp.bfloat16)
            ds_ref[rows, :] = ((tilted - lifted * offset) * (weight * logit_scale)).astype(
                jnp.bfloat16
            )
        dq_ref[...] = dot_f32(ds_ref[...], k_ref[...])
        for c in range(columns):
            lanes = slice(c * feature, (c + 1) * feature)
            dq_ref[:, lanes] += dot_f32(
                dl_ref[c * tokens : (c + 1) * tokens, :], sk_ref[:, lanes], LEAD_PAIR
            )
        core = core_ref[0]
        for x in range(chunks // 2):
            rows = slice(x * rows_dev, (x + 1) * rows_dev)
            mine = pl.multiple_of((2 * x + core) * rows_dev, rows_dev)
            theirs = pl.multiple_of((2 * x + 1 - core) * rows_dev, rows_dev)
            own_ref[rows, :] = dq_ref[pl.ds(mine, rows_dev), :]
            other_ref[rows, :] = dq_ref[pl.ds(theirs, rows_dev), :].astype(jnp.bfloat16)

    vmem = pl.BlockSpec(memory_space=pltpu.VMEM)
    return pl.pallas_call(
        kernel,
        in_specs=[pl.BlockSpec(memory_space=pltpu.SMEM)] + [vmem] * 5,
        out_shape=(
            jax.ShapeDtypeStruct((block_rows, width), jnp.bfloat16),
            jax.ShapeDtypeStruct((block_rows, width), jnp.bfloat16),
            jax.ShapeDtypeStruct((block_rows // 2, flat_width), jnp.float32),
            jax.ShapeDtypeStruct((block_rows // 2, flat_width), jnp.bfloat16),
        ),
        scratch_shapes=[pltpu.VMEM((block_rows, flat_width), jnp.float32)],
        compiler_params=pltpu.CompilerParams(vmem_limit_bytes=40 * 1024 * 1024),
        name="query_grads",
    )(core, both, scaling, k_blk, cross_dl, sum_k)


def key_grads(prob, dlogit, q_blk, g_blk, dk_sum, dv_sum, pieces):
    width, flat_width = prob.shape[1], q_blk.shape[1]
    tokens = dk_sum.shape[0]
    group = width // tokens
    piece = width // pieces

    def kernel(p_ref, ds_ref, q_ref, g_ref, dk_ref, dv_ref, *out_refs):
        for half, (w_ref, t_ref, s_ref) in enumerate(
            ((ds_ref, q_ref, dk_ref), (p_ref, g_ref, dv_ref))
        ):
            grads = dot_f32(w_ref[...], t_ref[...], LEAD_PAIR)
            grads = (
                grads.reshape(tokens, group, flat_width) + s_ref[...][:, None, :]
            ).reshape(width, flat_width)
            for s, out_ref in enumerate(out_refs):
                out_ref[:, half * flat_width : (half + 1) * flat_width] = grads[
                    s * piece : (s + 1) * piece
                ].astype(jnp.bfloat16)

    return pl.pallas_call(
        kernel,
        out_shape=tuple(
            jax.ShapeDtypeStruct((piece, 2 * flat_width), jnp.bfloat16) for _ in range(pieces)
        ),
        compiler_params=pltpu.CompilerParams(vmem_limit_bytes=40 * 1024 * 1024),
        name="key_grads",
    )(prob, dlogit, q_blk, g_blk, dk_sum, dv_sum)


def merge_stats(stats):
    peak = jnp.max(stats[:, 0], axis=0)
    weight = jnp.exp(stats[:, 0] - peak)
    total = jnp.sum(weight * stats[:, 1], axis=0)
    delta = jnp.sum(weight * stats[:, 2], axis=0) / total
    return peak, total, delta


def shards(queries, keys, values, out_grad, row_keep, row_lengths):
    rows_dev, cols_dev, feature = queries.shape
    row_axis = lax.axis_size("row")
    ys = row_axis // (2 * XS)
    near_size = 2 * XS
    total_rows = rows_dev * row_axis
    total_cols = cols_dev * lax.axis_size("col")
    group_rows = total_rows // SUMMARIES
    flat_width = cols_dev * feature
    block_rows = near_size * rows_dev
    block_keys = ys * rows_dev
    near = [[y * near_size + i for i in range(near_size)] for y in range(ys)]
    place = lax.axis_index("row")
    own_x = (place // 2) % XS
    own_core = place % 2

    def at(y, x, core):
        return ((y % ys) * XS + x % XS) * 2 + core

    cells = [(y, x, c) for y in range(ys) for x in range(XS) for c in range(2)]

    def shift_y(table, step):
        return lax.ppermute(table, "row", [(at(y, x, c), at(y + step, x, c)) for y, x, c in cells])

    def shift_x(table, step):
        return lax.ppermute(table, "row", [(at(y, x, c), at(y, x + step, c)) for y, x, c in cells])

    def swap_core(table):
        return lax.ppermute(table, "row", [(at(y, x, c), at(y, x, 1 - c)) for y, x, c in cells])

    def share(table, axis, groups=None):
        count = lax.axis_size(axis) if groups is None else len(groups[0])
        copies = jnp.broadcast_to(table[None], (count,) + table.shape)
        return lax.all_to_all(
            copies, axis, split_axis=0, concat_axis=0, tiled=True, axis_index_groups=groups
        )

    def by_core(own, other):
        first = jnp.where(own_core == 0, own, other)
        second = jnp.where(own_core == 0, other, own)
        return first, second

    column_ids = lax.axis_index("col") * cols_dev + jnp.arange(cols_dev, dtype=jnp.int32)
    cell_keep = (row_keep[:, None] == 1) & (column_ids[None, :] < row_lengths[:, None])
    keep_flat = jnp.broadcast_to(cell_keep[:, :, None], queries.shape).reshape(
        rows_dev, flat_width
    )
    zero = jnp.zeros((), queries.dtype)

    def masked(table):
        flat = jnp.where(keep_flat, table.reshape(rows_dev, flat_width), zero)
        return with_layout_constraint(flat, Layout((0, 1)))

    def key_block(table):
        return [table] + [shift_y(table, s) for s in range(1, ys)]

    def query_block(table):
        pieces = [table] + [shift_x(table, s) for s in range(1, XS)]
        line = jnp.zeros((XS,) + table.shape, table.dtype)
        for s, piece in enumerate(pieces):
            line = lax.dynamic_update_slice(line, piece[None], ((own_x - s) % XS, 0, 0))
        pair = jnp.stack(by_core(line, swap_core(line)), axis=1)
        return pair.reshape(block_rows, flat_width)

    logit_scale = 1.0 / math.sqrt(total_cols * feature)
    inv_root = 1.0 / math.sqrt(feature)

    q_flat, k_flat = lax.optimization_barrier((masked(queries), masked(keys)))
    k_blk = jnp.concatenate(key_block(k_flat), axis=0)
    q_blk = query_block(q_flat)
    logit_piece = dot_f32(q_blk, k_blk, ROW_PAIR)
    keep_flat, _ = lax.optimization_barrier((keep_flat, logit_piece))
    logit_sum = lax.psum_scatter(logit_piece, "col", scatter_dimension=0, tiled=True)

    v_flat, g_flat = masked(values), masked(out_grad)
    flag_row = jnp.pad(
        row_keep.astype(jnp.bfloat16)[None, :], ((0, 15), (0, flat_width - rows_dev))
    )
    v_pieces = key_block(jnp.concatenate([v_flat, flag_row], axis=0))
    v_blk = jnp.concatenate([p[:rows_dev] for p in v_pieces], axis=0)
    key_flags = jnp.concatenate([p[rows_dev, :rows_dev] for p in v_pieces])
    g_blk = query_block(g_flat)
    dprob_piece = dot_f32(g_blk, v_blk, ROW_PAIR).astype(jnp.bfloat16)
    zs = lax.axis_size("col")
    own_z = lax.axis_index("col")
    dprob_chunks = dprob_piece.reshape(zs, block_rows // zs, block_keys)

    def part(step):
        return lax.dynamic_index_in_dim(dprob_chunks, (own_z + step) % zs, axis=0, keepdims=False)

    def shift_z(table, step):
        return lax.ppermute(table, "col", [(z, (z + step) % zs) for z in range(zs)])

    def passed(step, count):
        moving = part(step * count)
        for left in range(count - 1, -1, -1):
            moving = shift_z(moving, step)
            if left > 0:
                moving = (
                    moving.astype(jnp.float32) + part(step * left).astype(jnp.float32)
                ).astype(jnp.bfloat16)
        return moving

    dprob_forward = passed(1, zs // 2)
    dprob_back = passed(-1, zs - 1 - zs // 2)

    k_tok, _ = lax.optimization_barrier((k_blk, dprob_piece))
    tokens = block_keys // group_rows

    def pooled(blk):
        summed = jnp.sum(
            blk.reshape(tokens, group_rows, flat_width), axis=1, dtype=jnp.float32
        )
        return (summed / group_rows).astype(jnp.bfloat16)

    sum_k, sum_v = pooled(k_tok), pooled(v_blk)
    cross_exp, cross_dp, cross_stats = [], [], []
    for c in range(cols_dev):
        lanes = slice(c * feature, (c + 1) * feature)
        cl = dot_f32(sum_k[:, lanes], q_blk[:, lanes], ROW_PAIR) * inv_root
        dp = dot_f32(sum_v[:, lanes], g_blk[:, lanes], ROW_PAIR)
        peak = jnp.max(cl, axis=0)
        lifted = jnp.exp(cl - peak[None, :])
        cross_exp.append(lifted)
        cross_dp.append(dp)
        cross_stats.append(
            jnp.stack([peak, jnp.sum(lifted, axis=0), jnp.sum(lifted * dp, axis=0)])
        )
    own_stats = jnp.stack(cross_stats, axis=1)
    logit_sum, own_stats, cross_exp, cross_dp = lax.optimization_barrier(
        (logit_sum, own_stats, cross_exp, cross_dp)
    )

    def spread(wide):
        return jnp.broadcast_to(wide[:, None, :], (tokens, group_rows, flat_width)).reshape(
            block_keys, flat_width
        )

    both, stats = block_softmax(
        logit_scale, logit_sum, part(0), dprob_forward, dprob_back, key_flags[None, :]
    )
    peak, total, weighted, delta = stats[0], stats[1], stats[2], stats[3]
    both = lax.all_gather(both, "col", axis=0, tiled=True)
    row_stats = stats[:3].reshape(1, 3 * rows_dev)
    packed = jnp.concatenate(
        [
            own_stats.reshape(3 * cols_dev, block_rows),
            jnp.pad(row_stats, ((0, 0), (0, block_rows - 3 * rows_dev))),
        ],
        axis=0,
    )
    packed = share(packed, "row", near)
    m_peak, m_total, m_delta = merge_stats(
        packed[:, -1, : 3 * rows_dev].reshape(near_size, 3, rows_dev)
    )
    scaling = jnp.stack([jnp.exp(peak - m_peak) / m_total, m_delta - delta])
    scaling = share(scaling, "col")
    c_peak, c_total, c_delta = merge_stats(
        packed[:, :-1].reshape(near_size, 3, cols_dev, block_rows)
    )
    cross_dl, dk_sum, dv_sum = [], [], []
    for c in range(cols_dev):
        lanes = slice(c * feature, (c + 1) * feature)
        weight = jnp.exp(own_stats[0, c] - c_peak[c]) / c_total[c]
        probs = cross_exp[c] * weight[None, :]
        prob_bf = probs.astype(jnp.bfloat16)
        dl_bf = (inv_root * probs * (cross_dp[c] - c_delta[c][None, :])).astype(jnp.bfloat16)
        cross_dl.append(dl_bf)
        dk_sum.append(dot_f32(dl_bf, q_blk[:, lanes]))
        dv_sum.append(dot_f32(prob_bf, g_blk[:, lanes]))
    cross_dl = jnp.concatenate(cross_dl, axis=0)
    dk_sum = jnp.concatenate(dk_sum, axis=1) / group_rows
    dv_sum = jnp.concatenate(dv_sum, axis=1) / group_rows
    both, scaling, cross_dl, dk_sum, dv_sum = lax.optimization_barrier(
        (both, scaling, cross_dl, dk_sum, dv_sum)
    )
    core = jnp.reshape(own_core, (1,)).astype(jnp.int32)
    prob, dlogit, dq_own, dq_other = query_grads(
        logit_scale, core, both, scaling, k_blk, cross_dl, sum_k, rows_dev
    )
    dq_swapped = swap_core(dq_other)
    pieces = key_grads(prob, dlogit, q_blk, g_blk, dk_sum, dv_sum, ys)
    line = (dq_own + dq_swapped.astype(jnp.float32)).astype(jnp.bfloat16)
    line = line.reshape(XS, rows_dev, flat_width)
    line, pieces = lax.optimization_barrier((line, pieces))

    def line_piece(s):
        return lax.dynamic_index_in_dim(line, (own_x - s) % XS, axis=0, keepdims=False)

    def added(parts):
        return sum(p.astype(jnp.float32) for p in parts)

    grad_q = added([line_piece(0)] + [shift_x(line_piece(s), -s) for s in range(1, XS)])
    grad_kv = added([pieces[0]] + [shift_y(pieces[s], -s) for s in range(1, ys)])

    def finished(rows):
        return (
            jnp.where(keep_flat, rows, 0.0)
            .astype(jnp.bfloat16)
            .reshape(rows_dev, cols_dev, feature)
        )

    return (
        finished(grad_q),
        finished(grad_kv[:, :flat_width]),
        finished(grad_kv[:, flat_width:]),
    )


def solution(mesh):
    return jax.shard_map(
        shards,
        mesh=mesh,
        in_specs=(
            P("row", "col", None),
            P("row", "col", None),
            P("row", "col", None),
            P("row", "col", None),
            P("row"),
            P("row"),
        ),
        out_specs=(P("row", "col", None), P("row", "col", None), P("row", "col", None)),
        check_vma=False,
    )
```

```python
import math

import jax
import jax.numpy as jnp
from jax import lax
from jax.experimental import pallas as pl
from jax.experimental.layout import Layout, with_layout_constraint
from jax.experimental.pallas import tpu as pltpu
from jax.sharding import PartitionSpec as P

SUMMARIES = 256
XS = 4
FLAG_ROWS = 16

ROW_PAIR = (((1,), (1,)), ((), ()))
LEAD_PAIR = (((0,), (0,)), ((), ()))
PLAIN = (((1,), (0,)), ((), ()))

VMEM = pl.BlockSpec(memory_space=pltpu.VMEM)
SMEM = pl.BlockSpec(memory_space=pltpu.SMEM)
ROOM = pltpu.CompilerParams(vmem_limit_bytes=40 * 1024 * 1024)


def dot_f32(left, right, dims=PLAIN):
    return lax.dot_general(left, right, dims, preferred_element_type=jnp.float32)


def diagonal(n):
    return lax.broadcasted_iota(jnp.int32, (n, n), 0) == lax.broadcasted_iota(jnp.int32, (n, n), 1)


def across(column):
    return jnp.sum(jnp.where(diagonal(column.shape[0]), column, 0.0), axis=0, keepdims=True)


def upright(row):
    return jnp.sum(jnp.where(diagonal(row.shape[1]), row, 0.0), axis=1, keepdims=True)


def block_products(place, line, other_line, key_pieces, rows_dev, flat_width):
    lines = line.shape[0]
    block_rows, block_keys = 2 * lines * rows_dev, len(key_pieces) * rows_dev

    def kernel(place_ref, line_ref, other_ref, *refs):
        piece_refs, (qg_ref, kv_ref, logit_ref, dprob_ref) = refs[:-4], refs[-4:]
        core = place_ref[0]
        for s, piece_ref in enumerate(piece_refs):
            kv_ref[s * rows_dev : (s + 1) * rows_dev, :] = piece_ref[:rows_dev, :]
        for x in range(lines):
            mine = pl.multiple_of((2 * x + core) * rows_dev, rows_dev)
            theirs = pl.multiple_of((2 * x + 1 - core) * rows_dev, rows_dev)
            qg_ref[pl.ds(mine, rows_dev), :] = line_ref[x]
            qg_ref[pl.ds(theirs, rows_dev), :] = other_ref[x]
        logit_ref[...] = dot_f32(qg_ref[:, :flat_width], kv_ref[:, :flat_width], ROW_PAIR)
        dprob_ref[...] = dot_f32(qg_ref[:, flat_width:], kv_ref[:, flat_width:], ROW_PAIR).astype(
            jnp.bfloat16
        )

    return pl.pallas_call(
        kernel,
        in_specs=[SMEM] + [VMEM] * (2 + len(key_pieces)),
        out_shape=(
            jax.ShapeDtypeStruct((block_rows, 2 * flat_width), jnp.bfloat16),
            jax.ShapeDtypeStruct((block_keys, 2 * flat_width), jnp.bfloat16),
            jax.ShapeDtypeStruct((block_rows, block_keys), jnp.float32),
            jax.ShapeDtypeStruct((block_rows, block_keys), jnp.bfloat16),
        ),
        compiler_params=ROOM,
        name="block_products",
    )(place, line, other_line, *key_pieces)


def cross_scores(sums_ref, qg_ref, column, feature, inv_root):
    flat_width = qg_ref.shape[1] // 2
    lanes = slice(column * feature, (column + 1) * feature)
    other = slice(flat_width + column * feature, flat_width + (column + 1) * feature)
    scores = dot_f32(sums_ref[:, lanes], qg_ref[:, lanes], ROW_PAIR) * inv_root
    dprob = dot_f32(sums_ref[:, other], qg_ref[:, other], ROW_PAIR)
    return scores, dprob, lanes, other


def cross_statistics(qg_blk, kv_blk, tokens, feature, inv_root):
    block_keys, both_width = kv_blk.shape
    block_rows = qg_blk.shape[0]
    group = block_keys // tokens
    columns = both_width // (2 * feature)
    stat_rows = -(-3 * columns // 8) * 8

    def kernel(qg_ref, kv_ref, sums_ref, stat_ref):
        pooled = jnp.sum(
            kv_ref[...].astype(jnp.float32).reshape(tokens, group, both_width), axis=1
        )
        sums_ref[...] = (pooled / group).astype(jnp.bfloat16)
        for c in range(columns):
            scores, dprob, _, _ = cross_scores(sums_ref, qg_ref, c, feature, inv_root)
            peak = jnp.max(scores, axis=0, keepdims=True)
            lifted = jnp.exp(scores - peak)
            stat_ref[c : c + 1, :] = peak
            stat_ref[columns + c : columns + c + 1, :] = jnp.sum(lifted, axis=0, keepdims=True)
            stat_ref[2 * columns + c : 2 * columns + c + 1, :] = jnp.sum(
                lifted * dprob, axis=0, keepdims=True
            )
        if stat_rows > 3 * columns:
            stat_ref[3 * columns :, :] = jnp.zeros(
                (stat_rows - 3 * columns, block_rows), jnp.float32
            )

    return pl.pallas_call(
        kernel,
        in_specs=[VMEM] * 2,
        out_shape=(
            jax.ShapeDtypeStruct((tokens, both_width), jnp.bfloat16),
            jax.ShapeDtypeStruct((stat_rows, block_rows), jnp.float32),
        ),
        compiler_params=ROOM,
        name="cross_statistics",
    )(qg_blk, kv_blk)


def cross_grads(qg_blk, sums, all_stats, feature, inv_root):
    tokens, both_width = sums.shape
    block_rows = qg_blk.shape[0]
    columns = both_width // (2 * feature)

    def kernel(qg_ref, sums_ref, stat_ref, dl_ref, dsum_ref):
        peaks = stat_ref[:, :columns, :]
        peak = jnp.max(peaks, axis=0)
        weight = jnp.exp(peaks - peak[None])
        total = jnp.sum(weight * stat_ref[:, columns : 2 * columns, :], axis=0)
        delta = jnp.sum(weight * stat_ref[:, 2 * columns : 3 * columns, :], axis=0) / total
        for c in range(columns):
            scores, dprob, lanes, other = cross_scores(sums_ref, qg_ref, c, feature, inv_root)
            probs = jnp.exp(scores - peak[c : c + 1, :]) / total[c : c + 1, :]
            dl = (inv_root * probs * (dprob - delta[c : c + 1, :])).astype(jnp.bfloat16)
            dl_ref[c * tokens : (c + 1) * tokens, :] = dl
            dsum_ref[:, lanes] = dot_f32(dl, qg_ref[:, lanes])
            dsum_ref[:, other] = dot_f32(probs.astype(jnp.bfloat16), qg_ref[:, other])

    return pl.pallas_call(
        kernel,
        in_specs=[VMEM] * 3,
        out_shape=(
            jax.ShapeDtypeStruct((columns * tokens, block_rows), jnp.bfloat16),
            jax.ShapeDtypeStruct((tokens, both_width), jnp.float32),
        ),
        compiler_params=ROOM,
        name="cross_grads",
    )(qg_blk, sums, all_stats)


def block_softmax(logit_scale, logit_sum, own, forward, back, key_flags):
    rows, width = logit_sum.shape

    def kernel(logit_ref, own_ref, forward_ref, back_ref, flag_ref, both_ref, stat_ref):
        dprob = (
            own_ref[...].astype(jnp.float32)
            + forward_ref[...].astype(jnp.float32)
            + back_ref[...].astype(jnp.float32)
        )
        logits = jnp.where(flag_ref[...] > 0, logit_ref[...] * logit_scale, -1e30)
        peak = jnp.max(logits, axis=1, keepdims=True)
        lifted = jnp.exp(logits - peak)
        total = jnp.sum(lifted, axis=1, keepdims=True)
        weighted = jnp.sum(lifted * dprob, axis=1, keepdims=True)
        delta = weighted / total
        both_ref[:, :width] = lifted.astype(jnp.bfloat16)
        both_ref[:, width:] = (lifted * (dprob - delta)).astype(jnp.bfloat16)
        for i, column in enumerate((peak, total, weighted, delta)):
            stat_ref[i : i + 1, :] = across(column)
        stat_ref[4:8, :] = jnp.zeros((4, rows), jnp.float32)

    return pl.pallas_call(
        kernel,
        in_specs=[VMEM] * 5,
        out_shape=(
            jax.ShapeDtypeStruct((rows, 2 * width), jnp.bfloat16),
            jax.ShapeDtypeStruct((8, rows), jnp.float32),
        ),
        compiler_params=ROOM,
        name="block_softmax",
    )(logit_sum, own, forward, back, key_flags)


def query_grads(logit_scale, place, pieces, steps, scaling, kv_blk, cross_dl, sums):
    rows, width = pieces[0].shape[0], pieces[0].shape[1] // 2
    chunks = len(pieces)
    block_rows = chunks * rows
    flat_width = kv_blk.shape[1] // 2
    tokens = sums.shape[0]
    columns = cross_dl.shape[0] // tokens
    feature = flat_width // columns

    def kernel(place_ref, scale_ref, kv_ref, dl_ref, sums_ref, *refs):
        piece_refs = refs[:chunks]
        p_ref, ds_ref, own_ref, other_ref, dq_ref = refs[chunks:]
        core, own_z = place_ref[0], place_ref[1]
        for piece_ref, step in zip(piece_refs, steps):
            source = lax.rem(own_z + (2 * chunks - step), chunks)
            scale = scale_ref[source]
            weight, offset = upright(scale[0:1, :]), upright(scale[1:2, :])
            lifted = piece_ref[:, :width].astype(jnp.float32)
            tilted = piece_ref[:, width:].astype(jnp.float32)
            at = pl.ds(pl.multiple_of(source * rows, rows), rows)
            p_ref[at, :] = (lifted * weight).astype(jnp.bfloat16)
            ds_ref[at, :] = ((tilted - lifted * offset) * (weight * logit_scale)).astype(
                jnp.bfloat16
            )
        dq_ref[...] = dot_f32(ds_ref[...], kv_ref[:, :flat_width])
        for c in range(columns):
            lanes = slice(c * feature, (c + 1) * feature)
            dq_ref[:, lanes] += dot_f32(
                dl_ref[c * tokens : (c + 1) * tokens, :], sums_ref[:, lanes], LEAD_PAIR
            )
        for x in range(chunks // 2):
            to = slice(x * rows, (x + 1) * rows)
            mine = pl.multiple_of((2 * x + core) * rows, rows)
            theirs = pl.multiple_of((2 * x + 1 - core) * rows, rows)
            own_ref[to, :] = dq_ref[pl.ds(mine, rows), :]
            other_ref[to, :] = dq_ref[pl.ds(theirs, rows), :].astype(jnp.bfloat16)

    return pl.pallas_call(
        kernel,
        in_specs=[SMEM] + [VMEM] * (4 + chunks),
        out_shape=(
            jax.ShapeDtypeStruct((block_rows, width), jnp.bfloat16),
            jax.ShapeDtypeStruct((block_rows, width), jnp.bfloat16),
            jax.ShapeDtypeStruct((block_rows // 2, flat_width), jnp.float32),
            jax.ShapeDtypeStruct((block_rows // 2, flat_width), jnp.bfloat16),
        ),
        scratch_shapes=[pltpu.VMEM((block_rows, flat_width), jnp.float32)],
        compiler_params=ROOM,
        name="query_grads",
    )(place, scaling, kv_blk, cross_dl, sums, *pieces)


def key_grads(prob, dlogit, qg_blk, dsum, pieces):
    width, flat_width = prob.shape[1], qg_blk.shape[1] // 2
    tokens = dsum.shape[0]
    group = width // tokens
    piece = width // pieces

    def kernel(p_ref, ds_ref, qg_ref, dsum_ref, *out_refs):
        for half, w_ref in enumerate((ds_ref, p_ref)):
            lanes = slice(half * flat_width, (half + 1) * flat_width)
            grads = dot_f32(w_ref[...], qg_ref[:, lanes], LEAD_PAIR)
            shared = dsum_ref[:, lanes] / group
            grads = grads.reshape(tokens, group, flat_width) + shared[:, None, :]
            grads = grads.reshape(width, flat_width).astype(jnp.bfloat16)
            for s, out_ref in enumerate(out_refs):
                out_ref[:, lanes] = grads[s * piece : (s + 1) * piece]

    return pl.pallas_call(
        kernel,
        in_specs=[VMEM] * 4,
        out_shape=tuple(
            jax.ShapeDtypeStruct((piece, 2 * flat_width), jnp.bfloat16) for _ in range(pieces)
        ),
        compiler_params=ROOM,
        name="key_grads",
    )(prob, dlogit, qg_blk, dsum)


def shards(queries, keys, values, out_grad, row_keep, row_lengths):
    rows_dev, cols_dev, feature = queries.shape
    row_axis, zs = lax.axis_size("row"), lax.axis_size("col")
    ys = row_axis // (2 * XS)
    near_size = 2 * XS
    total_rows = rows_dev * row_axis
    total_cols = cols_dev * zs
    group_rows = total_rows // SUMMARIES
    flat_width = cols_dev * feature
    block_rows = near_size * rows_dev
    block_keys = ys * rows_dev
    tokens = block_keys // group_rows
    near = [[y * near_size + i for i in range(near_size)] for y in range(ys)]
    own_x = (lax.axis_index("row") // 2) % XS
    own_core = lax.axis_index("row") % 2
    own_z = lax.axis_index("col")
    place = jnp.stack([own_core, own_z]).astype(jnp.int32)
    logit_scale = 1.0 / math.sqrt(total_cols * feature)
    inv_root = 1.0 / math.sqrt(feature)

    def at(y, x, core):
        return ((y % ys) * XS + x % XS) * 2 + core

    cells = [(y, x, c) for y in range(ys) for x in range(XS) for c in range(2)]

    def shift_y(table, step):
        return lax.ppermute(table, "row", [(at(y, x, c), at(y + step, x, c)) for y, x, c in cells])

    def shift_x(table, step):
        return lax.ppermute(table, "row", [(at(y, x, c), at(y, x + step, c)) for y, x, c in cells])

    def swap_core(table):
        return lax.ppermute(table, "row", [(at(y, x, c), at(y, x, 1 - c)) for y, x, c in cells])

    def shift_z(table, step):
        return lax.ppermute(table, "col", [(z, (z + step) % zs) for z in range(zs)])

    def share(table, axis, groups=None):
        count = lax.axis_size(axis) if groups is None else len(groups[0])
        copies = jnp.broadcast_to(table[None], (count,) + table.shape)
        return lax.all_to_all(
            copies, axis, split_axis=0, concat_axis=0, tiled=True, axis_index_groups=groups
        )

    column_ids = own_z * cols_dev + jnp.arange(cols_dev, dtype=jnp.int32)
    cell_keep = (row_keep[:, None] == 1) & (column_ids[None, :] < row_lengths[:, None])
    keep_flat = jnp.broadcast_to(cell_keep[:, :, None], queries.shape).reshape(
        rows_dev, flat_width
    )
    zero = jnp.zeros((), queries.dtype)

    def masked(first, second):
        tables = (t.reshape(rows_dev, flat_width) for t in (first, second))
        flat = jnp.concatenate([jnp.where(keep_flat, t, zero) for t in tables], axis=1)
        return with_layout_constraint(flat, Layout((0, 1)))

    qg_flat = masked(queries, out_grad)
    flag_rows = jnp.pad(
        row_keep.astype(jnp.bfloat16)[None, :],
        ((0, FLAG_ROWS - 1), (0, 2 * flat_width - rows_dev)),
    )
    kv_flat = jnp.concatenate([masked(keys, values), flag_rows], axis=0)
    qg_flat, kv_flat = lax.optimization_barrier((qg_flat, kv_flat))
    order = (1, XS - 1, 2)
    query_pieces = {0: qg_flat} | {s: shift_x(qg_flat, s) for s in order}
    key_pieces = [kv_flat] + [shift_y(kv_flat, s) for s in range(1, ys)]
    query_pieces, key_pieces = lax.optimization_barrier((query_pieces, key_pieces))
    line = jnp.zeros((XS, rows_dev, 2 * flat_width), queries.dtype)
    for s, piece in query_pieces.items():
        line = lax.dynamic_update_slice(line, piece[None], ((own_x - s) % XS, 0, 0))
    qg_blk, kv_blk, logit_piece, dprob_piece = block_products(
        place, line, swap_core(line), key_pieces, rows_dev, flat_width
    )
    key_flags = jnp.concatenate([p[rows_dev, :rows_dev] for p in key_pieces])[None, :]
    logit_sum = lax.psum_scatter(logit_piece, "col", scatter_dimension=0, tiled=True)

    dprob_chunks = dprob_piece.reshape(zs, block_rows // zs, block_keys)

    def part(step):
        return lax.dynamic_index_in_dim(dprob_chunks, (own_z + step) % zs, axis=0, keepdims=False)

    def passed(step, count):
        moving = part(step * count)
        for left in range(count - 1, -1, -1):
            moving = shift_z(moving, step)
            if left > 0:
                moving = (
                    moving.astype(jnp.float32) + part(step * left).astype(jnp.float32)
                ).astype(jnp.bfloat16)
        return moving

    dprob_forward = passed(1, zs // 2)
    dprob_back = passed(-1, zs - 1 - zs // 2)

    sums, own_stats = cross_statistics(qg_blk, kv_blk, tokens, feature, inv_root)
    cross_dl, dsum = cross_grads(
        qg_blk, sums, share(own_stats, "row", near), feature, inv_root
    )

    both, stats = block_softmax(
        logit_scale, logit_sum, part(0), dprob_forward, dprob_back, key_flags
    )
    both, stats, cross_dl, dsum = lax.optimization_barrier((both, stats, cross_dl, dsum))
    forward, back = [both], []
    for _ in range(zs // 2):
        forward.append(shift_z(forward[-1], 1))
    for _ in range(zs - 1 - zs // 2):
        back.append(shift_z(back[-1] if back else both, -1))
    pieces = forward + back
    steps = list(range(zs // 2 + 1)) + [-s for s in range(1, zs - zs // 2)]

    all_stats = share(stats, "row", near)
    weight = jnp.exp(all_stats[:, 0] - jnp.max(all_stats[:, 0], axis=0))
    total = jnp.sum(weight * all_stats[:, 1], axis=0)
    delta = jnp.sum(weight * all_stats[:, 2], axis=0) / total
    own_weight = jnp.exp(stats[0] - jnp.max(all_stats[:, 0], axis=0)) / total
    scaling = share(jnp.stack([own_weight, delta - stats[3]]), "col")

    prob, dlogit, dq_own, dq_other = query_grads(
        logit_scale, place, pieces, steps, scaling, kv_blk, cross_dl, sums
    )
    dq_swapped = swap_core(dq_other)
    key_parts = key_grads(prob, dlogit, qg_blk, dsum, ys)
    key_moved = [shift_y(key_parts[s], -s) for s in range(1, ys)]
    line = (dq_own + dq_swapped.astype(jnp.float32)).astype(jnp.bfloat16)
    line = line.reshape(XS, rows_dev, flat_width)
    line, key_moved[0] = lax.optimization_barrier((line, key_moved[0]))

    def line_piece(s):
        return lax.dynamic_index_in_dim(line, (own_x - s) % XS, axis=0, keepdims=False)

    def added(parts):
        return sum(p.astype(jnp.float32) for p in parts)

    grad_q = added([line_piece(0)] + [shift_x(line_piece(s), -s) for s in range(1, XS)])
    grad_kv = added([key_parts[0]] + key_moved)

    def finished(rows):
        return (
            jnp.where(keep_flat, rows, 0.0)
            .astype(jnp.bfloat16)
            .reshape(rows_dev, cols_dev, feature)
        )

    return (
        finished(grad_q),
        finished(grad_kv[:, :flat_width]),
        finished(grad_kv[:, flat_width:]),
    )


def solution(mesh):
    return jax.shard_map(
        shards,
        mesh=mesh,
        in_specs=(
            P("row", "col", None),
            P("row", "col", None),
            P("row", "col", None),
            P("row", "col", None),
            P("row"),
            P("row"),
        ),
        out_specs=(P("row", "col", None), P("row", "col", None), P("row", "col", None)),
        check_vma=False,
    )
```

```python
import math

import jax
import jax.numpy as jnp
from jax import lax
from jax.experimental import pallas as pl
from jax.experimental.layout import Layout, with_layout_constraint
from jax.experimental.pallas import tpu as pltpu
from jax.sharding import PartitionSpec as P

SUMMARIES = 256
XS = 4
FLAG_ROWS = 16

ROW_PAIR = (((1,), (1,)), ((), ()))
LEAD_PAIR = (((0,), (0,)), ((), ()))
PLAIN = (((1,), (0,)), ((), ()))

WHOLE = pl.BlockSpec()
SMEM = pl.BlockSpec(memory_space=pltpu.SMEM)
ROOM = pltpu.CompilerParams(vmem_limit_bytes=24 * 1024 * 1024)


def dot_f32(left, right, dims=PLAIN):
    return lax.dot_general(left, right, dims, preferred_element_type=jnp.float32)


def diagonal(n):
    return lax.broadcasted_iota(jnp.int32, (n, n), 0) == lax.broadcasted_iota(jnp.int32, (n, n), 1)


def across(column):
    return jnp.sum(jnp.where(diagonal(column.shape[0]), column, 0.0), axis=0, keepdims=True)


def upright(row):
    return jnp.sum(jnp.where(diagonal(row.shape[1]), row, 0.0), axis=1, keepdims=True)


def cross_scores(sums_ref, q_ref, g_ref, column, feature, inv_root):
    flat_width = q_ref.shape[1]
    lanes = slice(column * feature, (column + 1) * feature)
    other = slice(flat_width + column * feature, flat_width + (column + 1) * feature)
    scores = dot_f32(sums_ref[:, lanes], q_ref[:, lanes], ROW_PAIR) * inv_root
    dprob = dot_f32(sums_ref[:, other], g_ref[:, lanes], ROW_PAIR)
    return scores, dprob, lanes, other


def cross_statistics(q_blk, g_blk, k_blk, v_blk, tokens, feature, inv_root):
    block_keys, flat_width = k_blk.shape
    both_width = 2 * flat_width
    block_rows = q_blk.shape[0]
    group = block_keys // tokens
    columns = both_width // (2 * feature)
    stat_rows = -(-3 * columns // 8) * 8

    def kernel(q_ref, g_ref, k_ref, v_ref, sums_ref, stat_ref):
        for half, table_ref in enumerate((k_ref, v_ref)):
            pooled = jnp.sum(
                table_ref[...].astype(jnp.float32).reshape(tokens, group, flat_width), axis=1
            )
            sums_ref[:, half * flat_width : (half + 1) * flat_width] = (pooled / group).astype(
                jnp.bfloat16
            )
        for c in range(columns):
            scores, dprob, _, _ = cross_scores(sums_ref, q_ref, g_ref, c, feature, inv_root)
            peak = jnp.max(scores, axis=0, keepdims=True)
            lifted = jnp.exp(scores - peak)
            stat_ref[c : c + 1, :] = peak
            stat_ref[columns + c : columns + c + 1, :] = jnp.sum(lifted, axis=0, keepdims=True)
            stat_ref[2 * columns + c : 2 * columns + c + 1, :] = jnp.sum(
                lifted * dprob, axis=0, keepdims=True
            )
        if stat_rows > 3 * columns:
            stat_ref[3 * columns :, :] = jnp.zeros(
                (stat_rows - 3 * columns, block_rows), jnp.float32
            )

    return pl.pallas_call(
        kernel,
        out_shape=(
            jax.ShapeDtypeStruct((tokens, both_width), jnp.bfloat16),
            jax.ShapeDtypeStruct((stat_rows, block_rows), jnp.float32),
        ),
        compiler_params=ROOM,
        name="cross_statistics",
    )(q_blk, g_blk, k_blk, v_blk)


def cross_grads(q_blk, g_blk, sums, all_stats, feature, inv_root):
    tokens, both_width = sums.shape
    block_rows = q_blk.shape[0]
    columns = both_width // (2 * feature)

    def kernel(q_ref, g_ref, sums_ref, stat_ref, dl_ref, dsum_ref):
        peaks = stat_ref[:, :columns, :]
        peak = jnp.max(peaks, axis=0)
        weight = jnp.exp(peaks - peak[None])
        total = jnp.sum(weight * stat_ref[:, columns : 2 * columns, :], axis=0)
        delta = jnp.sum(weight * stat_ref[:, 2 * columns : 3 * columns, :], axis=0) / total
        for c in range(columns):
            scores, dprob, lanes, other = cross_scores(sums_ref, q_ref, g_ref, c, feature, inv_root)
            probs = jnp.exp(scores - peak[c : c + 1, :]) / total[c : c + 1, :]
            dl = (inv_root * probs * (dprob - delta[c : c + 1, :])).astype(jnp.bfloat16)
            dl_ref[c * tokens : (c + 1) * tokens, :] = dl
            dsum_ref[:, lanes] = dot_f32(dl, q_ref[:, lanes])
            dsum_ref[:, other] = dot_f32(probs.astype(jnp.bfloat16), g_ref[:, lanes])

    return pl.pallas_call(
        kernel,
        out_shape=(
            jax.ShapeDtypeStruct((columns * tokens, block_rows), jnp.bfloat16),
            jax.ShapeDtypeStruct((tokens, both_width), jnp.float32),
        ),
        compiler_params=ROOM,
        name="cross_grads",
    )(q_blk, g_blk, sums, all_stats)


def block_softmax(logit_scale, logit_sum, own, forward, back, key_flags):
    rows, width = logit_sum.shape

    def kernel(logit_ref, own_ref, forward_ref, back_ref, flag_ref, both_ref, stat_ref):
        dprob = (
            own_ref[...].astype(jnp.float32)
            + forward_ref[...].astype(jnp.float32)
            + back_ref[...].astype(jnp.float32)
        )
        logits = jnp.where(flag_ref[...] > 0, logit_ref[...] * logit_scale, -1e30)
        peak = jnp.max(logits, axis=1, keepdims=True)
        lifted = jnp.exp(logits - peak)
        total = jnp.sum(lifted, axis=1, keepdims=True)
        weighted = jnp.sum(lifted * dprob, axis=1, keepdims=True)
        delta = weighted / total
        both_ref[:, :width] = lifted.astype(jnp.bfloat16)
        both_ref[:, width:] = (lifted * (dprob - delta)).astype(jnp.bfloat16)
        for i, column in enumerate((peak, total, weighted, delta)):
            stat_ref[i : i + 1, :] = across(column)
        stat_ref[4:8, :] = jnp.zeros((4, rows), jnp.float32)

    return pl.pallas_call(
        kernel,
        out_shape=(
            jax.ShapeDtypeStruct((rows, 2 * width), jnp.bfloat16),
            jax.ShapeDtypeStruct((8, rows), jnp.float32),
        ),
        compiler_params=ROOM,
        name="block_softmax",
    )(logit_sum, own, forward, back, key_flags)


def query_grads(logit_scale, place, both, scaling, k_blk, cross_dl, sums, chunks):
    block_rows, width = both.shape[0], both.shape[1] // 2
    rows = block_rows // chunks
    flat_width = k_blk.shape[1]
    tokens = sums.shape[0]
    columns = cross_dl.shape[0] // tokens
    feature = flat_width // columns

    def kernel(place_ref, both_ref, scale_ref, k_ref, dl_ref, sums_ref, p_ref, ds_ref, own_ref, other_ref, dq_ref):
        core = place_ref[0]
        for i in range(chunks):
            at = slice(i * rows, (i + 1) * rows)
            weight, offset = upright(scale_ref[i, 0:1, :]), upright(scale_ref[i, 1:2, :])
            lifted = both_ref[at, :width].astype(jnp.float32)
            tilted = both_ref[at, width:].astype(jnp.float32)
            p_ref[at, :] = (lifted * weight).astype(jnp.bfloat16)
            ds_ref[at, :] = ((tilted - lifted * offset) * (weight * logit_scale)).astype(
                jnp.bfloat16
            )
        dq_ref[...] = dot_f32(ds_ref[...], k_ref[...])
        for c in range(columns):
            lanes = slice(c * feature, (c + 1) * feature)
            dq_ref[:, lanes] += dot_f32(
                dl_ref[c * tokens : (c + 1) * tokens, :], sums_ref[:, lanes], LEAD_PAIR
            )
        for x in range(chunks // 2):
            to = slice(x * rows, (x + 1) * rows)
            mine = pl.multiple_of((2 * x + core) * rows, rows)
            theirs = pl.multiple_of((2 * x + 1 - core) * rows, rows)
            own_ref[to, :] = dq_ref[pl.ds(mine, rows), :]
            other_ref[to, :] = dq_ref[pl.ds(theirs, rows), :].astype(jnp.bfloat16)

    return pl.pallas_call(
        kernel,
        in_specs=[SMEM] + [WHOLE] * 5,
        out_shape=(
            jax.ShapeDtypeStruct((block_rows, width), jnp.bfloat16),
            jax.ShapeDtypeStruct((block_rows, width), jnp.bfloat16),
            jax.ShapeDtypeStruct((block_rows // 2, flat_width), jnp.float32),
            jax.ShapeDtypeStruct((block_rows // 2, flat_width), jnp.bfloat16),
        ),
        scratch_shapes=[pltpu.VMEM((block_rows, flat_width), jnp.float32)],
        compiler_params=ROOM,
        name="query_grads",
    )(place, both, scaling, k_blk, cross_dl, sums)


def key_grads(prob, dlogit, q_blk, g_blk, dsum, pieces):
    width, flat_width = prob.shape[1], q_blk.shape[1]
    tokens = dsum.shape[0]
    group = width // tokens
    piece = width // pieces

    def kernel(p_ref, ds_ref, q_ref, g_ref, dsum_ref, *out_refs):
        for half, (w_ref, t_ref) in enumerate(((ds_ref, q_ref), (p_ref, g_ref))):
            lanes = slice(half * flat_width, (half + 1) * flat_width)
            grads = dot_f32(w_ref[...], t_ref[...], LEAD_PAIR)
            shared = dsum_ref[:, lanes] / group
            grads = grads.reshape(tokens, group, flat_width) + shared[:, None, :]
            grads = grads.reshape(width, flat_width).astype(jnp.bfloat16)
            for s, out_ref in enumerate(out_refs):
                out_ref[:, lanes] = grads[s * piece : (s + 1) * piece]

    return pl.pallas_call(
        kernel,
        out_shape=tuple(
            jax.ShapeDtypeStruct((piece, 2 * flat_width), jnp.bfloat16) for _ in range(pieces)
        ),
        compiler_params=ROOM,
        name="key_grads",
    )(prob, dlogit, q_blk, g_blk, dsum)


def shards(queries, keys, values, out_grad, row_keep, row_lengths):
    rows_dev, cols_dev, feature = queries.shape
    row_axis, zs = lax.axis_size("row"), lax.axis_size("col")
    ys = row_axis // (2 * XS)
    near_size = 2 * XS
    total_rows = rows_dev * row_axis
    total_cols = cols_dev * zs
    group_rows = total_rows // SUMMARIES
    flat_width = cols_dev * feature
    block_rows = near_size * rows_dev
    block_keys = ys * rows_dev
    tokens = block_keys // group_rows
    near = [[y * near_size + i for i in range(near_size)] for y in range(ys)]
    own_x = (lax.axis_index("row") // 2) % XS
    own_core = lax.axis_index("row") % 2
    own_z = lax.axis_index("col")
    place = jnp.stack([own_core, own_z]).astype(jnp.int32)
    logit_scale = 1.0 / math.sqrt(total_cols * feature)
    inv_root = 1.0 / math.sqrt(feature)

    def at(y, x, core):
        return ((y % ys) * XS + x % XS) * 2 + core

    cells = [(y, x, c) for y in range(ys) for x in range(XS) for c in range(2)]

    def shift_y(table, step):
        return lax.ppermute(table, "row", [(at(y, x, c), at(y + step, x, c)) for y, x, c in cells])

    def shift_x(table, step):
        return lax.ppermute(table, "row", [(at(y, x, c), at(y, x + step, c)) for y, x, c in cells])

    def swap_core(table):
        return lax.ppermute(table, "row", [(at(y, x, c), at(y, x, 1 - c)) for y, x, c in cells])

    def shift_z(table, step):
        return lax.ppermute(table, "col", [(z, (z + step) % zs) for z in range(zs)])

    def share(table, axis, groups=None):
        count = lax.axis_size(axis) if groups is None else len(groups[0])
        copies = jnp.broadcast_to(table[None], (count,) + table.shape)
        return lax.all_to_all(
            copies, axis, split_axis=0, concat_axis=0, tiled=True, axis_index_groups=groups
        )

    column_ids = own_z * cols_dev + jnp.arange(cols_dev, dtype=jnp.int32)
    cell_keep = (row_keep[:, None] == 1) & (column_ids[None, :] < row_lengths[:, None])
    keep_flat = jnp.broadcast_to(cell_keep[:, :, None], queries.shape).reshape(
        rows_dev, flat_width
    )
    zero = jnp.zeros((), queries.dtype)

    def masked(first, second):
        tables = (t.reshape(rows_dev, flat_width) for t in (first, second))
        flat = jnp.concatenate([jnp.where(keep_flat, t, zero) for t in tables], axis=1)
        return with_layout_constraint(flat, Layout((0, 1)))

    qg_flat = masked(queries, out_grad)
    flag_rows = jnp.pad(
        row_keep.astype(jnp.bfloat16)[None, :],
        ((0, FLAG_ROWS - 1), (0, 2 * flat_width - rows_dev)),
    )
    kv_flat = jnp.concatenate([masked(keys, values), flag_rows], axis=0)
    qg_flat, kv_flat = lax.optimization_barrier((qg_flat, kv_flat))
    order = (1, XS - 1, 2)
    query_pieces = {0: qg_flat} | {s: shift_x(qg_flat, s) for s in order}
    key_pieces = [kv_flat] + [shift_y(kv_flat, s) for s in range(1, ys)]
    query_pieces, key_pieces = lax.optimization_barrier((query_pieces, key_pieces))
    halves = (slice(0, flat_width), slice(flat_width, 2 * flat_width))

    def query_block(half):
        line = jnp.zeros((XS, rows_dev, flat_width), queries.dtype)
        for s, piece in query_pieces.items():
            line = lax.dynamic_update_slice(line, piece[None, :, half], ((own_x - s) % XS, 0, 0))
        other = swap_core(line)
        first = jnp.where(own_core == 0, line, other)
        second = jnp.where(own_core == 0, other, line)
        return jnp.stack([first, second], axis=1).reshape(block_rows, flat_width)

    def key_block(half):
        return jnp.concatenate([p[:rows_dev, half] for p in key_pieces], axis=0)

    q_blk, g_blk = query_block(halves[0]), query_block(halves[1])
    k_blk, v_blk = key_block(halves[0]), key_block(halves[1])
    logit_piece = dot_f32(q_blk, k_blk, ROW_PAIR)
    g_blk, _ = lax.optimization_barrier((g_blk, logit_piece))
    dprob_piece = dot_f32(g_blk, v_blk, ROW_PAIR).astype(jnp.bfloat16)
    key_flags = jnp.concatenate([p[rows_dev, :rows_dev] for p in key_pieces])[None, :]
    logit_sum = lax.psum_scatter(logit_piece, "col", scatter_dimension=0, tiled=True)

    dprob_chunks = dprob_piece.reshape(zs, block_rows // zs, block_keys)

    def part(step):
        return lax.dynamic_index_in_dim(dprob_chunks, (own_z + step) % zs, axis=0, keepdims=False)

    def passed(step, count):
        moving = part(step * count)
        for left in range(count - 1, -1, -1):
            moving = shift_z(moving, step)
            if left > 0:
                moving = (
                    moving.astype(jnp.float32) + part(step * left).astype(jnp.float32)
                ).astype(jnp.bfloat16)
        return moving

    dprob_forward = passed(1, zs // 2)
    dprob_back = passed(-1, zs - 1 - zs // 2)

    sums, own_stats = cross_statistics(q_blk, g_blk, k_blk, v_blk, tokens, feature, inv_root)
    cross_dl, dsum = cross_grads(
        q_blk, g_blk, sums, share(own_stats, "row", near), feature, inv_root
    )

    both, stats = block_softmax(
        logit_scale, logit_sum, part(0), dprob_forward, dprob_back, key_flags
    )
    both, stats, cross_dl, dsum = lax.optimization_barrier((both, stats, cross_dl, dsum))
    both = lax.all_gather(both, "col", axis=0, tiled=True)
    all_stats = share(stats, "row", near)
    weight = jnp.exp(all_stats[:, 0] - jnp.max(all_stats[:, 0], axis=0))
    total = jnp.sum(weight * all_stats[:, 1], axis=0)
    delta = jnp.sum(weight * all_stats[:, 2], axis=0) / total
    own_weight = jnp.exp(stats[0] - jnp.max(all_stats[:, 0], axis=0)) / total
    scaling = share(jnp.stack([own_weight, delta - stats[3]]), "col")

    prob, dlogit, dq_own, dq_other = query_grads(
        logit_scale, place, both, scaling, k_blk, cross_dl, sums, zs
    )
    dq_swapped = swap_core(dq_other)
    key_parts = key_grads(prob, dlogit, q_blk, g_blk, dsum, ys)
    key_moved = [shift_y(key_parts[s], -s) for s in range(1, ys)]
    line = (dq_own + dq_swapped.astype(jnp.float32)).astype(jnp.bfloat16)
    line = line.reshape(XS, rows_dev, flat_width)
    line, key_moved[0] = lax.optimization_barrier((line, key_moved[0]))

    def line_piece(s):
        return lax.dynamic_index_in_dim(line, (own_x - s) % XS, axis=0, keepdims=False)

    def added(parts):
        return sum(p.astype(jnp.float32) for p in parts)

    grad_q = added([line_piece(0)] + [shift_x(line_piece(s), -s) for s in range(1, XS)])
    grad_kv = added([key_parts[0]] + key_moved)

    def finished(rows):
        return (
            jnp.where(keep_flat, rows, 0.0)
            .astype(jnp.bfloat16)
            .reshape(rows_dev, cols_dev, feature)
        )

    return (
        finished(grad_q),
        finished(grad_kv[:, :flat_width]),
        finished(grad_kv[:, flat_width:]),
    )


def solution(mesh):
    return jax.shard_map(
        shards,
        mesh=mesh,
        in_specs=(
            P("row", "col", None),
            P("row", "col", None),
            P("row", "col", None),
            P("row", "col", None),
            P("row"),
            P("row"),
        ),
        out_specs=(P("row", "col", None), P("row", "col", None), P("row", "col", None)),
        check_vma=False,
    )
```

```python
import math

import jax
import jax.numpy as jnp
from jax import lax
from jax.experimental import pallas as pl
from jax.experimental.layout import Layout, with_layout_constraint
from jax.experimental.pallas import tpu as pltpu
from jax.sharding import PartitionSpec as P

SUMMARIES = 256
XS = 4
FLAG_ROWS = 16

ROW_PAIR = (((1,), (1,)), ((), ()))
LEAD_PAIR = (((0,), (0,)), ((), ()))
PLAIN = (((1,), (0,)), ((), ()))

WHOLE = pl.BlockSpec()
SMEM = pl.BlockSpec(memory_space=pltpu.SMEM)
ROOM = pltpu.CompilerParams(vmem_limit_bytes=24 * 1024 * 1024)


def dot_f32(left, right, dims=PLAIN):
    return lax.dot_general(left, right, dims, preferred_element_type=jnp.float32)


def diagonal(n):
    return lax.broadcasted_iota(jnp.int32, (n, n), 0) == lax.broadcasted_iota(jnp.int32, (n, n), 1)


def across(column):
    return jnp.sum(jnp.where(diagonal(column.shape[0]), column, 0.0), axis=0, keepdims=True)


def upright(row):
    return jnp.sum(jnp.where(diagonal(row.shape[1]), row, 0.0), axis=1, keepdims=True)


def cross_scores(sums_ref, q_ref, g_ref, column, feature, inv_root):
    flat_width = q_ref.shape[1]
    lanes = slice(column * feature, (column + 1) * feature)
    other = slice(flat_width + column * feature, flat_width + (column + 1) * feature)
    scores = dot_f32(sums_ref[:, lanes], q_ref[:, lanes], ROW_PAIR) * inv_root
    dprob = dot_f32(sums_ref[:, other], g_ref[:, lanes], ROW_PAIR)
    return scores, dprob, lanes, other


def cross_statistics(q_blk, g_blk, k_blk, v_blk, tokens, feature, inv_root):
    block_keys, flat_width = k_blk.shape
    both_width = 2 * flat_width
    block_rows = q_blk.shape[0]
    group = block_keys // tokens
    columns = both_width // (2 * feature)
    stat_rows = -(-3 * columns // 8) * 8

    def kernel(q_ref, g_ref, k_ref, v_ref, sums_ref, stat_ref):
        for half, table_ref in enumerate((k_ref, v_ref)):
            pooled = jnp.sum(
                table_ref[...].astype(jnp.float32).reshape(tokens, group, flat_width), axis=1
            )
            sums_ref[:, half * flat_width : (half + 1) * flat_width] = (pooled / group).astype(
                jnp.bfloat16
            )
        for c in range(columns):
            scores, dprob, _, _ = cross_scores(sums_ref, q_ref, g_ref, c, feature, inv_root)
            peak = jnp.max(scores, axis=0, keepdims=True)
            lifted = jnp.exp(scores - peak)
            stat_ref[c : c + 1, :] = peak
            stat_ref[columns + c : columns + c + 1, :] = jnp.sum(lifted, axis=0, keepdims=True)
            stat_ref[2 * columns + c : 2 * columns + c + 1, :] = jnp.sum(
                lifted * dprob, axis=0, keepdims=True
            )
        if stat_rows > 3 * columns:
            stat_ref[3 * columns :, :] = jnp.zeros(
                (stat_rows - 3 * columns, block_rows), jnp.float32
            )

    return pl.pallas_call(
        kernel,
        out_shape=(
            jax.ShapeDtypeStruct((tokens, both_width), jnp.bfloat16),
            jax.ShapeDtypeStruct((stat_rows, block_rows), jnp.float32),
        ),
        compiler_params=ROOM,
        name="cross_statistics",
    )(q_blk, g_blk, k_blk, v_blk)


def cross_grads(q_blk, g_blk, sums, all_stats, feature, inv_root):
    tokens, both_width = sums.shape
    block_rows = q_blk.shape[0]
    columns = both_width // (2 * feature)

    def kernel(q_ref, g_ref, sums_ref, stat_ref, dl_ref, dsum_ref):
        peaks = stat_ref[:, :columns, :]
        peak = jnp.max(peaks, axis=0)
        weight = jnp.exp(peaks - peak[None])
        total = jnp.sum(weight * stat_ref[:, columns : 2 * columns, :], axis=0)
        delta = jnp.sum(weight * stat_ref[:, 2 * columns : 3 * columns, :], axis=0) / total
        for c in range(columns):
            scores, dprob, lanes, other = cross_scores(sums_ref, q_ref, g_ref, c, feature, inv_root)
            probs = jnp.exp(scores - peak[c : c + 1, :]) / total[c : c + 1, :]
            dl = (inv_root * probs * (dprob - delta[c : c + 1, :])).astype(jnp.bfloat16)
            dl_ref[c * tokens : (c + 1) * tokens, :] = dl
            dsum_ref[:, lanes] = dot_f32(dl, q_ref[:, lanes])
            dsum_ref[:, other] = dot_f32(probs.astype(jnp.bfloat16), g_ref[:, lanes])

    return pl.pallas_call(
        kernel,
        out_shape=(
            jax.ShapeDtypeStruct((columns * tokens, block_rows), jnp.bfloat16),
            jax.ShapeDtypeStruct((tokens, both_width), jnp.float32),
        ),
        compiler_params=ROOM,
        name="cross_grads",
    )(q_blk, g_blk, sums, all_stats)


def block_softmax(logit_scale, logit_sum, own, forward, back, key_flags):
    rows, width = logit_sum.shape

    def kernel(logit_ref, own_ref, forward_ref, back_ref, flag_ref, both_ref, stat_ref):
        dprob = (
            own_ref[...].astype(jnp.float32)
            + forward_ref[...].astype(jnp.float32)
            + back_ref[...].astype(jnp.float32)
        )
        logits = jnp.where(flag_ref[...] > 0, logit_ref[...] * logit_scale, -1e30)
        peak = jnp.max(logits, axis=1, keepdims=True)
        lifted = jnp.exp(logits - peak)
        total = jnp.sum(lifted, axis=1, keepdims=True)
        weighted = jnp.sum(lifted * dprob, axis=1, keepdims=True)
        delta = weighted / total
        both_ref[:, :width] = lifted.astype(jnp.bfloat16)
        both_ref[:, width:] = (lifted * (dprob - delta)).astype(jnp.bfloat16)
        for i, column in enumerate((peak, total, weighted, delta)):
            stat_ref[i : i + 1, :] = across(column)
        stat_ref[4:8, :] = jnp.zeros((4, rows), jnp.float32)

    return pl.pallas_call(
        kernel,
        out_shape=(
            jax.ShapeDtypeStruct((rows, 2 * width), jnp.bfloat16),
            jax.ShapeDtypeStruct((8, rows), jnp.float32),
        ),
        compiler_params=ROOM,
        name="block_softmax",
    )(logit_sum, own, forward, back, key_flags)


def query_grads(logit_scale, place, both, scaling, k_blk, cross_dl, sums, chunks):
    block_rows, width = both.shape[0], both.shape[1] // 2
    rows = block_rows // chunks
    flat_width = k_blk.shape[1]
    tokens = sums.shape[0]
    columns = cross_dl.shape[0] // tokens
    feature = flat_width // columns

    def kernel(place_ref, both_ref, scale_ref, k_ref, dl_ref, sums_ref, p_ref, ds_ref, own_ref, other_ref, dq_ref):
        core = place_ref[0]
        for i in range(chunks):
            at = slice(i * rows, (i + 1) * rows)
            weight, offset = upright(scale_ref[i, 0:1, :]), upright(scale_ref[i, 1:2, :])
            lifted = both_ref[at, :width].astype(jnp.float32)
            tilted = both_ref[at, width:].astype(jnp.float32)
            p_ref[at, :] = (lifted * weight).astype(jnp.bfloat16)
            ds_ref[at, :] = ((tilted - lifted * offset) * (weight * logit_scale)).astype(
                jnp.bfloat16
            )
        dq_ref[...] = dot_f32(ds_ref[...], k_ref[...])
        for c in range(columns):
            lanes = slice(c * feature, (c + 1) * feature)
            dq_ref[:, lanes] += dot_f32(
                dl_ref[c * tokens : (c + 1) * tokens, :], sums_ref[:, lanes], LEAD_PAIR
            )
        for x in range(chunks // 2):
            to = slice(x * rows, (x + 1) * rows)
            mine = pl.multiple_of((2 * x + core) * rows, rows)
            theirs = pl.multiple_of((2 * x + 1 - core) * rows, rows)
            own_ref[to, :] = dq_ref[pl.ds(mine, rows), :]
            other_ref[to, :] = dq_ref[pl.ds(theirs, rows), :].astype(jnp.bfloat16)

    return pl.pallas_call(
        kernel,
        in_specs=[SMEM] + [WHOLE] * 5,
        out_shape=(
            jax.ShapeDtypeStruct((block_rows, width), jnp.bfloat16),
            jax.ShapeDtypeStruct((block_rows, width), jnp.bfloat16),
            jax.ShapeDtypeStruct((block_rows // 2, flat_width), jnp.float32),
            jax.ShapeDtypeStruct((block_rows // 2, flat_width), jnp.bfloat16),
        ),
        scratch_shapes=[pltpu.VMEM((block_rows, flat_width), jnp.float32)],
        compiler_params=ROOM,
        name="query_grads",
    )(place, both, scaling, k_blk, cross_dl, sums)


def key_grads(prob, dlogit, q_blk, g_blk, dsum, pieces):
    width, flat_width = prob.shape[1], q_blk.shape[1]
    tokens = dsum.shape[0]
    group = width // tokens
    piece = width // pieces

    def kernel(p_ref, ds_ref, q_ref, g_ref, dsum_ref, *out_refs):
        for half, (w_ref, t_ref) in enumerate(((ds_ref, q_ref), (p_ref, g_ref))):
            lanes = slice(half * flat_width, (half + 1) * flat_width)
            grads = dot_f32(w_ref[...], t_ref[...], LEAD_PAIR)
            shared = dsum_ref[:, lanes] / group
            grads = grads.reshape(tokens, group, flat_width) + shared[:, None, :]
            grads = grads.reshape(width, flat_width).astype(jnp.bfloat16)
            for s, out_ref in enumerate(out_refs):
                out_ref[:, lanes] = grads[s * piece : (s + 1) * piece]

    return pl.pallas_call(
        kernel,
        out_shape=tuple(
            jax.ShapeDtypeStruct((piece, 2 * flat_width), jnp.bfloat16) for _ in range(pieces)
        ),
        compiler_params=ROOM,
        name="key_grads",
    )(prob, dlogit, q_blk, g_blk, dsum)


def shards(queries, keys, values, out_grad, row_keep, row_lengths):
    rows_dev, cols_dev, feature = queries.shape
    row_axis, zs = lax.axis_size("row"), lax.axis_size("col")
    ys = row_axis // (2 * XS)
    near_size = 2 * XS
    total_rows = rows_dev * row_axis
    total_cols = cols_dev * zs
    group_rows = total_rows // SUMMARIES
    flat_width = cols_dev * feature
    block_rows = near_size * rows_dev
    block_keys = ys * rows_dev
    tokens = block_keys // group_rows
    near = [[y * near_size + i for i in range(near_size)] for y in range(ys)]
    own_x = (lax.axis_index("row") // 2) % XS
    own_core = lax.axis_index("row") % 2
    own_z = lax.axis_index("col")
    place = jnp.stack([own_core, own_z]).astype(jnp.int32)
    logit_scale = 1.0 / math.sqrt(total_cols * feature)
    inv_root = 1.0 / math.sqrt(feature)

    def at(y, x, core):
        return ((y % ys) * XS + x % XS) * 2 + core

    cells = [(y, x, c) for y in range(ys) for x in range(XS) for c in range(2)]

    def shift_y(table, step):
        return lax.ppermute(table, "row", [(at(y, x, c), at(y + step, x, c)) for y, x, c in cells])

    def shift_x(table, step):
        return lax.ppermute(table, "row", [(at(y, x, c), at(y, x + step, c)) for y, x, c in cells])

    def swap_core(table):
        return lax.ppermute(table, "row", [(at(y, x, c), at(y, x, 1 - c)) for y, x, c in cells])

    def shift_z(table, step):
        return lax.ppermute(table, "col", [(z, (z + step) % zs) for z in range(zs)])

    def share(table, axis, groups=None):
        count = lax.axis_size(axis) if groups is None else len(groups[0])
        copies = jnp.broadcast_to(table[None], (count,) + table.shape)
        return lax.all_to_all(
            copies, axis, split_axis=0, concat_axis=0, tiled=True, axis_index_groups=groups
        )

    column_ids = own_z * cols_dev + jnp.arange(cols_dev, dtype=jnp.int32)
    cell_keep = (row_keep[:, None] == 1) & (column_ids[None, :] < row_lengths[:, None])
    keep_flat = jnp.broadcast_to(cell_keep[:, :, None], queries.shape).reshape(
        rows_dev, flat_width
    )
    zero = jnp.zeros((), queries.dtype)

    def masked(table):
        flat = jnp.where(keep_flat, table.reshape(rows_dev, flat_width), zero)
        return with_layout_constraint(flat, Layout((0, 1)))

    def in_line(table, moved):
        line = jnp.zeros((XS, rows_dev, flat_width), queries.dtype)
        for s, piece in ({0: table} | moved).items():
            line = lax.dynamic_update_slice(line, piece[None], ((own_x - s) % XS, 0, 0))
        return line

    def both_lines(line, other):
        first = jnp.where(own_core == 0, line, other)
        second = jnp.where(own_core == 0, other, line)
        return jnp.stack([first, second], axis=1).reshape(block_rows, flat_width)

    flag_rows = jnp.pad(
        row_keep.astype(jnp.bfloat16)[None, :], ((0, FLAG_ROWS - 1), (0, flat_width - rows_dev))
    )
    q_flat, k_flat = lax.optimization_barrier((masked(queries), masked(keys)))
    g_flat, v_flat = masked(out_grad), masked(values)
    v_flat = jnp.concatenate([v_flat, flag_rows], axis=0)
    q_moved = {s: shift_x(q_flat, s) for s in (2, 1, XS - 1)}
    k_moved = {s: shift_y(k_flat, s) for s in range(1, ys)}
    g_flat, v_flat, q_moved[1], k_moved[1] = lax.optimization_barrier(
        (g_flat, v_flat, q_moved[1], k_moved[1])
    )
    q_moved, k_moved = lax.optimization_barrier((q_moved, k_moved))
    k_blk = jnp.concatenate([k_flat] + [k_moved[s] for s in range(1, ys)], axis=0)
    q_line = in_line(q_flat, q_moved)
    q_other = swap_core(q_line)
    g_moved = {s: shift_x(g_flat, s) for s in (1, XS - 1)}
    v_moved = {s: shift_y(v_flat, s) for s in (1, ys - 1)}
    g_late, v_late, q_other, g_moved, v_moved = lax.optimization_barrier(
        (g_flat, v_flat, q_other, g_moved, v_moved)
    )
    q_blk = both_lines(q_line, q_other)
    logit_piece = dot_f32(q_blk, k_blk, ROW_PAIR)
    for s in range(2, XS - 1):
        g_moved[s] = shift_x(g_late, s)
    for s in range(2, ys - 1):
        v_moved[s] = shift_y(v_late, s)
    key_pieces = [v_flat] + [v_moved[s] for s in range(1, ys)]
    v_blk = jnp.concatenate([p[:rows_dev] for p in key_pieces], axis=0)
    g_line = in_line(g_flat, g_moved)
    g_blk = both_lines(g_line, swap_core(g_line))
    g_blk, _ = lax.optimization_barrier((g_blk, logit_piece))
    dprob_piece = dot_f32(g_blk, v_blk, ROW_PAIR).astype(jnp.bfloat16)
    key_flags = jnp.concatenate([p[rows_dev, :rows_dev] for p in key_pieces])[None, :]
    logit_sum = lax.psum_scatter(logit_piece, "col", scatter_dimension=0, tiled=True)

    dprob_chunks = dprob_piece.reshape(zs, block_rows // zs, block_keys)

    def part(step):
        return lax.dynamic_index_in_dim(dprob_chunks, (own_z + step) % zs, axis=0, keepdims=False)

    def passed(step, count):
        moving = part(step * count)
        for left in range(count - 1, -1, -1):
            moving = shift_z(moving, step)
            if left > 0:
                moving = (
                    moving.astype(jnp.float32) + part(step * left).astype(jnp.float32)
                ).astype(jnp.bfloat16)
        return moving

    dprob_forward = passed(1, zs // 2)
    dprob_back = passed(-1, zs - 1 - zs // 2)

    sums, own_stats = cross_statistics(q_blk, g_blk, k_blk, v_blk, tokens, feature, inv_root)
    cross_dl, dsum = cross_grads(
        q_blk, g_blk, sums, share(own_stats, "row", near), feature, inv_root
    )

    both, stats = block_softmax(
        logit_scale, logit_sum, part(0), dprob_forward, dprob_back, key_flags
    )
    both, stats, cross_dl, dsum = lax.optimization_barrier((both, stats, cross_dl, dsum))
    both = lax.all_gather(both, "col", axis=0, tiled=True)
    all_stats = share(stats, "row", near)
    weight = jnp.exp(all_stats[:, 0] - jnp.max(all_stats[:, 0], axis=0))
    total = jnp.sum(weight * all_stats[:, 1], axis=0)
    delta = jnp.sum(weight * all_stats[:, 2], axis=0) / total
    own_weight = jnp.exp(stats[0] - jnp.max(all_stats[:, 0], axis=0)) / total
    scaling = share(jnp.stack([own_weight, delta - stats[3]]), "col")

    prob, dlogit, dq_own, dq_other = query_grads(
        logit_scale, place, both, scaling, k_blk, cross_dl, sums, zs
    )
    dq_swapped = swap_core(dq_other)
    key_parts = key_grads(prob, dlogit, q_blk, g_blk, dsum, ys)
    key_moved = [shift_y(key_parts[s], -s) for s in range(1, ys)]
    line = (dq_own + dq_swapped.astype(jnp.float32)).astype(jnp.bfloat16)
    line = line.reshape(XS, rows_dev, flat_width)
    lines = [[at(y, x, c) for x in range(XS)] for y in range(ys) for c in range(2)]
    line = lax.all_to_all(
        line, "row", split_axis=0, concat_axis=0, tiled=True, axis_index_groups=lines
    )

    def added(parts):
        return sum(p.astype(jnp.float32) for p in parts)

    grad_q = added([line[x] for x in range(XS)])
    grad_kv = added([key_parts[0]] + key_moved)

    def finished(rows):
        return (
            jnp.where(keep_flat, rows, 0.0)
            .astype(jnp.bfloat16)
            .reshape(rows_dev, cols_dev, feature)
        )

    return (
        finished(grad_q),
        finished(grad_kv[:, :flat_width]),
        finished(grad_kv[:, flat_width:]),
    )


def solution(mesh):
    return jax.shard_map(
        shards,
        mesh=mesh,
        in_specs=(
            P("row", "col", None),
            P("row", "col", None),
            P("row", "col", None),
            P("row", "col", None),
            P("row"),
            P("row"),
        ),
        out_specs=(P("row", "col", None), P("row", "col", None), P("row", "col", None)),
        check_vma=False,
    )
```

```python
import math

import jax
import jax.numpy as jnp
from jax import lax
from jax.experimental import pallas as pl
from jax.experimental.layout import Layout, with_layout_constraint
from jax.experimental.pallas import tpu as pltpu
from jax.sharding import PartitionSpec as P

SUMMARIES = 256
XS = 4
FLAG_ROWS = 16

ROW_PAIR = (((1,), (1,)), ((), ()))
LEAD_PAIR = (((0,), (0,)), ((), ()))
PLAIN = (((1,), (0,)), ((), ()))

WHOLE = pl.BlockSpec()
SMEM = pl.BlockSpec(memory_space=pltpu.SMEM)
ROOM = pltpu.CompilerParams(vmem_limit_bytes=24 * 1024 * 1024)


def dot_f32(left, right, dims=PLAIN):
    return lax.dot_general(left, right, dims, preferred_element_type=jnp.float32)


def diagonal(n):
    return lax.broadcasted_iota(jnp.int32, (n, n), 0) == lax.broadcasted_iota(jnp.int32, (n, n), 1)


def across(column):
    return jnp.sum(jnp.where(diagonal(column.shape[0]), column, 0.0), axis=0, keepdims=True)


def upright(row):
    return jnp.sum(jnp.where(diagonal(row.shape[1]), row, 0.0), axis=1, keepdims=True)


def cross_scores(sums_ref, q_ref, g_ref, column, feature, inv_root):
    flat_width = q_ref.shape[1]
    lanes = slice(column * feature, (column + 1) * feature)
    other = slice(flat_width + column * feature, flat_width + (column + 1) * feature)
    scores = dot_f32(sums_ref[:, lanes], q_ref[:, lanes], ROW_PAIR) * inv_root
    dprob = dot_f32(sums_ref[:, other], g_ref[:, lanes], ROW_PAIR)
    return scores, dprob, lanes, other


def cross_statistics(q_blk, g_blk, k_blk, v_blk, row_stats, tokens, feature, inv_root):
    block_keys, flat_width = k_blk.shape
    both_width = 2 * flat_width
    block_rows = q_blk.shape[0]
    group = block_keys // tokens
    columns = both_width // (2 * feature)
    stat_rows = -(-(3 * columns + 1) // 8) * 8
    kinds, rows = 3, row_stats.shape[1]

    def kernel(q_ref, g_ref, k_ref, v_ref, row_ref, sums_ref, stat_ref):
        for half, table_ref in enumerate((k_ref, v_ref)):
            pooled = jnp.sum(
                table_ref[...].astype(jnp.float32).reshape(tokens, group, flat_width), axis=1
            )
            sums_ref[:, half * flat_width : (half + 1) * flat_width] = (pooled / group).astype(
                jnp.bfloat16
            )
        for c in range(columns):
            scores, dprob, _, _ = cross_scores(sums_ref, q_ref, g_ref, c, feature, inv_root)
            peak = jnp.max(scores, axis=0, keepdims=True)
            lifted = jnp.exp(scores - peak)
            stat_ref[c : c + 1, :] = peak
            stat_ref[columns + c : columns + c + 1, :] = jnp.sum(lifted, axis=0, keepdims=True)
            stat_ref[2 * columns + c : 2 * columns + c + 1, :] = jnp.sum(
                lifted * dprob, axis=0, keepdims=True
            )
        stat_ref[3 * columns :, :] = jnp.zeros((stat_rows - 3 * columns, block_rows), jnp.float32)
        for i in range(kinds):
            stat_ref[3 * columns : 3 * columns + 1, i * rows : (i + 1) * rows] = row_ref[
                i : i + 1, :
            ]

    return pl.pallas_call(
        kernel,
        out_shape=(
            jax.ShapeDtypeStruct((tokens, both_width), jnp.bfloat16),
            jax.ShapeDtypeStruct((stat_rows, block_rows), jnp.float32),
        ),
        compiler_params=ROOM,
        name="cross_statistics",
    )(q_blk, g_blk, k_blk, v_blk, row_stats)


def cross_grads(q_blk, g_blk, sums, all_stats, feature, inv_root):
    tokens, both_width = sums.shape
    block_rows = q_blk.shape[0]
    columns = both_width // (2 * feature)

    def kernel(q_ref, g_ref, sums_ref, stat_ref, dl_ref, dsum_ref):
        peaks = stat_ref[:, :columns, :]
        peak = jnp.max(peaks, axis=0)
        weight = jnp.exp(peaks - peak[None])
        total = jnp.sum(weight * stat_ref[:, columns : 2 * columns, :], axis=0)
        delta = jnp.sum(weight * stat_ref[:, 2 * columns : 3 * columns, :], axis=0) / total
        for c in range(columns):
            scores, dprob, lanes, other = cross_scores(sums_ref, q_ref, g_ref, c, feature, inv_root)
            probs = jnp.exp(scores - peak[c : c + 1, :]) / total[c : c + 1, :]
            dl = (inv_root * probs * (dprob - delta[c : c + 1, :])).astype(jnp.bfloat16)
            dl_ref[c * tokens : (c + 1) * tokens, :] = dl
            dsum_ref[:, lanes] = dot_f32(dl, q_ref[:, lanes])
            dsum_ref[:, other] = dot_f32(probs.astype(jnp.bfloat16), g_ref[:, lanes])

    return pl.pallas_call(
        kernel,
        out_shape=(
            jax.ShapeDtypeStruct((columns * tokens, block_rows), jnp.bfloat16),
            jax.ShapeDtypeStruct((tokens, both_width), jnp.float32),
        ),
        compiler_params=ROOM,
        name="cross_grads",
    )(q_blk, g_blk, sums, all_stats)


def block_softmax(logit_scale, logit_sum, own, forward, back, key_flags):
    rows, width = logit_sum.shape

    def kernel(logit_ref, own_ref, forward_ref, back_ref, flag_ref, both_ref, stat_ref):
        dprob = (
            own_ref[...].astype(jnp.float32)
            + forward_ref[...].astype(jnp.float32)
            + back_ref[...].astype(jnp.float32)
        )
        logits = jnp.where(flag_ref[...] > 0, logit_ref[...] * logit_scale, -1e30)
        peak = jnp.max(logits, axis=1, keepdims=True)
        lifted = jnp.exp(logits - peak)
        total = jnp.sum(lifted, axis=1, keepdims=True)
        weighted = jnp.sum(lifted * dprob, axis=1, keepdims=True)
        delta = weighted / total
        both_ref[:, :width] = lifted.astype(jnp.bfloat16)
        both_ref[:, width:] = (lifted * (dprob - delta)).astype(jnp.bfloat16)
        for i, column in enumerate((peak, total, weighted, delta)):
            stat_ref[i : i + 1, :] = across(column)
        stat_ref[4:8, :] = jnp.zeros((4, rows), jnp.float32)

    return pl.pallas_call(
        kernel,
        out_shape=(
            jax.ShapeDtypeStruct((rows, 2 * width), jnp.bfloat16),
            jax.ShapeDtypeStruct((8, rows), jnp.float32),
        ),
        compiler_params=ROOM,
        name="block_softmax",
    )(logit_sum, own, forward, back, key_flags)


def query_grads(logit_scale, place, both, scaling, k_blk, cross_dl, sums, chunks):
    block_rows, width = both.shape[0], both.shape[1] // 2
    rows = block_rows // chunks
    flat_width = k_blk.shape[1]
    tokens = sums.shape[0]
    columns = cross_dl.shape[0] // tokens
    feature = flat_width // columns

    def kernel(place_ref, both_ref, scale_ref, k_ref, dl_ref, sums_ref, p_ref, ds_ref, own_ref, other_ref, dq_ref, held_ref, sems):
        core = place_ref[0]
        copies = []
        for i in range(chunks):
            at = pl.ds(i * rows, rows)
            copies.append(pltpu.make_async_copy(both_ref.at[at], held_ref.at[at], sems.at[i]))
            copies[i].start()
        for i in range(chunks):
            at = slice(i * rows, (i + 1) * rows)
            copies[i].wait()
            weight, offset = upright(scale_ref[i, 0:1, :]), upright(scale_ref[i, 1:2, :])
            lifted = held_ref[at, :width].astype(jnp.float32)
            tilted = held_ref[at, width:].astype(jnp.float32)
            p_ref[at, :] = (lifted * weight).astype(jnp.bfloat16)
            ds_ref[at, :] = ((tilted - lifted * offset) * (weight * logit_scale)).astype(
                jnp.bfloat16
            )
        dq_ref[...] = dot_f32(ds_ref[...], k_ref[...])
        for c in range(columns):
            lanes = slice(c * feature, (c + 1) * feature)
            dq_ref[:, lanes] += dot_f32(
                dl_ref[c * tokens : (c + 1) * tokens, :], sums_ref[:, lanes], LEAD_PAIR
            )
        for x in range(chunks // 2):
            to = slice(x * rows, (x + 1) * rows)
            mine = pl.multiple_of((2 * x + core) * rows, rows)
            theirs = pl.multiple_of((2 * x + 1 - core) * rows, rows)
            own_ref[to, :] = dq_ref[pl.ds(mine, rows), :]
            other_ref[to, :] = dq_ref[pl.ds(theirs, rows), :].astype(jnp.bfloat16)

    return pl.pallas_call(
        kernel,
        in_specs=[SMEM, pl.BlockSpec(memory_space=pltpu.HBM)] + [WHOLE] * 4,
        out_shape=(
            jax.ShapeDtypeStruct((block_rows, width), jnp.bfloat16),
            jax.ShapeDtypeStruct((block_rows, width), jnp.bfloat16),
            jax.ShapeDtypeStruct((block_rows // 2, flat_width), jnp.float32),
            jax.ShapeDtypeStruct((block_rows // 2, flat_width), jnp.bfloat16),
        ),
        scratch_shapes=[
            pltpu.VMEM((block_rows, flat_width), jnp.float32),
            pltpu.VMEM((block_rows, 2 * width), jnp.bfloat16),
            pltpu.SemaphoreType.DMA((chunks,)),
        ],
        compiler_params=ROOM,
        name="query_grads",
    )(place, both, scaling, k_blk, cross_dl, sums)


def key_grads(prob, dlogit, q_blk, g_blk, dsum, pieces):
    width, flat_width = prob.shape[1], q_blk.shape[1]
    tokens = dsum.shape[0]
    group = width // tokens
    piece = width // pieces

    def kernel(p_ref, ds_ref, q_ref, g_ref, dsum_ref, *out_refs):
        for half, (w_ref, t_ref) in enumerate(((ds_ref, q_ref), (p_ref, g_ref))):
            lanes = slice(half * flat_width, (half + 1) * flat_width)
            grads = dot_f32(w_ref[...], t_ref[...], LEAD_PAIR)
            shared = dsum_ref[:, lanes] / group
            grads = grads.reshape(tokens, group, flat_width) + shared[:, None, :]
            grads = grads.reshape(width, flat_width).astype(jnp.bfloat16)
            for s, out_ref in enumerate(out_refs):
                out_ref[:, lanes] = grads[s * piece : (s + 1) * piece]

    return pl.pallas_call(
        kernel,
        out_shape=tuple(
            jax.ShapeDtypeStruct((piece, 2 * flat_width), jnp.bfloat16) for _ in range(pieces)
        ),
        compiler_params=ROOM,
        name="key_grads",
    )(prob, dlogit, q_blk, g_blk, dsum)


def shards(queries, keys, values, out_grad, row_keep, row_lengths):
    rows_dev, cols_dev, feature = queries.shape
    row_axis, zs = lax.axis_size("row"), lax.axis_size("col")
    ys = row_axis // (2 * XS)
    near_size = 2 * XS
    total_rows = rows_dev * row_axis
    total_cols = cols_dev * zs
    group_rows = total_rows // SUMMARIES
    flat_width = cols_dev * feature
    block_rows = near_size * rows_dev
    block_keys = ys * rows_dev
    tokens = block_keys // group_rows
    near = [[y * near_size + i for i in range(near_size)] for y in range(ys)]
    own_x = (lax.axis_index("row") // 2) % XS
    own_core = lax.axis_index("row") % 2
    own_z = lax.axis_index("col")
    place = jnp.stack([own_core, own_z]).astype(jnp.int32)
    logit_scale = 1.0 / math.sqrt(total_cols * feature)
    inv_root = 1.0 / math.sqrt(feature)

    def at(y, x, core):
        return ((y % ys) * XS + x % XS) * 2 + core

    cells = [(y, x, c) for y in range(ys) for x in range(XS) for c in range(2)]

    def shift_y(table, step):
        return lax.ppermute(table, "row", [(at(y, x, c), at(y + step, x, c)) for y, x, c in cells])

    def shift_x(table, step):
        return lax.ppermute(table, "row", [(at(y, x, c), at(y, x + step, c)) for y, x, c in cells])

    def swap_core(table):
        return lax.ppermute(table, "row", [(at(y, x, c), at(y, x, 1 - c)) for y, x, c in cells])

    def shift_z(table, step):
        return lax.ppermute(table, "col", [(z, (z + step) % zs) for z in range(zs)])

    def share(table, axis, groups=None):
        count = lax.axis_size(axis) if groups is None else len(groups[0])
        copies = jnp.broadcast_to(table[None], (count,) + table.shape)
        return lax.all_to_all(
            copies, axis, split_axis=0, concat_axis=0, tiled=True, axis_index_groups=groups
        )

    column_ids = own_z * cols_dev + jnp.arange(cols_dev, dtype=jnp.int32)
    cell_keep = (row_keep[:, None] == 1) & (column_ids[None, :] < row_lengths[:, None])
    keep_flat = jnp.broadcast_to(cell_keep[:, :, None], queries.shape).reshape(
        rows_dev, flat_width
    )
    zero = jnp.zeros((), queries.dtype)

    def masked(first, second):
        tables = (t.reshape(rows_dev, flat_width) for t in (first, second))
        flat = jnp.concatenate([jnp.where(keep_flat, t, zero) for t in tables], axis=1)
        return with_layout_constraint(flat, Layout((0, 1)))

    qg_flat = masked(queries, out_grad)
    flag_rows = jnp.pad(
        row_keep.astype(jnp.bfloat16)[None, :],
        ((0, FLAG_ROWS - 1), (0, 2 * flat_width - rows_dev)),
    )
    kv_flat = jnp.concatenate([masked(keys, values), flag_rows], axis=0)
    qg_flat, kv_flat = lax.optimization_barrier((qg_flat, kv_flat))
    order = (1, XS - 1, 2)
    query_pieces = {0: qg_flat} | {s: shift_x(qg_flat, s) for s in order}
    key_pieces = [kv_flat] + [shift_y(kv_flat, s) for s in range(1, ys)]
    query_pieces, key_pieces = lax.optimization_barrier((query_pieces, key_pieces))
    halves = (slice(0, flat_width), slice(flat_width, 2 * flat_width))

    def query_block(half):
        line = jnp.zeros((XS, rows_dev, flat_width), queries.dtype)
        for s, piece in query_pieces.items():
            line = lax.dynamic_update_slice(line, piece[None, :, half], ((own_x - s) % XS, 0, 0))
        other = swap_core(line)
        first = jnp.where(own_core == 0, line, other)
        second = jnp.where(own_core == 0, other, line)
        return jnp.stack([first, second], axis=1).reshape(block_rows, flat_width)

    def key_block(half):
        return jnp.concatenate([p[:rows_dev, half] for p in key_pieces], axis=0)

    q_blk, g_blk = query_block(halves[0]), query_block(halves[1])
    k_blk, v_blk = key_block(halves[0]), key_block(halves[1])
    logit_piece = dot_f32(q_blk, k_blk, ROW_PAIR)
    g_blk, _ = lax.optimization_barrier((g_blk, logit_piece))
    dprob_piece = dot_f32(g_blk, v_blk, ROW_PAIR).astype(jnp.bfloat16)
    key_flags = jnp.concatenate([p[rows_dev, :rows_dev] for p in key_pieces])[None, :]
    logit_sum = lax.psum_scatter(logit_piece, "col", scatter_dimension=0, tiled=True)

    dprob_chunks = dprob_piece.reshape(zs, block_rows // zs, block_keys)

    def part(step):
        return lax.dynamic_index_in_dim(dprob_chunks, (own_z + step) % zs, axis=0, keepdims=False)

    def passed(step, count):
        moving = part(step * count)
        for left in range(count - 1, -1, -1):
            moving = shift_z(moving, step)
            if left > 0:
                moving = (
                    moving.astype(jnp.float32) + part(step * left).astype(jnp.float32)
                ).astype(jnp.bfloat16)
        return moving

    dprob_forward = passed(1, zs // 2)
    dprob_back = passed(-1, zs - 1 - zs // 2)

    both, stats = block_softmax(
        logit_scale, logit_sum, part(0), dprob_forward, dprob_back, key_flags
    )
    both = lax.all_gather(both, "col", axis=0, tiled=True)

    sums, own_stats = cross_statistics(
        q_blk, g_blk, k_blk, v_blk, stats, tokens, feature, inv_root
    )
    all_stats = share(own_stats, "row", near)
    row_stats = all_stats[:, 3 * cols_dev, : 3 * rows_dev].reshape(near_size, 3, rows_dev)
    peak = jnp.max(row_stats[:, 0], axis=0)
    weight = jnp.exp(row_stats[:, 0] - peak)
    total = jnp.sum(weight * row_stats[:, 1], axis=0)
    delta = jnp.sum(weight * row_stats[:, 2], axis=0) / total
    scaling = share(jnp.stack([jnp.exp(stats[0] - peak) / total, delta - stats[3]]), "col")
    cross_dl, dsum = cross_grads(q_blk, g_blk, sums, all_stats, feature, inv_root)
    both, scaling, cross_dl, dsum = lax.optimization_barrier((both, scaling, cross_dl, dsum))

    prob, dlogit, dq_own, dq_other = query_grads(
        logit_scale, place, both, scaling, k_blk, cross_dl, sums, zs
    )
    dq_swapped = swap_core(dq_other)
    key_parts = key_grads(prob, dlogit, q_blk, g_blk, dsum, ys)
    key_moved = [shift_y(key_parts[s], -s) for s in range(1, ys)]
    line = (dq_own + dq_swapped.astype(jnp.float32)).astype(jnp.bfloat16)
    line = line.reshape(XS, rows_dev, flat_width)
    lines = [[at(y, x, c) for x in range(XS)] for y in range(ys) for c in range(2)]
    line = lax.all_to_all(
        line, "row", split_axis=0, concat_axis=0, tiled=True, axis_index_groups=lines
    )

    def added(parts):
        return sum(p.astype(jnp.float32) for p in parts)

    grad_q = added([line[x] for x in range(XS)])
    grad_kv = added([key_parts[0]] + key_moved)

    def finished(rows):
        return (
            jnp.where(keep_flat, rows, 0.0)
            .astype(jnp.bfloat16)
            .reshape(rows_dev, cols_dev, feature)
        )

    return (
        finished(grad_q),
        finished(grad_kv[:, :flat_width]),
        finished(grad_kv[:, flat_width:]),
    )


def solution(mesh):
    return jax.shard_map(
        shards,
        mesh=mesh,
        in_specs=(
            P("row", "col", None),
            P("row", "col", None),
            P("row", "col", None),
            P("row", "col", None),
            P("row"),
            P("row"),
        ),
        out_specs=(P("row", "col", None), P("row", "col", None), P("row", "col", None)),
        check_vma=False,
    )
```

```python
import math

import jax
import jax.numpy as jnp
from jax import lax
from jax.experimental import pallas as pl
from jax.experimental.layout import Layout, with_layout_constraint
from jax.experimental.pallas import tpu as pltpu
from jax.sharding import PartitionSpec as P

SUMMARIES = 256
XS = 4
FLAG_ROWS = 16

ROW_PAIR = (((1,), (1,)), ((), ()))
LEAD_PAIR = (((0,), (0,)), ((), ()))
PLAIN = (((1,), (0,)), ((), ()))

WHOLE = pl.BlockSpec()
SMEM = pl.BlockSpec(memory_space=pltpu.SMEM)
ROOM = pltpu.CompilerParams(vmem_limit_bytes=24 * 1024 * 1024)


def dot_f32(left, right, dims=PLAIN):
    return lax.dot_general(left, right, dims, preferred_element_type=jnp.float32)


def diagonal(n):
    return lax.broadcasted_iota(jnp.int32, (n, n), 0) == lax.broadcasted_iota(jnp.int32, (n, n), 1)


def across(column):
    return jnp.sum(jnp.where(diagonal(column.shape[0]), column, 0.0), axis=0, keepdims=True)


def upright(row):
    return jnp.sum(jnp.where(diagonal(row.shape[1]), row, 0.0), axis=1, keepdims=True)


def cross_scores(sums_ref, q_ref, g_ref, column, feature, inv_root):
    flat_width = q_ref.shape[1]
    lanes = slice(column * feature, (column + 1) * feature)
    other = slice(flat_width + column * feature, flat_width + (column + 1) * feature)
    scores = dot_f32(sums_ref[:, lanes], q_ref[:, lanes], ROW_PAIR) * inv_root
    dprob = dot_f32(sums_ref[:, other], g_ref[:, lanes], ROW_PAIR)
    return scores, dprob, lanes, other


def cross_statistics(q_blk, g_blk, k_blk, v_blk, row_stats, tokens, feature, inv_root):
    block_keys, flat_width = k_blk.shape
    both_width = 2 * flat_width
    block_rows = q_blk.shape[0]
    group = block_keys // tokens
    columns = both_width // (2 * feature)
    stat_rows = -(-(3 * columns + 1) // 8) * 8
    kinds, rows = 3, row_stats.shape[1]

    def kernel(q_ref, g_ref, k_ref, v_ref, row_ref, sums_ref, stat_ref):
        for half, table_ref in enumerate((k_ref, v_ref)):
            pooled = jnp.sum(
                table_ref[...].astype(jnp.float32).reshape(tokens, group, flat_width), axis=1
            )
            sums_ref[:, half * flat_width : (half + 1) * flat_width] = (pooled / group).astype(
                jnp.bfloat16
            )
        for c in range(columns):
            scores, dprob, _, _ = cross_scores(sums_ref, q_ref, g_ref, c, feature, inv_root)
            peak = jnp.max(scores, axis=0, keepdims=True)
            lifted = jnp.exp(scores - peak)
            stat_ref[c : c + 1, :] = peak
            stat_ref[columns + c : columns + c + 1, :] = jnp.sum(lifted, axis=0, keepdims=True)
            stat_ref[2 * columns + c : 2 * columns + c + 1, :] = jnp.sum(
                lifted * dprob, axis=0, keepdims=True
            )
        stat_ref[3 * columns :, :] = jnp.zeros((stat_rows - 3 * columns, block_rows), jnp.float32)
        for i in range(kinds):
            stat_ref[3 * columns : 3 * columns + 1, i * rows : (i + 1) * rows] = row_ref[
                i : i + 1, :
            ]

    return pl.pallas_call(
        kernel,
        out_shape=(
            jax.ShapeDtypeStruct((tokens, both_width), jnp.bfloat16),
            jax.ShapeDtypeStruct((stat_rows, block_rows), jnp.float32),
        ),
        compiler_params=ROOM,
        name="cross_statistics",
    )(q_blk, g_blk, k_blk, v_blk, row_stats)


def cross_grads(q_blk, g_blk, sums, all_stats, feature, inv_root):
    tokens, both_width = sums.shape
    block_rows = q_blk.shape[0]
    columns = both_width // (2 * feature)

    def kernel(q_ref, g_ref, sums_ref, stat_ref, dl_ref, dsum_ref):
        peaks = stat_ref[:, :columns, :]
        peak = jnp.max(peaks, axis=0)
        weight = jnp.exp(peaks - peak[None])
        total = jnp.sum(weight * stat_ref[:, columns : 2 * columns, :], axis=0)
        delta = jnp.sum(weight * stat_ref[:, 2 * columns : 3 * columns, :], axis=0) / total
        for c in range(columns):
            scores, dprob, lanes, other = cross_scores(sums_ref, q_ref, g_ref, c, feature, inv_root)
            probs = jnp.exp(scores - peak[c : c + 1, :]) / total[c : c + 1, :]
            dl = (inv_root * probs * (dprob - delta[c : c + 1, :])).astype(jnp.bfloat16)
            dl_ref[c * tokens : (c + 1) * tokens, :] = dl
            dsum_ref[:, lanes] = dot_f32(dl, q_ref[:, lanes])
            dsum_ref[:, other] = dot_f32(probs.astype(jnp.bfloat16), g_ref[:, lanes])

    return pl.pallas_call(
        kernel,
        out_shape=(
            jax.ShapeDtypeStruct((columns * tokens, block_rows), jnp.bfloat16),
            jax.ShapeDtypeStruct((tokens, both_width), jnp.float32),
        ),
        compiler_params=ROOM,
        name="cross_grads",
    )(q_blk, g_blk, sums, all_stats)


def block_softmax(logit_scale, logit_sum, own, forward, back, key_flags):
    rows, width = logit_sum.shape

    def kernel(logit_ref, own_ref, forward_ref, back_ref, flag_ref, both_ref, stat_ref):
        dprob = (
            own_ref[...].astype(jnp.float32)
            + forward_ref[...].astype(jnp.float32)
            + back_ref[...].astype(jnp.float32)
        )
        logits = jnp.where(flag_ref[...] > 0, logit_ref[...] * logit_scale, -1e30)
        peak = jnp.max(logits, axis=1, keepdims=True)
        lifted = jnp.exp(logits - peak)
        total = jnp.sum(lifted, axis=1, keepdims=True)
        weighted = jnp.sum(lifted * dprob, axis=1, keepdims=True)
        delta = weighted / total
        both_ref[:, :width] = lifted.astype(jnp.bfloat16)
        both_ref[:, width:] = (lifted * (dprob - delta)).astype(jnp.bfloat16)
        for i, column in enumerate((peak, total, weighted, delta)):
            stat_ref[i : i + 1, :] = across(column)
        stat_ref[4:8, :] = jnp.zeros((4, rows), jnp.float32)

    return pl.pallas_call(
        kernel,
        out_shape=(
            jax.ShapeDtypeStruct((rows, 2 * width), jnp.bfloat16),
            jax.ShapeDtypeStruct((8, rows), jnp.float32),
        ),
        compiler_params=ROOM,
        name="block_softmax",
    )(logit_sum, own, forward, back, key_flags)


def query_grads(logit_scale, place, both, scaling, k_blk, cross_dl, sums, chunks):
    block_rows, width = both.shape[0], both.shape[1] // 2
    rows = block_rows // chunks
    flat_width = k_blk.shape[1]
    tokens = sums.shape[0]
    columns = cross_dl.shape[0] // tokens
    feature = flat_width // columns

    def kernel(place_ref, both_ref, scale_ref, k_ref, dl_ref, sums_ref, p_ref, ds_ref, own_ref, other_ref, dq_ref, held_ref, sems):
        core = place_ref[0]
        copies = []
        for i in range(chunks):
            at = pl.ds(i * rows, rows)
            copies.append(pltpu.make_async_copy(both_ref.at[at], held_ref.at[at], sems.at[i]))
            copies[i].start()
        for i in range(chunks):
            at = slice(i * rows, (i + 1) * rows)
            copies[i].wait()
            weight, offset = upright(scale_ref[i, 0:1, :]), upright(scale_ref[i, 1:2, :])
            lifted = held_ref[at, :width].astype(jnp.float32)
            tilted = held_ref[at, width:].astype(jnp.float32)
            p_ref[at, :] = (lifted * weight).astype(jnp.bfloat16)
            ds_ref[at, :] = ((tilted - lifted * offset) * (weight * logit_scale)).astype(
                jnp.bfloat16
            )
        dq_ref[...] = dot_f32(ds_ref[...], k_ref[...])
        for c in range(columns):
            lanes = slice(c * feature, (c + 1) * feature)
            dq_ref[:, lanes] += dot_f32(
                dl_ref[c * tokens : (c + 1) * tokens, :], sums_ref[:, lanes], LEAD_PAIR
            )
        for x in range(chunks // 2):
            to = slice(x * rows, (x + 1) * rows)
            mine = pl.multiple_of((2 * x + core) * rows, rows)
            theirs = pl.multiple_of((2 * x + 1 - core) * rows, rows)
            own_ref[to, :] = dq_ref[pl.ds(mine, rows), :]
            other_ref[to, :] = dq_ref[pl.ds(theirs, rows), :].astype(jnp.bfloat16)

    return pl.pallas_call(
        kernel,
        in_specs=[SMEM, pl.BlockSpec(memory_space=pltpu.HBM)] + [WHOLE] * 4,
        out_shape=(
            jax.ShapeDtypeStruct((block_rows, width), jnp.bfloat16),
            jax.ShapeDtypeStruct((block_rows, width), jnp.bfloat16),
            jax.ShapeDtypeStruct((block_rows // 2, flat_width), jnp.float32),
            jax.ShapeDtypeStruct((block_rows // 2, flat_width), jnp.bfloat16),
        ),
        scratch_shapes=[
            pltpu.VMEM((block_rows, flat_width), jnp.float32),
            pltpu.VMEM((block_rows, 2 * width), jnp.bfloat16),
            pltpu.SemaphoreType.DMA((chunks,)),
        ],
        compiler_params=ROOM,
        name="query_grads",
    )(place, pltpu.with_memory_space_constraint(both, pltpu.HBM), scaling, k_blk, cross_dl, sums)


def key_grads(prob, dlogit, q_blk, g_blk, dsum, pieces):
    width, flat_width = prob.shape[1], q_blk.shape[1]
    tokens = dsum.shape[0]
    group = width // tokens
    piece = width // pieces

    def kernel(p_ref, ds_ref, q_ref, g_ref, dsum_ref, *out_refs):
        for half, (w_ref, t_ref) in enumerate(((ds_ref, q_ref), (p_ref, g_ref))):
            lanes = slice(half * flat_width, (half + 1) * flat_width)
            grads = dot_f32(w_ref[...], t_ref[...], LEAD_PAIR)
            shared = dsum_ref[:, lanes] / group
            grads = grads.reshape(tokens, group, flat_width) + shared[:, None, :]
            grads = grads.reshape(width, flat_width).astype(jnp.bfloat16)
            for s, out_ref in enumerate(out_refs):
                out_ref[:, lanes] = grads[s * piece : (s + 1) * piece]

    return pl.pallas_call(
        kernel,
        out_shape=tuple(
            jax.ShapeDtypeStruct((piece, 2 * flat_width), jnp.bfloat16) for _ in range(pieces)
        ),
        compiler_params=ROOM,
        name="key_grads",
    )(prob, dlogit, q_blk, g_blk, dsum)


def shards(queries, keys, values, out_grad, row_keep, row_lengths):
    rows_dev, cols_dev, feature = queries.shape
    row_axis, zs = lax.axis_size("row"), lax.axis_size("col")
    ys = row_axis // (2 * XS)
    near_size = 2 * XS
    total_rows = rows_dev * row_axis
    total_cols = cols_dev * zs
    group_rows = total_rows // SUMMARIES
    flat_width = cols_dev * feature
    block_rows = near_size * rows_dev
    block_keys = ys * rows_dev
    tokens = block_keys // group_rows
    near = [[y * near_size + i for i in range(near_size)] for y in range(ys)]
    own_x = (lax.axis_index("row") // 2) % XS
    own_core = lax.axis_index("row") % 2
    own_z = lax.axis_index("col")
    place = jnp.stack([own_core, own_z]).astype(jnp.int32)
    logit_scale = 1.0 / math.sqrt(total_cols * feature)
    inv_root = 1.0 / math.sqrt(feature)

    def at(y, x, core):
        return ((y % ys) * XS + x % XS) * 2 + core

    cells = [(y, x, c) for y in range(ys) for x in range(XS) for c in range(2)]

    def shift_y(table, step):
        return lax.ppermute(table, "row", [(at(y, x, c), at(y + step, x, c)) for y, x, c in cells])

    def shift_x(table, step):
        return lax.ppermute(table, "row", [(at(y, x, c), at(y, x + step, c)) for y, x, c in cells])

    def swap_core(table):
        return lax.ppermute(table, "row", [(at(y, x, c), at(y, x, 1 - c)) for y, x, c in cells])

    def shift_z(table, step):
        return lax.ppermute(table, "col", [(z, (z + step) % zs) for z in range(zs)])

    def share(table, axis, groups=None):
        count = lax.axis_size(axis) if groups is None else len(groups[0])
        copies = jnp.broadcast_to(table[None], (count,) + table.shape)
        return lax.all_to_all(
            copies, axis, split_axis=0, concat_axis=0, tiled=True, axis_index_groups=groups
        )

    column_ids = own_z * cols_dev + jnp.arange(cols_dev, dtype=jnp.int32)
    cell_keep = (row_keep[:, None] == 1) & (column_ids[None, :] < row_lengths[:, None])
    keep_flat = jnp.broadcast_to(cell_keep[:, :, None], queries.shape).reshape(
        rows_dev, flat_width
    )
    zero = jnp.zeros((), queries.dtype)

    def masked(table):
        flat = jnp.where(keep_flat, table.reshape(rows_dev, flat_width), zero)
        return with_layout_constraint(flat, Layout((0, 1)))

    def key_pieces_of(table):
        return [table] + [shift_y(table, s) for s in range(1, ys)]

    def query_pieces_of(table):
        return [table] + [shift_x(table, s) for s in range(1, XS)]

    def query_block(pieces):
        line = jnp.zeros((XS, rows_dev, flat_width), queries.dtype)
        for s, piece in enumerate(pieces):
            line = lax.dynamic_update_slice(line, piece[None], ((own_x - s) % XS, 0, 0))
        other = swap_core(line)
        first = jnp.where(own_core == 0, line, other)
        second = jnp.where(own_core == 0, other, line)
        return jnp.stack([first, second], axis=1).reshape(block_rows, flat_width)

    q_flat, k_flat = lax.optimization_barrier((masked(queries), masked(keys)))
    k_pieces = key_pieces_of(k_flat)
    q_blk = query_block(query_pieces_of(q_flat))
    keep_flat, k_pieces = lax.optimization_barrier((keep_flat, k_pieces))
    k_blk = jnp.concatenate(k_pieces, axis=0)
    logit_piece = dot_f32(q_blk, k_blk, ROW_PAIR)
    flag_rows = jnp.pad(
        row_keep.astype(jnp.bfloat16)[None, :], ((0, FLAG_ROWS - 1), (0, flat_width - rows_dev))
    )
    g_pieces, key_pieces = lax.optimization_barrier(
        (
            query_pieces_of(masked(out_grad)),
            key_pieces_of(jnp.concatenate([masked(values), flag_rows], axis=0)),
        )
    )
    v_blk = jnp.concatenate([p[:rows_dev] for p in key_pieces], axis=0)
    g_blk, _ = lax.optimization_barrier((query_block(g_pieces), logit_piece))
    dprob_piece = dot_f32(g_blk, v_blk, ROW_PAIR).astype(jnp.bfloat16)
    key_flags = jnp.concatenate([p[rows_dev, :rows_dev] for p in key_pieces])[None, :]
    logit_sum = lax.psum_scatter(logit_piece, "col", scatter_dimension=0, tiled=True)

    dprob_chunks = dprob_piece.reshape(zs, block_rows // zs, block_keys)

    def part(step):
        return lax.dynamic_index_in_dim(dprob_chunks, (own_z + step) % zs, axis=0, keepdims=False)

    def passed(step, count):
        moving = part(step * count)
        for left in range(count - 1, -1, -1):
            moving = shift_z(moving, step)
            if left > 0:
                moving = (
                    moving.astype(jnp.float32) + part(step * left).astype(jnp.float32)
                ).astype(jnp.bfloat16)
        return moving

    dprob_forward = passed(1, zs // 2)
    dprob_back = passed(-1, zs - 1 - zs // 2)

    both, stats = block_softmax(
        logit_scale, logit_sum, part(0), dprob_forward, dprob_back, key_flags
    )
    both = lax.all_gather(both, "col", axis=0, tiled=True)

    sums, own_stats = cross_statistics(
        q_blk, g_blk, k_blk, v_blk, stats, tokens, feature, inv_root
    )
    all_stats = share(own_stats, "row", near)
    row_stats = all_stats[:, 3 * cols_dev, : 3 * rows_dev].reshape(near_size, 3, rows_dev)
    peak = jnp.max(row_stats[:, 0], axis=0)
    weight = jnp.exp(row_stats[:, 0] - peak)
    total = jnp.sum(weight * row_stats[:, 1], axis=0)
    delta = jnp.sum(weight * row_stats[:, 2], axis=0) / total
    scaling = share(jnp.stack([jnp.exp(stats[0] - peak) / total, delta - stats[3]]), "col")
    cross_dl, dsum = cross_grads(q_blk, g_blk, sums, all_stats, feature, inv_root)
    both, scaling, cross_dl, dsum = lax.optimization_barrier((both, scaling, cross_dl, dsum))

    prob, dlogit, dq_own, dq_other = query_grads(
        logit_scale, place, both, scaling, k_blk, cross_dl, sums, zs
    )
    dq_swapped = swap_core(dq_other)
    key_parts = key_grads(prob, dlogit, q_blk, g_blk, dsum, ys)
    key_moved = [shift_y(key_parts[s], -s) for s in range(1, ys)]
    line = (dq_own + dq_swapped.astype(jnp.float32)).astype(jnp.bfloat16)
    line = line.reshape(XS, rows_dev, flat_width)
    lines = [[at(y, x, c) for x in range(XS)] for y in range(ys) for c in range(2)]
    line = lax.all_to_all(
        line, "row", split_axis=0, concat_axis=0, tiled=True, axis_index_groups=lines
    )

    def added(parts):
        return sum(p.astype(jnp.float32) for p in parts)

    grad_q = added([line[x] for x in range(XS)])
    grad_kv = added([key_parts[0]] + key_moved)

    def finished(rows):
        return (
            jnp.where(keep_flat, rows, 0.0)
            .astype(jnp.bfloat16)
            .reshape(rows_dev, cols_dev, feature)
        )

    return (
        finished(grad_q),
        finished(grad_kv[:, :flat_width]),
        finished(grad_kv[:, flat_width:]),
    )


def solution(mesh):
    return jax.shard_map(
        shards,
        mesh=mesh,
        in_specs=(
            P("row", "col", None),
            P("row", "col", None),
            P("row", "col", None),
            P("row", "col", None),
            P("row"),
            P("row"),
        ),
        out_specs=(P("row", "col", None), P("row", "col", None), P("row", "col", None)),
        check_vma=False,
    )
```

```python
import math

import jax
import jax.numpy as jnp
from jax import lax
from jax.experimental import pallas as pl
from jax.experimental.layout import Layout, with_layout_constraint
from jax.experimental.pallas import tpu as pltpu
from jax.sharding import PartitionSpec as P

SUMMARIES = 256
XS = 4
FLAG_ROWS = 16

ROW_PAIR = (((1,), (1,)), ((), ()))
LEAD_PAIR = (((0,), (0,)), ((), ()))
PLAIN = (((1,), (0,)), ((), ()))

WHOLE = pl.BlockSpec()
SMEM = pl.BlockSpec(memory_space=pltpu.SMEM)
ROOM = pltpu.CompilerParams(vmem_limit_bytes=24 * 1024 * 1024)


def dot_f32(left, right, dims=PLAIN):
    return lax.dot_general(left, right, dims, preferred_element_type=jnp.float32)


def diagonal(n):
    return lax.broadcasted_iota(jnp.int32, (n, n), 0) == lax.broadcasted_iota(jnp.int32, (n, n), 1)


def across(column):
    return jnp.sum(jnp.where(diagonal(column.shape[0]), column, 0.0), axis=0, keepdims=True)


def upright(row):
    return jnp.sum(jnp.where(diagonal(row.shape[1]), row, 0.0), axis=1, keepdims=True)


def cross_scores(sums_ref, q_ref, g_ref, column, feature, inv_root):
    flat_width = q_ref.shape[1]
    lanes = slice(column * feature, (column + 1) * feature)
    other = slice(flat_width + column * feature, flat_width + (column + 1) * feature)
    scores = dot_f32(sums_ref[:, lanes], q_ref[:, lanes], ROW_PAIR) * inv_root
    dprob = dot_f32(sums_ref[:, other], g_ref[:, lanes], ROW_PAIR)
    return scores, dprob, lanes, other


def cross_statistics(q_blk, g_blk, k_blk, v_blk, row_stats, tokens, feature, inv_root):
    block_keys, flat_width = k_blk.shape
    both_width = 2 * flat_width
    block_rows = q_blk.shape[0]
    group = block_keys // tokens
    columns = both_width // (2 * feature)
    stat_rows = -(-(3 * columns + 1) // 8) * 8
    kinds, rows = 3, row_stats.shape[1]

    def kernel(q_ref, g_ref, k_ref, v_ref, row_ref, sums_ref, stat_ref):
        for half, table_ref in enumerate((k_ref, v_ref)):
            pooled = jnp.sum(
                table_ref[...].astype(jnp.float32).reshape(tokens, group, flat_width), axis=1
            )
            sums_ref[:, half * flat_width : (half + 1) * flat_width] = (pooled / group).astype(
                jnp.bfloat16
            )
        for c in range(columns):
            scores, dprob, _, _ = cross_scores(sums_ref, q_ref, g_ref, c, feature, inv_root)
            peak = jnp.max(scores, axis=0, keepdims=True)
            lifted = jnp.exp(scores - peak)
            stat_ref[c : c + 1, :] = peak
            stat_ref[columns + c : columns + c + 1, :] = jnp.sum(lifted, axis=0, keepdims=True)
            stat_ref[2 * columns + c : 2 * columns + c + 1, :] = jnp.sum(
                lifted * dprob, axis=0, keepdims=True
            )
        stat_ref[3 * columns :, :] = jnp.zeros((stat_rows - 3 * columns, block_rows), jnp.float32)
        for i in range(kinds):
            stat_ref[3 * columns : 3 * columns + 1, i * rows : (i + 1) * rows] = row_ref[
                i : i + 1, :
            ]

    return pl.pallas_call(
        kernel,
        out_shape=(
            jax.ShapeDtypeStruct((tokens, both_width), jnp.bfloat16),
            jax.ShapeDtypeStruct((stat_rows, block_rows), jnp.float32),
        ),
        compiler_params=ROOM,
        name="cross_statistics",
    )(q_blk, g_blk, k_blk, v_blk, row_stats)


def cross_grads(q_blk, g_blk, sums, all_stats, feature, inv_root):
    tokens, both_width = sums.shape
    block_rows = q_blk.shape[0]
    columns = both_width // (2 * feature)

    def kernel(q_ref, g_ref, sums_ref, stat_ref, dl_ref, dsum_ref):
        peaks = stat_ref[:, :columns, :]
        peak = jnp.max(peaks, axis=0)
        weight = jnp.exp(peaks - peak[None])
        total = jnp.sum(weight * stat_ref[:, columns : 2 * columns, :], axis=0)
        delta = jnp.sum(weight * stat_ref[:, 2 * columns : 3 * columns, :], axis=0) / total
        for c in range(columns):
            scores, dprob, lanes, other = cross_scores(sums_ref, q_ref, g_ref, c, feature, inv_root)
            probs = jnp.exp(scores - peak[c : c + 1, :]) / total[c : c + 1, :]
            dl = (inv_root * probs * (dprob - delta[c : c + 1, :])).astype(jnp.bfloat16)
            dl_ref[c * tokens : (c + 1) * tokens, :] = dl
            dsum_ref[:, lanes] = dot_f32(dl, q_ref[:, lanes])
            dsum_ref[:, other] = dot_f32(probs.astype(jnp.bfloat16), g_ref[:, lanes])

    return pl.pallas_call(
        kernel,
        out_shape=(
            jax.ShapeDtypeStruct((columns * tokens, block_rows), jnp.bfloat16),
            jax.ShapeDtypeStruct((tokens, both_width), jnp.float32),
        ),
        compiler_params=ROOM,
        name="cross_grads",
    )(q_blk, g_blk, sums, all_stats)


def block_softmax(logit_scale, logit_sum, own, forward, back, key_flags):
    rows, width = logit_sum.shape

    def kernel(logit_ref, own_ref, forward_ref, back_ref, flag_ref, both_ref, stat_ref):
        dprob = (
            own_ref[...].astype(jnp.float32)
            + forward_ref[...].astype(jnp.float32)
            + back_ref[...].astype(jnp.float32)
        )
        logits = jnp.where(flag_ref[...] > 0, logit_ref[...] * logit_scale, -1e30)
        peak = jnp.max(logits, axis=1, keepdims=True)
        lifted = jnp.exp(logits - peak)
        total = jnp.sum(lifted, axis=1, keepdims=True)
        weighted = jnp.sum(lifted * dprob, axis=1, keepdims=True)
        delta = weighted / total
        both_ref[:, :width] = lifted.astype(jnp.bfloat16)
        both_ref[:, width:] = (lifted * (dprob - delta)).astype(jnp.bfloat16)
        for i, column in enumerate((peak, total, weighted, delta)):
            stat_ref[i : i + 1, :] = across(column)
        stat_ref[4:8, :] = jnp.zeros((4, rows), jnp.float32)

    return pl.pallas_call(
        kernel,
        out_shape=(
            jax.ShapeDtypeStruct((rows, 2 * width), jnp.bfloat16),
            jax.ShapeDtypeStruct((8, rows), jnp.float32),
        ),
        compiler_params=ROOM,
        name="block_softmax",
    )(logit_sum, own, forward, back, key_flags)


def query_grads(logit_scale, place, both, scaling, k_blk, cross_dl, sums, chunks):
    block_rows, width = both.shape[0], both.shape[1] // 2
    rows = block_rows // chunks
    flat_width = k_blk.shape[1]
    tokens = sums.shape[0]
    columns = cross_dl.shape[0] // tokens
    feature = flat_width // columns

    def kernel(place_ref, both_ref, scale_ref, k_ref, dl_ref, sums_ref, p_ref, ds_ref, own_ref, other_ref, dq_ref, held_ref, sems):
        core = place_ref[0]
        copies = []
        for i in range(chunks):
            at = pl.ds(i * rows, rows)
            copies.append(pltpu.make_async_copy(both_ref.at[at], held_ref.at[at], sems.at[i]))
            copies[i].start()
        for i in range(chunks):
            at = slice(i * rows, (i + 1) * rows)
            copies[i].wait()
            weight, offset = upright(scale_ref[i, 0:1, :]), upright(scale_ref[i, 1:2, :])
            lifted = held_ref[at, :width].astype(jnp.float32)
            tilted = held_ref[at, width:].astype(jnp.float32)
            p_ref[at, :] = (lifted * weight).astype(jnp.bfloat16)
            ds_ref[at, :] = ((tilted - lifted * offset) * (weight * logit_scale)).astype(
                jnp.bfloat16
            )
        dq_ref[...] = dot_f32(ds_ref[...], k_ref[...])
        for c in range(columns):
            lanes = slice(c * feature, (c + 1) * feature)
            dq_ref[:, lanes] += dot_f32(
                dl_ref[c * tokens : (c + 1) * tokens, :], sums_ref[:, lanes], LEAD_PAIR
            )
        for x in range(chunks // 2):
            to = slice(x * rows, (x + 1) * rows)
            mine = pl.multiple_of((2 * x + core) * rows, rows)
            theirs = pl.multiple_of((2 * x + 1 - core) * rows, rows)
            own_ref[to, :] = dq_ref[pl.ds(mine, rows), :]
            other_ref[to, :] = dq_ref[pl.ds(theirs, rows), :].astype(jnp.bfloat16)

    return pl.pallas_call(
        kernel,
        in_specs=[SMEM, pl.BlockSpec(memory_space=pltpu.HBM)] + [WHOLE] * 4,
        out_shape=(
            jax.ShapeDtypeStruct((block_rows, width), jnp.bfloat16),
            jax.ShapeDtypeStruct((block_rows, width), jnp.bfloat16),
            jax.ShapeDtypeStruct((block_rows // 2, flat_width), jnp.float32),
            jax.ShapeDtypeStruct((block_rows // 2, flat_width), jnp.bfloat16),
        ),
        scratch_shapes=[
            pltpu.VMEM((block_rows, flat_width), jnp.float32),
            pltpu.VMEM((block_rows, 2 * width), jnp.bfloat16),
            pltpu.SemaphoreType.DMA((chunks,)),
        ],
        compiler_params=ROOM,
        name="query_grads",
    )(place, pltpu.with_memory_space_constraint(both, pltpu.HBM), scaling, k_blk, cross_dl, sums)


def key_grads(prob, dlogit, q_blk, g_blk, dsum, pieces):
    width, flat_width = prob.shape[1], q_blk.shape[1]
    tokens = dsum.shape[0]
    group = width // tokens
    piece = width // pieces

    def kernel(p_ref, ds_ref, q_ref, g_ref, dsum_ref, *out_refs):
        for half, (w_ref, t_ref) in enumerate(((ds_ref, q_ref), (p_ref, g_ref))):
            lanes = slice(half * flat_width, (half + 1) * flat_width)
            grads = dot_f32(w_ref[...], t_ref[...], LEAD_PAIR)
            shared = dsum_ref[:, lanes] / group
            grads = grads.reshape(tokens, group, flat_width) + shared[:, None, :]
            grads = grads.reshape(width, flat_width).astype(jnp.bfloat16)
            for s, out_ref in enumerate(out_refs):
                out_ref[:, lanes] = grads[s * piece : (s + 1) * piece]

    return pl.pallas_call(
        kernel,
        out_shape=tuple(
            jax.ShapeDtypeStruct((piece, 2 * flat_width), jnp.bfloat16) for _ in range(pieces)
        ),
        compiler_params=ROOM,
        name="key_grads",
    )(prob, dlogit, q_blk, g_blk, dsum)


def shards(queries, keys, values, out_grad, row_keep, row_lengths):
    rows_dev, cols_dev, feature = queries.shape
    row_axis, zs = lax.axis_size("row"), lax.axis_size("col")
    ys = row_axis // (2 * XS)
    near_size = 2 * XS
    total_rows = rows_dev * row_axis
    total_cols = cols_dev * zs
    group_rows = total_rows // SUMMARIES
    flat_width = cols_dev * feature
    block_rows = near_size * rows_dev
    block_keys = ys * rows_dev
    tokens = block_keys // group_rows
    near = [[y * near_size + i for i in range(near_size)] for y in range(ys)]
    own_x = (lax.axis_index("row") // 2) % XS
    own_core = lax.axis_index("row") % 2
    own_z = lax.axis_index("col")
    place = jnp.stack([own_core, own_z]).astype(jnp.int32)
    logit_scale = 1.0 / math.sqrt(total_cols * feature)
    inv_root = 1.0 / math.sqrt(feature)

    def at(y, x, core):
        return ((y % ys) * XS + x % XS) * 2 + core

    cells = [(y, x, c) for y in range(ys) for x in range(XS) for c in range(2)]

    def shift_y(table, step):
        return lax.ppermute(table, "row", [(at(y, x, c), at(y + step, x, c)) for y, x, c in cells])

    def shift_x(table, step):
        return lax.ppermute(table, "row", [(at(y, x, c), at(y, x + step, c)) for y, x, c in cells])

    def swap_core(table):
        return lax.ppermute(table, "row", [(at(y, x, c), at(y, x, 1 - c)) for y, x, c in cells])

    def shift_z(table, step):
        return lax.ppermute(table, "col", [(z, (z + step) % zs) for z in range(zs)])

    def share(table, axis, groups=None):
        count = lax.axis_size(axis) if groups is None else len(groups[0])
        copies = jnp.broadcast_to(table[None], (count,) + table.shape)
        return lax.all_to_all(
            copies, axis, split_axis=0, concat_axis=0, tiled=True, axis_index_groups=groups
        )

    column_ids = own_z * cols_dev + jnp.arange(cols_dev, dtype=jnp.int32)
    cell_keep = (row_keep[:, None] == 1) & (column_ids[None, :] < row_lengths[:, None])
    keep_flat = jnp.broadcast_to(cell_keep[:, :, None], queries.shape).reshape(
        rows_dev, flat_width
    )
    zero = jnp.zeros((), queries.dtype)

    def masked(table):
        flat = jnp.where(keep_flat, table.reshape(rows_dev, flat_width), zero)
        return with_layout_constraint(flat, Layout((0, 1)))

    def wave(first, second, chained):
        along_x = {s: shift_x(first, s) for s in range(1, XS)}
        late = second
        if chained:
            late, along_x[1] = lax.optimization_barrier((second, along_x[1]))
        along_y = {s: shift_y(late if s == ys - 1 else second, s) for s in range(1, ys)}
        return lax.optimization_barrier(
            (
                [first] + [along_x[s] for s in range(1, XS)],
                [second] + [along_y[s] for s in range(1, ys)],
            )
        )

    def in_line(pieces):
        line = jnp.zeros((XS, rows_dev, flat_width), queries.dtype)
        for s, piece in enumerate(pieces):
            line = lax.dynamic_update_slice(line, piece[None], ((own_x - s) % XS, 0, 0))
        return line

    def both_lines(line, other):
        first = jnp.where(own_core == 0, line, other)
        second = jnp.where(own_core == 0, other, line)
        return jnp.stack([first, second], axis=1).reshape(block_rows, flat_width)

    q_pieces, k_pieces = wave(*lax.optimization_barrier((masked(queries), masked(keys))), True)
    q_line = in_line(q_pieces)
    q_other, keep_flat = lax.optimization_barrier((swap_core(q_line), keep_flat))
    q_blk = both_lines(q_line, q_other)
    k_blk = jnp.concatenate(k_pieces, axis=0)
    logit_piece = dot_f32(q_blk, k_blk, ROW_PAIR)
    flag_rows = jnp.pad(
        row_keep.astype(jnp.bfloat16)[None, :], ((0, FLAG_ROWS - 1), (0, flat_width - rows_dev))
    )
    g_pieces, key_pieces = wave(
        masked(out_grad), jnp.concatenate([masked(values), flag_rows], axis=0), False
    )
    v_blk = jnp.concatenate([p[:rows_dev] for p in key_pieces], axis=0)
    g_line = in_line(g_pieces)
    g_blk = both_lines(g_line, swap_core(g_line))
    g_blk, _ = lax.optimization_barrier((g_blk, logit_piece))
    dprob_piece = dot_f32(g_blk, v_blk, ROW_PAIR).astype(jnp.bfloat16)
    key_flags = jnp.concatenate([p[rows_dev, :rows_dev] for p in key_pieces])[None, :]
    logit_sum = lax.psum_scatter(logit_piece, "col", scatter_dimension=0, tiled=True)

    dprob_chunks = dprob_piece.reshape(zs, block_rows // zs, block_keys)

    def part(step):
        return lax.dynamic_index_in_dim(dprob_chunks, (own_z + step) % zs, axis=0, keepdims=False)

    def passed(step, count):
        moving = part(step * count)
        for left in range(count - 1, -1, -1):
            moving = shift_z(moving, step)
            if left > 0:
                moving = (
                    moving.astype(jnp.float32) + part(step * left).astype(jnp.float32)
                ).astype(jnp.bfloat16)
        return moving

    dprob_forward = passed(1, zs // 2)
    dprob_back = passed(-1, zs - 1 - zs // 2)

    both, stats = block_softmax(
        logit_scale, logit_sum, part(0), dprob_forward, dprob_back, key_flags
    )
    both = lax.all_gather(both, "col", axis=0, tiled=True)

    sums, own_stats = cross_statistics(
        q_blk, g_blk, k_blk, v_blk, stats, tokens, feature, inv_root
    )
    all_stats = share(own_stats, "row", near)
    row_stats = all_stats[:, 3 * cols_dev, : 3 * rows_dev].reshape(near_size, 3, rows_dev)
    peak = jnp.max(row_stats[:, 0], axis=0)
    weight = jnp.exp(row_stats[:, 0] - peak)
    total = jnp.sum(weight * row_stats[:, 1], axis=0)
    delta = jnp.sum(weight * row_stats[:, 2], axis=0) / total
    scaling = share(jnp.stack([jnp.exp(stats[0] - peak) / total, delta - stats[3]]), "col")
    cross_dl, dsum = cross_grads(q_blk, g_blk, sums, all_stats, feature, inv_root)
    both, scaling, cross_dl, dsum = lax.optimization_barrier((both, scaling, cross_dl, dsum))

    prob, dlogit, dq_own, dq_other = query_grads(
        logit_scale, place, both, scaling, k_blk, cross_dl, sums, zs
    )
    dq_swapped = swap_core(dq_other)
    key_parts = key_grads(prob, dlogit, q_blk, g_blk, dsum, ys)
    key_moved = [shift_y(key_parts[s], -s) for s in range(1, ys)]
    line = (dq_own + dq_swapped.astype(jnp.float32)).astype(jnp.bfloat16)
    line = line.reshape(XS, rows_dev, flat_width)
    lines = [[at(y, x, c) for x in range(XS)] for y in range(ys) for c in range(2)]
    line = lax.all_to_all(
        line, "row", split_axis=0, concat_axis=0, tiled=True, axis_index_groups=lines
    )

    def added(parts):
        return sum(p.astype(jnp.float32) for p in parts)

    grad_q = added([line[x] for x in range(XS)])
    grad_kv = added([key_parts[0]] + key_moved)

    def finished(rows):
        return (
            jnp.where(keep_flat, rows, 0.0)
            .astype(jnp.bfloat16)
            .reshape(rows_dev, cols_dev, feature)
        )

    return (
        finished(grad_q),
        finished(grad_kv[:, :flat_width]),
        finished(grad_kv[:, flat_width:]),
    )


def solution(mesh):
    return jax.shard_map(
        shards,
        mesh=mesh,
        in_specs=(
            P("row", "col", None),
            P("row", "col", None),
            P("row", "col", None),
            P("row", "col", None),
            P("row"),
            P("row"),
        ),
        out_specs=(P("row", "col", None), P("row", "col", None), P("row", "col", None)),
        check_vma=False,
    )
```

```python
import math

import jax
import jax.numpy as jnp
from jax import lax
from jax.experimental import pallas as pl
from jax.experimental.layout import Layout, with_layout_constraint
from jax.experimental.pallas import tpu as pltpu
from jax.sharding import PartitionSpec as P

SUMMARIES = 256
XS = 4

ROW_PAIR = (((1,), (1,)), ((), ()))
LEAD_PAIR = (((0,), (0,)), ((), ()))
PLAIN = (((1,), (0,)), ((), ()))

WHOLE = pl.BlockSpec()
SMEM = pl.BlockSpec(memory_space=pltpu.SMEM)
ROOM = pltpu.CompilerParams(vmem_limit_bytes=24 * 1024 * 1024)


def dot_f32(left, right, dims=PLAIN):
    return lax.dot_general(left, right, dims, preferred_element_type=jnp.float32)


def diagonal(n):
    return lax.broadcasted_iota(jnp.int32, (n, n), 0) == lax.broadcasted_iota(jnp.int32, (n, n), 1)


def across(column):
    return jnp.sum(jnp.where(diagonal(column.shape[0]), column, 0.0), axis=0, keepdims=True)


def upright(row):
    return jnp.sum(jnp.where(diagonal(row.shape[1]), row, 0.0), axis=1, keepdims=True)


def cross_scores(sums_ref, q_ref, g_ref, column, feature, inv_root):
    flat_width = q_ref.shape[1]
    lanes = slice(column * feature, (column + 1) * feature)
    other = slice(flat_width + column * feature, flat_width + (column + 1) * feature)
    scores = dot_f32(sums_ref[:, lanes], q_ref[:, lanes], ROW_PAIR) * inv_root
    dprob = dot_f32(sums_ref[:, other], g_ref[:, lanes], ROW_PAIR)
    return scores, dprob, lanes, other


def cross_statistics(q_blk, g_blk, k_blk, v_blk, row_stats, tokens, feature, inv_root):
    block_keys, flat_width = k_blk.shape
    both_width = 2 * flat_width
    block_rows = q_blk.shape[0]
    group = block_keys // tokens
    columns = both_width // (2 * feature)
    stat_rows = -(-(3 * columns + 1) // 8) * 8
    kinds, rows = 3, row_stats.shape[1]

    def kernel(q_ref, g_ref, k_ref, v_ref, row_ref, sums_ref, stat_ref):
        for half, table_ref in enumerate((k_ref, v_ref)):
            pooled = jnp.sum(
                table_ref[...].astype(jnp.float32).reshape(tokens, group, flat_width), axis=1
            )
            sums_ref[:, half * flat_width : (half + 1) * flat_width] = (pooled / group).astype(
                jnp.bfloat16
            )
        for c in range(columns):
            scores, dprob, _, _ = cross_scores(sums_ref, q_ref, g_ref, c, feature, inv_root)
            peak = jnp.max(scores, axis=0, keepdims=True)
            lifted = jnp.exp(scores - peak)
            stat_ref[c : c + 1, :] = peak
            stat_ref[columns + c : columns + c + 1, :] = jnp.sum(lifted, axis=0, keepdims=True)
            stat_ref[2 * columns + c : 2 * columns + c + 1, :] = jnp.sum(
                lifted * dprob, axis=0, keepdims=True
            )
        stat_ref[3 * columns :, :] = jnp.zeros((stat_rows - 3 * columns, block_rows), jnp.float32)
        for i in range(kinds):
            stat_ref[3 * columns : 3 * columns + 1, i * rows : (i + 1) * rows] = row_ref[
                i : i + 1, :
            ]

    return pl.pallas_call(
        kernel,
        out_shape=(
            jax.ShapeDtypeStruct((tokens, both_width), jnp.bfloat16),
            jax.ShapeDtypeStruct((stat_rows, block_rows), jnp.float32),
        ),
        compiler_params=ROOM,
        name="cross_statistics",
    )(q_blk, g_blk, k_blk, v_blk, row_stats)


def cross_grads(q_blk, g_blk, sums, all_stats, feature, inv_root):
    tokens, both_width = sums.shape
    block_rows = q_blk.shape[0]
    columns = both_width // (2 * feature)

    def kernel(q_ref, g_ref, sums_ref, stat_ref, dl_ref, dsum_ref):
        peaks = stat_ref[:, :columns, :]
        peak = jnp.max(peaks, axis=0)
        weight = jnp.exp(peaks - peak[None])
        total = jnp.sum(weight * stat_ref[:, columns : 2 * columns, :], axis=0)
        delta = jnp.sum(weight * stat_ref[:, 2 * columns : 3 * columns, :], axis=0) / total
        for c in range(columns):
            scores, dprob, lanes, other = cross_scores(sums_ref, q_ref, g_ref, c, feature, inv_root)
            probs = jnp.exp(scores - peak[c : c + 1, :]) / total[c : c + 1, :]
            dl = (inv_root * probs * (dprob - delta[c : c + 1, :])).astype(jnp.bfloat16)
            dl_ref[c * tokens : (c + 1) * tokens, :] = dl
            dsum_ref[:, lanes] = dot_f32(dl, q_ref[:, lanes])
            dsum_ref[:, other] = dot_f32(probs.astype(jnp.bfloat16), g_ref[:, lanes])

    return pl.pallas_call(
        kernel,
        out_shape=(
            jax.ShapeDtypeStruct((columns * tokens, block_rows), jnp.bfloat16),
            jax.ShapeDtypeStruct((tokens, both_width), jnp.float32),
        ),
        compiler_params=ROOM,
        name="cross_grads",
    )(q_blk, g_blk, sums, all_stats)


def block_softmax(logit_scale, logit_sum, own, forward, back, key_flags):
    rows, width = logit_sum.shape

    def kernel(logit_ref, own_ref, forward_ref, back_ref, flag_ref, both_ref, stat_ref):
        dprob = (
            own_ref[...].astype(jnp.float32)
            + forward_ref[...].astype(jnp.float32)
            + back_ref[...].astype(jnp.float32)
        )
        logits = jnp.where(flag_ref[...] > 0, logit_ref[...] * logit_scale, -1e30)
        peak = jnp.max(logits, axis=1, keepdims=True)
        lifted = jnp.exp(logits - peak)
        total = jnp.sum(lifted, axis=1, keepdims=True)
        weighted = jnp.sum(lifted * dprob, axis=1, keepdims=True)
        delta = weighted / total
        both_ref[:, :width] = lifted.astype(jnp.bfloat16)
        both_ref[:, width:] = (lifted * (dprob - delta)).astype(jnp.bfloat16)
        for i, column in enumerate((peak, total, weighted, delta)):
            stat_ref[i : i + 1, :] = across(column)
        stat_ref[4:8, :] = jnp.zeros((4, rows), jnp.float32)

    return pl.pallas_call(
        kernel,
        out_shape=(
            jax.ShapeDtypeStruct((rows, 2 * width), jnp.bfloat16),
            jax.ShapeDtypeStruct((8, rows), jnp.float32),
        ),
        compiler_params=ROOM,
        name="block_softmax",
    )(logit_sum, own, forward, back, key_flags)


def key_grads(logit_scale, both, scaling, q_blk, g_blk, dsum, chunks, pieces):
    block_rows, width = both.shape[0], both.shape[1] // 2
    rows = block_rows // chunks
    flat_width = q_blk.shape[1]
    tokens = dsum.shape[0]
    group = width // tokens
    piece = width // pieces

    def kernel(both_ref, scale_ref, q_ref, g_ref, dsum_ref, ds_ref, *refs):
        out_refs, (p_ref, held_ref, sems) = refs[:pieces], refs[pieces:]
        copies = []
        for i in range(chunks):
            at = pl.ds(i * rows, rows)
            copies.append(pltpu.make_async_copy(both_ref.at[at], held_ref.at[at], sems.at[i]))
            copies[i].start()
        for i in range(chunks):
            at = slice(i * rows, (i + 1) * rows)
            weight, offset = upright(scale_ref[i, 0:1, :]), upright(scale_ref[i, 1:2, :])
            copies[i].wait()
            lifted = held_ref[at, :width].astype(jnp.float32)
            tilted = held_ref[at, width:].astype(jnp.float32)
            p_ref[at, :] = (lifted * weight).astype(jnp.bfloat16)
            ds_ref[at, :] = ((tilted - lifted * offset) * (weight * logit_scale)).astype(
                jnp.bfloat16
            )
        for half, (w_ref, t_ref) in enumerate(((ds_ref, q_ref), (p_ref, g_ref))):
            lanes = slice(half * flat_width, (half + 1) * flat_width)
            grads = dot_f32(w_ref[...], t_ref[...], LEAD_PAIR)
            shared = dsum_ref[:, lanes] / group
            grads = grads.reshape(tokens, group, flat_width) + shared[:, None, :]
            grads = grads.reshape(width, flat_width).astype(jnp.bfloat16)
            for s, out_ref in enumerate(out_refs):
                out_ref[:, lanes] = grads[s * piece : (s + 1) * piece]

    return pl.pallas_call(
        kernel,
        in_specs=[pl.BlockSpec(memory_space=pltpu.HBM)] + [WHOLE] * 4,
        out_shape=(jax.ShapeDtypeStruct((block_rows, width), jnp.bfloat16),)
        + tuple(
            jax.ShapeDtypeStruct((piece, 2 * flat_width), jnp.bfloat16) for _ in range(pieces)
        ),
        scratch_shapes=[
            pltpu.VMEM((block_rows, width), jnp.bfloat16),
            pltpu.VMEM((block_rows, 2 * width), jnp.bfloat16),
            pltpu.SemaphoreType.DMA((chunks,)),
        ],
        compiler_params=ROOM,
        name="key_grads",
    )(pltpu.with_memory_space_constraint(both, pltpu.HBM), scaling, q_blk, g_blk, dsum)


def query_grads(place, dlogit, k_blk, cross_dl, sums, chunks):
    block_rows = dlogit.shape[0]
    rows = block_rows // chunks
    flat_width = k_blk.shape[1]
    tokens = sums.shape[0]
    columns = cross_dl.shape[0] // tokens
    feature = flat_width // columns

    def kernel(place_ref, ds_ref, k_ref, dl_ref, sums_ref, own_ref, other_ref, dq_ref):
        core = place_ref[0]
        dq_ref[...] = dot_f32(ds_ref[...], k_ref[...])
        for c in range(columns):
            lanes = slice(c * feature, (c + 1) * feature)
            dq_ref[:, lanes] += dot_f32(
                dl_ref[c * tokens : (c + 1) * tokens, :], sums_ref[:, lanes], LEAD_PAIR
            )
        for x in range(chunks // 2):
            to = slice(x * rows, (x + 1) * rows)
            mine = pl.multiple_of((2 * x + core) * rows, rows)
            theirs = pl.multiple_of((2 * x + 1 - core) * rows, rows)
            own_ref[to, :] = dq_ref[pl.ds(mine, rows), :]
            other_ref[to, :] = dq_ref[pl.ds(theirs, rows), :].astype(jnp.bfloat16)

    return pl.pallas_call(
        kernel,
        in_specs=[SMEM] + [WHOLE] * 4,
        out_shape=(
            jax.ShapeDtypeStruct((block_rows // 2, flat_width), jnp.float32),
            jax.ShapeDtypeStruct((block_rows // 2, flat_width), jnp.bfloat16),
        ),
        scratch_shapes=[pltpu.VMEM((block_rows, flat_width), jnp.float32)],
        compiler_params=ROOM,
        name="query_grads",
    )(place, dlogit, k_blk, cross_dl, sums)


def shards(queries, keys, values, out_grad, row_keep, row_lengths):
    rows_dev, cols_dev, feature = queries.shape
    row_axis, zs = lax.axis_size("row"), lax.axis_size("col")
    ys = row_axis // (2 * XS)
    near_size = 2 * XS
    total_rows = rows_dev * row_axis
    total_cols = cols_dev * zs
    group_rows = total_rows // SUMMARIES
    flat_width = cols_dev * feature
    block_rows = near_size * rows_dev
    block_keys = ys * rows_dev
    tokens = block_keys // group_rows
    near = [[y * near_size + i for i in range(near_size)] for y in range(ys)]
    own_x = (lax.axis_index("row") // 2) % XS
    own_core = lax.axis_index("row") % 2
    own_z = lax.axis_index("col")
    place = jnp.stack([own_core, own_z]).astype(jnp.int32)
    logit_scale = 1.0 / math.sqrt(total_cols * feature)
    inv_root = 1.0 / math.sqrt(feature)

    def at(y, x, core):
        return ((y % ys) * XS + x % XS) * 2 + core

    cells = [(y, x, c) for y in range(ys) for x in range(XS) for c in range(2)]

    def shift_y(table, step):
        return lax.ppermute(table, "row", [(at(y, x, c), at(y + step, x, c)) for y, x, c in cells])

    def shift_x(table, step):
        return lax.ppermute(table, "row", [(at(y, x, c), at(y, x + step, c)) for y, x, c in cells])

    def swap_core(table):
        return lax.ppermute(table, "row", [(at(y, x, c), at(y, x, 1 - c)) for y, x, c in cells])

    def shift_z(table, step):
        return lax.ppermute(table, "col", [(z, (z + step) % zs) for z in range(zs)])

    def share(table, axis, groups=None):
        count = lax.axis_size(axis) if groups is None else len(groups[0])
        copies = jnp.broadcast_to(table[None], (count,) + table.shape)
        return lax.all_to_all(
            copies, axis, split_axis=0, concat_axis=0, tiled=True, axis_index_groups=groups
        )

    own_columns = jnp.where(row_keep == 1, row_lengths, 0) - own_z * cols_dev
    cell_keep = jnp.arange(cols_dev, dtype=jnp.int32)[None, :] < own_columns[:, None]
    keep_flat = jnp.broadcast_to(cell_keep[:, :, None], queries.shape).reshape(
        rows_dev, flat_width
    )
    zero = jnp.zeros((), queries.dtype)

    def masked(table):
        flat = jnp.where(keep_flat, table.reshape(rows_dev, flat_width), zero)
        return with_layout_constraint(flat, Layout((0, 1)))

    def wave(first, second, chained):
        along_x = {s: shift_x(first, s) for s in range(1, XS)}
        late = second
        if chained:
            late, along_x[1] = lax.optimization_barrier((second, along_x[1]))
        along_y = {s: shift_y(late if s == ys - 1 else second, s) for s in range(1, ys)}
        return lax.optimization_barrier(
            (
                [first] + [along_x[s] for s in range(1, XS)],
                [second] + [along_y[s] for s in range(1, ys)],
            )
        )

    def in_line(pieces):
        line = jnp.zeros((XS, rows_dev, flat_width), queries.dtype)
        for s, piece in enumerate(pieces):
            line = lax.dynamic_update_slice(line, piece[None], ((own_x - s) % XS, 0, 0))
        return line

    def both_lines(line, other):
        first = jnp.where(own_core == 0, line, other)
        second = jnp.where(own_core == 0, other, line)
        return jnp.stack([first, second], axis=1).reshape(block_rows, flat_width)

    q_pieces, k_pieces = wave(*lax.optimization_barrier((masked(queries), masked(keys))), True)
    q_line = in_line(q_pieces)
    q_other, keep_flat = lax.optimization_barrier((swap_core(q_line), keep_flat))
    q_blk = both_lines(q_line, q_other)
    k_blk = jnp.concatenate(k_pieces, axis=0)
    logit_piece = dot_f32(q_blk, k_blk, ROW_PAIR)
    g_pieces, v_pieces = wave(masked(out_grad), masked(values), False)
    v_blk = jnp.concatenate(v_pieces, axis=0)
    g_line = in_line(g_pieces)
    g_blk = both_lines(g_line, swap_core(g_line))
    g_blk, _ = lax.optimization_barrier((g_blk, logit_piece))
    dprob_piece = dot_f32(g_blk, v_blk, ROW_PAIR).astype(jnp.bfloat16)
    own_flags, _ = lax.optimization_barrier((row_keep.astype(jnp.float32)[None, :], dprob_piece))
    key_flags = jnp.concatenate(
        [own_flags] + [shift_y(own_flags, s) for s in range(1, ys)], axis=1
    )
    logit_sum = lax.psum_scatter(logit_piece, "col", scatter_dimension=0, tiled=True)

    dprob_chunks = dprob_piece.reshape(zs, block_rows // zs, block_keys)

    def part(step):
        return lax.dynamic_index_in_dim(dprob_chunks, (own_z + step) % zs, axis=0, keepdims=False)

    def passed(step, count, beside=None):
        moving = part(step * count)
        for left in range(count - 1, -1, -1):
            moving = shift_z(moving, step)
            if beside is not None and left == count - 1:
                moving, beside = lax.optimization_barrier((moving, beside))
            if left > 0:
                moving = (
                    moving.astype(jnp.float32) + part(step * left).astype(jnp.float32)
                ).astype(jnp.bfloat16)
        return moving, beside

    dprob_forward, key_flags = passed(1, zs // 2, key_flags)
    dprob_back, _ = passed(-1, zs - 1 - zs // 2)

    both, stats = block_softmax(
        logit_scale, logit_sum, part(0), dprob_forward, dprob_back, key_flags
    )
    both = lax.all_gather(both, "col", axis=0, tiled=True)

    sums, own_stats = cross_statistics(
        q_blk, g_blk, k_blk, v_blk, stats, tokens, feature, inv_root
    )
    all_stats = share(own_stats, "row", near)
    row_stats = all_stats[:, 3 * cols_dev, : 3 * rows_dev].reshape(near_size, 3, rows_dev)
    peak = jnp.max(row_stats[:, 0], axis=0)
    weight = jnp.exp(row_stats[:, 0] - peak)
    total = jnp.sum(weight * row_stats[:, 1], axis=0)
    delta = jnp.sum(weight * row_stats[:, 2], axis=0) / total
    scaling = share(jnp.stack([jnp.exp(stats[0] - peak) / total, delta - stats[3]]), "col")
    cross_dl, dsum = cross_grads(q_blk, g_blk, sums, all_stats, feature, inv_root)
    both, scaling, cross_dl, dsum = lax.optimization_barrier((both, scaling, cross_dl, dsum))

    dlogit, *key_parts = key_grads(logit_scale, both, scaling, q_blk, g_blk, dsum, zs, ys)
    dq_own, dq_other = query_grads(place, dlogit, k_blk, cross_dl, sums, near_size)
    dq_swapped = swap_core(dq_other)
    key_moved = [shift_y(key_parts[s], -s) for s in range(1, ys)]
    line = (dq_own + dq_swapped.astype(jnp.float32)).astype(jnp.bfloat16)
    line = line.reshape(XS, rows_dev, flat_width)
    lines = [[at(y, x, c) for x in range(XS)] for y in range(ys) for c in range(2)]
    line = lax.all_to_all(
        line, "row", split_axis=0, concat_axis=0, tiled=True, axis_index_groups=lines
    )

    def added(parts):
        return sum(p.astype(jnp.float32) for p in parts)

    grad_q = added([line[x] for x in range(XS)])
    grad_kv = added([key_parts[0]] + key_moved)

    def finished(rows):
        return (
            jnp.where(keep_flat, rows, 0.0)
            .astype(jnp.bfloat16)
            .reshape(rows_dev, cols_dev, feature)
        )

    return (
        finished(grad_q),
        finished(grad_kv[:, :flat_width]),
        finished(grad_kv[:, flat_width:]),
    )


def solution(mesh):
    return jax.shard_map(
        shards,
        mesh=mesh,
        in_specs=(
            P("row", "col", None),
            P("row", "col", None),
            P("row", "col", None),
            P("row", "col", None),
            P("row"),
            P("row"),
        ),
        out_specs=(P("row", "col", None), P("row", "col", None), P("row", "col", None)),
        check_vma=False,
    )
```

```python
import math

import jax
import jax.numpy as jnp
from jax import lax
from jax.experimental import pallas as pl
from jax.experimental.layout import Layout, with_layout_constraint
from jax.experimental.pallas import tpu as pltpu
from jax.sharding import PartitionSpec as P

SUMMARIES = 256
XS = 4

ROW_PAIR = (((1,), (1,)), ((), ()))
LEAD_PAIR = (((0,), (0,)), ((), ()))
PLAIN = (((1,), (0,)), ((), ()))

WHOLE = pl.BlockSpec()
SMEM = pl.BlockSpec(memory_space=pltpu.SMEM)
ROOM = pltpu.CompilerParams(vmem_limit_bytes=24 * 1024 * 1024)


def dot_f32(left, right, dims=PLAIN):
    return lax.dot_general(left, right, dims, preferred_element_type=jnp.float32)


def diagonal(n):
    return lax.broadcasted_iota(jnp.int32, (n, n), 0) == lax.broadcasted_iota(jnp.int32, (n, n), 1)


def across(column):
    return jnp.sum(jnp.where(diagonal(column.shape[0]), column, 0.0), axis=0, keepdims=True)


def upright(row):
    return jnp.sum(jnp.where(diagonal(row.shape[1]), row, 0.0), axis=1, keepdims=True)


def cross_scores(sums_ref, q_ref, g_ref, column, feature, inv_root):
    flat_width = q_ref.shape[1]
    lanes = slice(column * feature, (column + 1) * feature)
    other = slice(flat_width + column * feature, flat_width + (column + 1) * feature)
    scores = dot_f32(sums_ref[:, lanes], q_ref[:, lanes], ROW_PAIR) * inv_root
    dprob = dot_f32(sums_ref[:, other], g_ref[:, lanes], ROW_PAIR)
    return scores, dprob, lanes, other


def cross_statistics(q_blk, g_blk, k_blk, v_blk, row_stats, tokens, feature, inv_root):
    block_keys, flat_width = k_blk.shape
    both_width = 2 * flat_width
    block_rows = q_blk.shape[0]
    group = block_keys // tokens
    columns = both_width // (2 * feature)
    stat_rows = -(-(3 * columns + 1) // 8) * 8
    kinds, rows = 3, row_stats.shape[1]

    def kernel(q_ref, g_ref, k_ref, v_ref, row_ref, sums_ref, stat_ref):
        for half, table_ref in enumerate((k_ref, v_ref)):
            pooled = jnp.sum(
                table_ref[...].astype(jnp.float32).reshape(tokens, group, flat_width), axis=1
            )
            sums_ref[:, half * flat_width : (half + 1) * flat_width] = (pooled / group).astype(
                jnp.bfloat16
            )
        for c in range(columns):
            scores, dprob, _, _ = cross_scores(sums_ref, q_ref, g_ref, c, feature, inv_root)
            peak = jnp.max(scores, axis=0, keepdims=True)
            lifted = jnp.exp(scores - peak)
            stat_ref[c : c + 1, :] = peak
            stat_ref[columns + c : columns + c + 1, :] = jnp.sum(lifted, axis=0, keepdims=True)
            stat_ref[2 * columns + c : 2 * columns + c + 1, :] = jnp.sum(
                lifted * dprob, axis=0, keepdims=True
            )
        stat_ref[3 * columns :, :] = jnp.zeros((stat_rows - 3 * columns, block_rows), jnp.float32)
        for i in range(kinds):
            stat_ref[3 * columns : 3 * columns + 1, i * rows : (i + 1) * rows] = row_ref[
                i : i + 1, :
            ]

    return pl.pallas_call(
        kernel,
        out_shape=(
            jax.ShapeDtypeStruct((tokens, both_width), jnp.bfloat16),
            jax.ShapeDtypeStruct((stat_rows, block_rows), jnp.float32),
        ),
        compiler_params=ROOM,
        name="cross_statistics",
    )(q_blk, g_blk, k_blk, v_blk, row_stats)


def cross_grads(q_blk, g_blk, sums, all_stats, feature, inv_root):
    tokens, both_width = sums.shape
    block_rows = q_blk.shape[0]
    columns = both_width // (2 * feature)

    def kernel(q_ref, g_ref, sums_ref, stat_ref, dl_ref, dsum_ref):
        peaks = stat_ref[:, :columns, :]
        peak = jnp.max(peaks, axis=0)
        weight = jnp.exp(peaks - peak[None])
        total = jnp.sum(weight * stat_ref[:, columns : 2 * columns, :], axis=0)
        delta = jnp.sum(weight * stat_ref[:, 2 * columns : 3 * columns, :], axis=0) / total
        for c in range(columns):
            scores, dprob, lanes, other = cross_scores(sums_ref, q_ref, g_ref, c, feature, inv_root)
            probs = jnp.exp(scores - peak[c : c + 1, :]) / total[c : c + 1, :]
            dl = (inv_root * probs * (dprob - delta[c : c + 1, :])).astype(jnp.bfloat16)
            dl_ref[c * tokens : (c + 1) * tokens, :] = dl
            dsum_ref[:, lanes] = dot_f32(dl, q_ref[:, lanes])
            dsum_ref[:, other] = dot_f32(probs.astype(jnp.bfloat16), g_ref[:, lanes])

    return pl.pallas_call(
        kernel,
        out_shape=(
            jax.ShapeDtypeStruct((columns * tokens, block_rows), jnp.bfloat16),
            jax.ShapeDtypeStruct((tokens, both_width), jnp.float32),
        ),
        compiler_params=ROOM,
        name="cross_grads",
    )(q_blk, g_blk, sums, all_stats)


def block_softmax(logit_scale, logit_sum, own, forward, back, key_flags):
    rows, width = logit_sum.shape

    def kernel(logit_ref, own_ref, forward_ref, back_ref, flag_ref, both_ref, stat_ref):
        dprob = (
            own_ref[...].astype(jnp.float32)
            + forward_ref[...].astype(jnp.float32)
            + back_ref[...].astype(jnp.float32)
        )
        logits = jnp.where(flag_ref[...] > 0, logit_ref[...] * logit_scale, -1e30)
        peak = jnp.max(logits, axis=1, keepdims=True)
        lifted = jnp.exp(logits - peak)
        total = jnp.sum(lifted, axis=1, keepdims=True)
        weighted = jnp.sum(lifted * dprob, axis=1, keepdims=True)
        delta = weighted / total
        both_ref[:, :width] = lifted.astype(jnp.bfloat16)
        both_ref[:, width:] = (lifted * (dprob - delta)).astype(jnp.bfloat16)
        for i, column in enumerate((peak, total, weighted, delta)):
            stat_ref[i : i + 1, :] = across(column)
        stat_ref[4:8, :] = jnp.zeros((4, rows), jnp.float32)

    return pl.pallas_call(
        kernel,
        out_shape=(
            jax.ShapeDtypeStruct((rows, 2 * width), jnp.bfloat16),
            jax.ShapeDtypeStruct((8, rows), jnp.float32),
        ),
        compiler_params=ROOM,
        name="block_softmax",
    )(logit_sum, own, forward, back, key_flags)


def query_grads(logit_scale, place, both, scaling, k_blk, cross_dl, sums, chunks):
    block_rows, width = both.shape[0], both.shape[1] // 2
    rows = block_rows // chunks
    flat_width = k_blk.shape[1]
    tokens = sums.shape[0]
    columns = cross_dl.shape[0] // tokens
    feature = flat_width // columns

    def kernel(place_ref, both_ref, scale_ref, k_ref, dl_ref, sums_ref, p_ref, ds_ref, own_ref, other_ref, dq_ref, held_ref, sems):
        core = place_ref[0]
        copies = []
        for i in range(chunks):
            at = pl.ds(i * rows, rows)
            copies.append(pltpu.make_async_copy(both_ref.at[at], held_ref.at[at], sems.at[i]))
            copies[i].start()
        for i in range(chunks):
            at = slice(i * rows, (i + 1) * rows)
            copies[i].wait()
            weight, offset = upright(scale_ref[i, 0:1, :]), upright(scale_ref[i, 1:2, :])
            lifted = held_ref[at, :width].astype(jnp.float32)
            tilted = held_ref[at, width:].astype(jnp.float32)
            p_ref[at, :] = (lifted * weight).astype(jnp.bfloat16)
            ds_ref[at, :] = ((tilted - lifted * offset) * (weight * logit_scale)).astype(
                jnp.bfloat16
            )
        dq_ref[...] = dot_f32(ds_ref[...], k_ref[...])
        for c in range(columns):
            lanes = slice(c * feature, (c + 1) * feature)
            dq_ref[:, lanes] += dot_f32(
                dl_ref[c * tokens : (c + 1) * tokens, :], sums_ref[:, lanes], LEAD_PAIR
            )
        for x in range(chunks // 2):
            to = slice(x * rows, (x + 1) * rows)
            mine = pl.multiple_of((2 * x + core) * rows, rows)
            theirs = pl.multiple_of((2 * x + 1 - core) * rows, rows)
            own_ref[to, :] = dq_ref[pl.ds(mine, rows), :]
            other_ref[to, :] = dq_ref[pl.ds(theirs, rows), :].astype(jnp.bfloat16)

    return pl.pallas_call(
        kernel,
        in_specs=[SMEM, pl.BlockSpec(memory_space=pltpu.HBM)] + [WHOLE] * 4,
        out_shape=(
            jax.ShapeDtypeStruct((block_rows, width), jnp.bfloat16),
            jax.ShapeDtypeStruct((block_rows, width), jnp.bfloat16),
            jax.ShapeDtypeStruct((block_rows // 2, flat_width), jnp.float32),
            jax.ShapeDtypeStruct((block_rows // 2, flat_width), jnp.bfloat16),
        ),
        scratch_shapes=[
            pltpu.VMEM((block_rows, flat_width), jnp.float32),
            pltpu.VMEM((block_rows, 2 * width), jnp.bfloat16),
            pltpu.SemaphoreType.DMA((chunks,)),
        ],
        compiler_params=ROOM,
        name="query_grads",
    )(place, pltpu.with_memory_space_constraint(both, pltpu.HBM), scaling, k_blk, cross_dl, sums)


def key_grads(prob, dlogit, q_blk, g_blk, dsum, pieces):
    width, flat_width = prob.shape[1], q_blk.shape[1]
    tokens = dsum.shape[0]
    group = width // tokens
    piece = width // pieces

    def kernel(p_ref, ds_ref, q_ref, g_ref, dsum_ref, *out_refs):
        for half, (w_ref, t_ref) in enumerate(((ds_ref, q_ref), (p_ref, g_ref))):
            lanes = slice(half * flat_width, (half + 1) * flat_width)
            grads = dot_f32(w_ref[...], t_ref[...], LEAD_PAIR)
            shared = dsum_ref[:, lanes] / group
            grads = grads.reshape(tokens, group, flat_width) + shared[:, None, :]
            grads = grads.reshape(width, flat_width).astype(jnp.bfloat16)
            for s, out_ref in enumerate(out_refs):
                out_ref[:, lanes] = grads[s * piece : (s + 1) * piece]

    return pl.pallas_call(
        kernel,
        out_shape=tuple(
            jax.ShapeDtypeStruct((piece, 2 * flat_width), jnp.bfloat16) for _ in range(pieces)
        ),
        compiler_params=ROOM,
        name="key_grads",
    )(prob, dlogit, q_blk, g_blk, dsum)


def shards(queries, keys, values, out_grad, row_keep, row_lengths):
    rows_dev, cols_dev, feature = queries.shape
    row_axis, zs = lax.axis_size("row"), lax.axis_size("col")
    ys = row_axis // (2 * XS)
    near_size = 2 * XS
    total_rows = rows_dev * row_axis
    total_cols = cols_dev * zs
    group_rows = total_rows // SUMMARIES
    flat_width = cols_dev * feature
    block_rows = near_size * rows_dev
    block_keys = ys * rows_dev
    tokens = block_keys // group_rows
    near = [[y * near_size + i for i in range(near_size)] for y in range(ys)]
    own_x = (lax.axis_index("row") // 2) % XS
    own_core = lax.axis_index("row") % 2
    own_z = lax.axis_index("col")
    place = jnp.stack([own_core, own_z]).astype(jnp.int32)
    logit_scale = 1.0 / math.sqrt(total_cols * feature)
    inv_root = 1.0 / math.sqrt(feature)

    def at(y, x, core):
        return ((y % ys) * XS + x % XS) * 2 + core

    cells = [(y, x, c) for y in range(ys) for x in range(XS) for c in range(2)]

    def shift_y(table, step):
        return lax.ppermute(table, "row", [(at(y, x, c), at(y + step, x, c)) for y, x, c in cells])

    def shift_x(table, step):
        return lax.ppermute(table, "row", [(at(y, x, c), at(y, x + step, c)) for y, x, c in cells])

    def swap_core(table):
        return lax.ppermute(table, "row", [(at(y, x, c), at(y, x, 1 - c)) for y, x, c in cells])

    def shift_z(table, step):
        return lax.ppermute(table, "col", [(z, (z + step) % zs) for z in range(zs)])

    def share(table, axis, groups=None):
        count = lax.axis_size(axis) if groups is None else len(groups[0])
        copies = jnp.broadcast_to(table[None], (count,) + table.shape)
        return lax.all_to_all(
            copies, axis, split_axis=0, concat_axis=0, tiled=True, axis_index_groups=groups
        )

    own_columns = jnp.where(row_keep == 1, row_lengths, 0) - own_z * cols_dev
    cell_keep = jnp.arange(cols_dev, dtype=jnp.int32)[None, :] < own_columns[:, None]
    keep_flat = jnp.broadcast_to(cell_keep[:, :, None], queries.shape).reshape(
        rows_dev, flat_width
    )
    zero = jnp.zeros((), queries.dtype)

    def masked(table):
        flat = jnp.where(keep_flat, table.reshape(rows_dev, flat_width), zero)
        return with_layout_constraint(flat, Layout((0, 1)))

    def wave(first, second, chained):
        along_x = {s: shift_x(first, s) for s in range(1, XS)}
        late = second
        if chained:
            late, along_x[1] = lax.optimization_barrier((second, along_x[1]))
        along_y = {s: shift_y(late if s == ys - 1 else second, s) for s in range(1, ys)}
        return lax.optimization_barrier(
            (
                [first] + [along_x[s] for s in range(1, XS)],
                [second] + [along_y[s] for s in range(1, ys)],
            )
        )

    def in_line(pieces):
        line = jnp.zeros((XS, rows_dev, flat_width), queries.dtype)
        for s, piece in enumerate(pieces):
            line = lax.dynamic_update_slice(line, piece[None], ((own_x - s) % XS, 0, 0))
        return line

    def both_lines(line, other):
        first = jnp.where(own_core == 0, line, other)
        second = jnp.where(own_core == 0, other, line)
        return jnp.stack([first, second], axis=1).reshape(block_rows, flat_width)

    q_pieces, k_pieces = wave(*lax.optimization_barrier((masked(queries), masked(keys))), True)
    q_line = in_line(q_pieces)
    q_other, keep_flat = lax.optimization_barrier((swap_core(q_line), keep_flat))
    q_blk = both_lines(q_line, q_other)
    k_blk = jnp.concatenate(k_pieces, axis=0)
    logit_piece = dot_f32(q_blk, k_blk, ROW_PAIR)
    g_pieces, v_pieces = wave(masked(out_grad), masked(values), False)
    v_blk = jnp.concatenate(v_pieces, axis=0)
    g_line = in_line(g_pieces)
    g_blk = both_lines(g_line, swap_core(g_line))
    g_blk, _ = lax.optimization_barrier((g_blk, logit_piece))
    dprob_piece = dot_f32(g_blk, v_blk, ROW_PAIR).astype(jnp.bfloat16)
    logit_sum = lax.psum_scatter(logit_piece, "col", scatter_dimension=0, tiled=True)

    dprob_chunks = dprob_piece.reshape(zs, block_rows // zs, block_keys)

    def part(step):
        return lax.dynamic_index_in_dim(dprob_chunks, (own_z + step) % zs, axis=0, keepdims=False)

    def onward(moving, step, left):
        if left > 0:
            moving = (
                moving.astype(jnp.float32) + part(step * left).astype(jnp.float32)
            ).astype(jnp.bfloat16)
        return moving

    def passed(moving, step, left):
        while left > 0:
            left -= 1
            moving = onward(shift_z(moving, step), step, left)
        return moving

    ahead, behind = zs // 2, zs - 1 - zs // 2
    dprob_forward = onward(shift_z(part(ahead), 1), 1, ahead - 1)
    own_flags, dprob_forward = lax.optimization_barrier(
        (row_keep.astype(jnp.float32)[None, :], dprob_forward)
    )
    key_flags = jnp.concatenate(
        [own_flags] + [shift_y(own_flags, s) for s in range(1, ys)], axis=1
    )
    dprob_forward, key_flags = lax.optimization_barrier((shift_z(dprob_forward, 1), key_flags))
    dprob_forward = passed(onward(dprob_forward, 1, ahead - 2), 1, ahead - 2)
    dprob_back = passed(part(-behind), -1, behind)

    both, stats = block_softmax(
        logit_scale, logit_sum, part(0), dprob_forward, dprob_back, key_flags
    )
    both = lax.all_gather(both, "col", axis=0, tiled=True)

    sums, own_stats = cross_statistics(
        q_blk, g_blk, k_blk, v_blk, stats, tokens, feature, inv_root
    )
    all_stats = share(own_stats, "row", near)
    row_stats = all_stats[:, 3 * cols_dev, : 3 * rows_dev].reshape(near_size, 3, rows_dev)
    peak = jnp.max(row_stats[:, 0], axis=0)
    weight = jnp.exp(row_stats[:, 0] - peak)
    total = jnp.sum(weight * row_stats[:, 1], axis=0)
    delta = jnp.sum(weight * row_stats[:, 2], axis=0) / total
    scaling = share(jnp.stack([jnp.exp(stats[0] - peak) / total, delta - stats[3]]), "col")
    cross_dl, dsum = cross_grads(q_blk, g_blk, sums, all_stats, feature, inv_root)
    both, scaling, cross_dl, dsum = lax.optimization_barrier((both, scaling, cross_dl, dsum))

    prob, dlogit, dq_own, dq_other = query_grads(
        logit_scale, place, both, scaling, k_blk, cross_dl, sums, zs
    )
    dq_swapped = swap_core(dq_other)
    key_parts = key_grads(prob, dlogit, q_blk, g_blk, dsum, ys)
    key_moved = [shift_y(key_parts[s], -s) for s in range(1, ys)]
    line = (dq_own + dq_swapped.astype(jnp.float32)).astype(jnp.bfloat16)
    line = line.reshape(XS, rows_dev, flat_width)
    lines = [[at(y, x, c) for x in range(XS)] for y in range(ys) for c in range(2)]
    line = lax.all_to_all(
        line, "row", split_axis=0, concat_axis=0, tiled=True, axis_index_groups=lines
    )

    def added(parts):
        return sum(p.astype(jnp.float32) for p in parts)

    grad_q = added([line[x] for x in range(XS)])
    grad_kv = added([key_parts[0]] + key_moved)

    def finished(rows):
        return (
            jnp.where(keep_flat, rows, 0.0)
            .astype(jnp.bfloat16)
            .reshape(rows_dev, cols_dev, feature)
        )

    return (
        finished(grad_q),
        finished(grad_kv[:, :flat_width]),
        finished(grad_kv[:, flat_width:]),
    )


def solution(mesh):
    return jax.shard_map(
        shards,
        mesh=mesh,
        in_specs=(
            P("row", "col", None),
            P("row", "col", None),
            P("row", "col", None),
            P("row", "col", None),
            P("row"),
            P("row"),
        ),
        out_specs=(P("row", "col", None), P("row", "col", None), P("row", "col", None)),
        check_vma=False,
    )
```

```python
import math

import jax
import jax.numpy as jnp
from jax import lax
from jax.experimental import pallas as pl
from jax.experimental.layout import Layout, with_layout_constraint
from jax.experimental.pallas import tpu as pltpu
from jax.sharding import PartitionSpec as P

SUMMARIES = 256
XS = 4
FLAG_ROWS = 16

ROW_PAIR = (((1,), (1,)), ((), ()))
LEAD_PAIR = (((0,), (0,)), ((), ()))
PLAIN = (((1,), (0,)), ((), ()))

WHOLE = pl.BlockSpec()
SMEM = pl.BlockSpec(memory_space=pltpu.SMEM)
ROOM = pltpu.CompilerParams(vmem_limit_bytes=24 * 1024 * 1024)


def dot_f32(left, right, dims=PLAIN):
    return lax.dot_general(left, right, dims, preferred_element_type=jnp.float32)


def diagonal(n):
    return lax.broadcasted_iota(jnp.int32, (n, n), 0) == lax.broadcasted_iota(jnp.int32, (n, n), 1)


def across(column):
    return jnp.sum(jnp.where(diagonal(column.shape[0]), column, 0.0), axis=0, keepdims=True)


def upright(row):
    return jnp.sum(jnp.where(diagonal(row.shape[1]), row, 0.0), axis=1, keepdims=True)


def cross_scores(sums_ref, q_ref, g_ref, column, feature, inv_root):
    flat_width = q_ref.shape[1]
    lanes = slice(column * feature, (column + 1) * feature)
    other = slice(flat_width + column * feature, flat_width + (column + 1) * feature)
    scores = dot_f32(sums_ref[:, lanes], q_ref[:, lanes], ROW_PAIR) * inv_root
    dprob = dot_f32(sums_ref[:, other], g_ref[:, lanes], ROW_PAIR)
    return scores, dprob, lanes, other


def cross_statistics(q_blk, g_blk, k_blk, v_blk, row_stats, tokens, feature, inv_root):
    block_keys, flat_width = k_blk.shape
    both_width = 2 * flat_width
    block_rows = q_blk.shape[0]
    group = block_keys // tokens
    columns = both_width // (2 * feature)
    stat_rows = -(-(3 * columns + 1) // 8) * 8
    kinds, rows = 3, row_stats.shape[1]

    def kernel(q_ref, g_ref, k_ref, v_ref, row_ref, sums_ref, stat_ref):
        for half, table_ref in enumerate((k_ref, v_ref)):
            pooled = jnp.sum(
                table_ref[...].astype(jnp.float32).reshape(tokens, group, flat_width), axis=1
            )
            sums_ref[:, half * flat_width : (half + 1) * flat_width] = (pooled / group).astype(
                jnp.bfloat16
            )
        for c in range(columns):
            scores, dprob, _, _ = cross_scores(sums_ref, q_ref, g_ref, c, feature, inv_root)
            peak = jnp.max(scores, axis=0, keepdims=True)
            lifted = jnp.exp(scores - peak)
            stat_ref[c : c + 1, :] = peak
            stat_ref[columns + c : columns + c + 1, :] = jnp.sum(lifted, axis=0, keepdims=True)
            stat_ref[2 * columns + c : 2 * columns + c + 1, :] = jnp.sum(
                lifted * dprob, axis=0, keepdims=True
            )
        stat_ref[3 * columns :, :] = jnp.zeros((stat_rows - 3 * columns, block_rows), jnp.float32)
        for i in range(kinds):
            stat_ref[3 * columns : 3 * columns + 1, i * rows : (i + 1) * rows] = row_ref[
                i : i + 1, :
            ]

    return pl.pallas_call(
        kernel,
        out_shape=(
            jax.ShapeDtypeStruct((tokens, both_width), jnp.bfloat16),
            jax.ShapeDtypeStruct((stat_rows, block_rows), jnp.float32),
        ),
        compiler_params=ROOM,
        name="cross_statistics",
    )(q_blk, g_blk, k_blk, v_blk, row_stats)


def cross_grads(q_blk, g_blk, sums, all_stats, feature, inv_root):
    tokens, both_width = sums.shape
    block_rows = q_blk.shape[0]
    columns = both_width // (2 * feature)

    def kernel(q_ref, g_ref, sums_ref, stat_ref, dl_ref, dsum_ref):
        peaks = stat_ref[:, :columns, :]
        peak = jnp.max(peaks, axis=0)
        weight = jnp.exp(peaks - peak[None])
        total = jnp.sum(weight * stat_ref[:, columns : 2 * columns, :], axis=0)
        delta = jnp.sum(weight * stat_ref[:, 2 * columns : 3 * columns, :], axis=0) / total
        for c in range(columns):
            scores, dprob, lanes, other = cross_scores(sums_ref, q_ref, g_ref, c, feature, inv_root)
            probs = jnp.exp(scores - peak[c : c + 1, :]) / total[c : c + 1, :]
            dl = (inv_root * probs * (dprob - delta[c : c + 1, :])).astype(jnp.bfloat16)
            dl_ref[c * tokens : (c + 1) * tokens, :] = dl
            dsum_ref[:, lanes] = dot_f32(dl, q_ref[:, lanes])
            dsum_ref[:, other] = dot_f32(probs.astype(jnp.bfloat16), g_ref[:, lanes])

    return pl.pallas_call(
        kernel,
        out_shape=(
            jax.ShapeDtypeStruct((columns * tokens, block_rows), jnp.bfloat16),
            jax.ShapeDtypeStruct((tokens, both_width), jnp.float32),
        ),
        compiler_params=ROOM,
        name="cross_grads",
    )(q_blk, g_blk, sums, all_stats)


def block_softmax(logit_scale, logit_sum, own, forward, back, key_flags):
    rows, width = logit_sum.shape

    def kernel(
        logit_ref, own_ref, forward_ref, back_ref, flag_ref, both_ref, stat_ref, held_ref, sem
    ):
        copy = pltpu.make_async_copy(logit_ref, held_ref, sem)
        copy.start()
        dprob = (
            own_ref[...].astype(jnp.float32)
            + forward_ref[...].astype(jnp.float32)
            + back_ref[...].astype(jnp.float32)
        )
        copy.wait()
        logits = jnp.where(flag_ref[...] > 0, held_ref[...] * logit_scale, -1e30)
        peak = jnp.max(logits, axis=1, keepdims=True)
        lifted = jnp.exp(logits - peak)
        total = jnp.sum(lifted, axis=1, keepdims=True)
        weighted = jnp.sum(lifted * dprob, axis=1, keepdims=True)
        delta = weighted / total
        both_ref[:, :width] = lifted.astype(jnp.bfloat16)
        both_ref[:, width:] = (lifted * (dprob - delta)).astype(jnp.bfloat16)
        for i, column in enumerate((peak, total, weighted, delta)):
            stat_ref[i : i + 1, :] = across(column)
        stat_ref[4:8, :] = jnp.zeros((4, rows), jnp.float32)

    return pl.pallas_call(
        kernel,
        out_shape=(
            jax.ShapeDtypeStruct((rows, 2 * width), jnp.bfloat16),
            jax.ShapeDtypeStruct((8, rows), jnp.float32),
        ),
        in_specs=[pl.BlockSpec(memory_space=pltpu.HBM)] + [WHOLE] * 4,
        scratch_shapes=[pltpu.VMEM((rows, width), jnp.float32), pltpu.SemaphoreType.DMA],
        compiler_params=ROOM,
        name="block_softmax",
    )(
        pltpu.with_memory_space_constraint(logit_sum, pltpu.HBM), own, forward, back, key_flags
    )


def query_grads(logit_scale, place, both, scaling, k_blk, cross_dl, sums, chunks):
    block_rows, width = both.shape[0], both.shape[1] // 2
    rows = block_rows // chunks
    flat_width = k_blk.shape[1]
    tokens = sums.shape[0]
    columns = cross_dl.shape[0] // tokens
    feature = flat_width // columns

    def kernel(place_ref, both_ref, scale_ref, k_ref, dl_ref, sums_ref, p_ref, ds_ref, own_ref, other_ref, dq_ref, held_ref, sems):
        core = place_ref[0]
        copies = []
        for i in range(chunks):
            at = pl.ds(i * rows, rows)
            copies.append(pltpu.make_async_copy(both_ref.at[at], held_ref.at[at], sems.at[i]))
            copies[i].start()
        for i in range(chunks):
            at = slice(i * rows, (i + 1) * rows)
            copies[i].wait()
            weight, offset = upright(scale_ref[i, 0:1, :]), upright(scale_ref[i, 1:2, :])
            lifted = held_ref[at, :width].astype(jnp.float32)
            tilted = held_ref[at, width:].astype(jnp.float32)
            p_ref[at, :] = (lifted * weight).astype(jnp.bfloat16)
            ds_ref[at, :] = ((tilted - lifted * offset) * (weight * logit_scale)).astype(
                jnp.bfloat16
            )
        dq_ref[...] = dot_f32(ds_ref[...], k_ref[...])
        for c in range(columns):
            lanes = slice(c * feature, (c + 1) * feature)
            dq_ref[:, lanes] += dot_f32(
                dl_ref[c * tokens : (c + 1) * tokens, :], sums_ref[:, lanes], LEAD_PAIR
            )
        for x in range(chunks // 2):
            to = slice(x * rows, (x + 1) * rows)
            mine = pl.multiple_of((2 * x + core) * rows, rows)
            theirs = pl.multiple_of((2 * x + 1 - core) * rows, rows)
            own_ref[to, :] = dq_ref[pl.ds(mine, rows), :]
            other_ref[to, :] = dq_ref[pl.ds(theirs, rows), :].astype(jnp.bfloat16)

    return pl.pallas_call(
        kernel,
        in_specs=[SMEM, pl.BlockSpec(memory_space=pltpu.HBM)] + [WHOLE] * 4,
        out_shape=(
            jax.ShapeDtypeStruct((block_rows, width), jnp.bfloat16),
            jax.ShapeDtypeStruct((block_rows, width), jnp.bfloat16),
            jax.ShapeDtypeStruct((block_rows // 2, flat_width), jnp.float32),
            jax.ShapeDtypeStruct((block_rows // 2, flat_width), jnp.bfloat16),
        ),
        scratch_shapes=[
            pltpu.VMEM((block_rows, flat_width), jnp.float32),
            pltpu.VMEM((block_rows, 2 * width), jnp.bfloat16),
            pltpu.SemaphoreType.DMA((chunks,)),
        ],
        compiler_params=ROOM,
        name="query_grads",
    )(place, pltpu.with_memory_space_constraint(both, pltpu.HBM), scaling, k_blk, cross_dl, sums)


def key_grads(prob, dlogit, q_blk, g_blk, dsum, pieces):
    width, flat_width = prob.shape[1], q_blk.shape[1]
    tokens = dsum.shape[0]
    group = width // tokens
    piece = width // pieces

    def kernel(p_ref, ds_ref, q_ref, g_ref, dsum_ref, *out_refs):
        for half, (w_ref, t_ref) in enumerate(((ds_ref, q_ref), (p_ref, g_ref))):
            lanes = slice(half * flat_width, (half + 1) * flat_width)
            grads = dot_f32(w_ref[...], t_ref[...], LEAD_PAIR)
            shared = dsum_ref[:, lanes] / group
            grads = grads.reshape(tokens, group, flat_width) + shared[:, None, :]
            grads = grads.reshape(width, flat_width).astype(jnp.bfloat16)
            for s, out_ref in enumerate(out_refs):
                out_ref[:, lanes] = grads[s * piece : (s + 1) * piece]

    return pl.pallas_call(
        kernel,
        out_shape=tuple(
            jax.ShapeDtypeStruct((piece, 2 * flat_width), jnp.bfloat16) for _ in range(pieces)
        ),
        compiler_params=ROOM,
        name="key_grads",
    )(prob, dlogit, q_blk, g_blk, dsum)


def shards(queries, keys, values, out_grad, row_keep, row_lengths):
    rows_dev, cols_dev, feature = queries.shape
    row_axis, zs = lax.axis_size("row"), lax.axis_size("col")
    ys = row_axis // (2 * XS)
    near_size = 2 * XS
    total_rows = rows_dev * row_axis
    total_cols = cols_dev * zs
    group_rows = total_rows // SUMMARIES
    flat_width = cols_dev * feature
    block_rows = near_size * rows_dev
    block_keys = ys * rows_dev
    tokens = block_keys // group_rows
    near = [[y * near_size + i for i in range(near_size)] for y in range(ys)]
    own_x = (lax.axis_index("row") // 2) % XS
    own_core = lax.axis_index("row") % 2
    own_z = lax.axis_index("col")
    place = jnp.stack([own_core, own_z]).astype(jnp.int32)
    logit_scale = 1.0 / math.sqrt(total_cols * feature)
    inv_root = 1.0 / math.sqrt(feature)

    def at(y, x, core):
        return ((y % ys) * XS + x % XS) * 2 + core

    cells = [(y, x, c) for y in range(ys) for x in range(XS) for c in range(2)]

    def shift_y(table, step):
        return lax.ppermute(table, "row", [(at(y, x, c), at(y + step, x, c)) for y, x, c in cells])

    def shift_x(table, step):
        return lax.ppermute(table, "row", [(at(y, x, c), at(y, x + step, c)) for y, x, c in cells])

    def swap_core(table):
        return lax.ppermute(table, "row", [(at(y, x, c), at(y, x, 1 - c)) for y, x, c in cells])

    def shift_z(table, step):
        return lax.ppermute(table, "col", [(z, (z + step) % zs) for z in range(zs)])

    def share(table, axis, groups=None):
        count = lax.axis_size(axis) if groups is None else len(groups[0])
        copies = jnp.broadcast_to(table[None], (count,) + table.shape)
        return lax.all_to_all(
            copies, axis, split_axis=0, concat_axis=0, tiled=True, axis_index_groups=groups
        )

    own_columns = jnp.where(row_keep == 1, row_lengths, 0) - own_z * cols_dev
    cell_keep = jnp.arange(cols_dev, dtype=jnp.int32)[None, :] < own_columns[:, None]
    keep_flat = jnp.broadcast_to(cell_keep[:, :, None], queries.shape).reshape(
        rows_dev, flat_width
    )
    zero = jnp.zeros((), queries.dtype)

    def masked(table):
        flat = jnp.where(keep_flat, table.reshape(rows_dev, flat_width), zero)
        return with_layout_constraint(flat, Layout((0, 1)))

    def wave(first, second, chained):
        along_x = {s: shift_x(first, s) for s in range(1, XS)}
        late = second
        if chained:
            late, along_x[1] = lax.optimization_barrier((second, along_x[1]))
        along_y = {s: shift_y(late if s == ys - 1 else second, s) for s in range(1, ys)}
        return lax.optimization_barrier(
            (
                [first] + [along_x[s] for s in range(1, XS)],
                [second] + [along_y[s] for s in range(1, ys)],
            )
        )

    def in_line(pieces):
        line = jnp.zeros((XS, rows_dev, flat_width), queries.dtype)
        for s, piece in enumerate(pieces):
            line = lax.dynamic_update_slice(line, piece[None], ((own_x - s) % XS, 0, 0))
        return line

    def both_lines(line, other):
        first = jnp.where(own_core == 0, line, other)
        second = jnp.where(own_core == 0, other, line)
        return jnp.stack([first, second], axis=1).reshape(block_rows, flat_width)

    q_pieces, k_pieces = wave(*lax.optimization_barrier((masked(queries), masked(keys))), True)
    q_line = in_line(q_pieces)
    q_other, keep_flat = lax.optimization_barrier((swap_core(q_line), keep_flat))
    q_blk = both_lines(q_line, q_other)
    k_blk = jnp.concatenate(k_pieces, axis=0)
    logit_piece = dot_f32(q_blk, k_blk, ROW_PAIR)
    flag_rows = jnp.pad(
        row_keep.astype(jnp.bfloat16)[None, :], ((0, FLAG_ROWS - 1), (0, flat_width - rows_dev))
    )
    g_pieces, key_pieces = wave(
        masked(out_grad), jnp.concatenate([masked(values), flag_rows], axis=0), False
    )
    v_blk = jnp.concatenate([p[:rows_dev] for p in key_pieces], axis=0)
    g_line = in_line(g_pieces)
    g_blk = both_lines(g_line, swap_core(g_line))
    g_blk, _ = lax.optimization_barrier((g_blk, logit_piece))
    dprob_piece = dot_f32(g_blk, v_blk, ROW_PAIR).astype(jnp.bfloat16)
    key_flags = jnp.concatenate([p[rows_dev, :rows_dev] for p in key_pieces])[None, :]
    logit_sum = lax.psum_scatter(logit_piece, "col", scatter_dimension=0, tiled=True)

    dprob_chunks = dprob_piece.reshape(zs, block_rows // zs, block_keys)

    def part(step):
        return lax.dynamic_index_in_dim(dprob_chunks, (own_z + step) % zs, axis=0, keepdims=False)

    def passed(step, count):
        moving = part(step * count)
        for left in range(count - 1, -1, -1):
            moving = shift_z(moving, step)
            if left > 0:
                moving = (
                    moving.astype(jnp.float32) + part(step * left).astype(jnp.float32)
                ).astype(jnp.bfloat16)
        return moving

    dprob_forward = passed(1, zs // 2)
    dprob_back = passed(-1, zs - 1 - zs // 2)

    both, stats = block_softmax(
        logit_scale, logit_sum, part(0), dprob_forward, dprob_back, key_flags
    )
    both = lax.all_gather(both, "col", axis=0, tiled=True)

    sums, own_stats = cross_statistics(
        q_blk, g_blk, k_blk, v_blk, stats, tokens, feature, inv_root
    )
    all_stats = share(own_stats, "row", near)
    row_stats = all_stats[:, 3 * cols_dev, : 3 * rows_dev].reshape(near_size, 3, rows_dev)
    peak = jnp.max(row_stats[:, 0], axis=0)
    weight = jnp.exp(row_stats[:, 0] - peak)
    total = jnp.sum(weight * row_stats[:, 1], axis=0)
    delta = jnp.sum(weight * row_stats[:, 2], axis=0) / total
    scaling = share(jnp.stack([jnp.exp(stats[0] - peak) / total, delta - stats[3]]), "col")
    cross_dl, dsum = cross_grads(q_blk, g_blk, sums, all_stats, feature, inv_root)
    both, scaling, cross_dl, dsum = lax.optimization_barrier((both, scaling, cross_dl, dsum))

    prob, dlogit, dq_own, dq_other = query_grads(
        logit_scale, place, both, scaling, k_blk, cross_dl, sums, zs
    )
    dq_swapped = swap_core(dq_other)
    key_parts = key_grads(prob, dlogit, q_blk, g_blk, dsum, ys)
    key_moved = [shift_y(key_parts[s], -s) for s in range(1, ys)]
    line = (dq_own + dq_swapped.astype(jnp.float32)).astype(jnp.bfloat16)
    line = line.reshape(XS, rows_dev, flat_width)
    lines = [[at(y, x, c) for x in range(XS)] for y in range(ys) for c in range(2)]
    line = lax.all_to_all(
        line, "row", split_axis=0, concat_axis=0, tiled=True, axis_index_groups=lines
    )

    def added(parts):
        return sum(p.astype(jnp.float32) for p in parts)

    grad_q = added([line[x] for x in range(XS)])
    def finished(rows):
        return (
            jnp.where(keep_flat, rows, 0.0)
            .astype(jnp.bfloat16)
            .reshape(rows_dev, cols_dev, feature)
        )

    grad_q = finished(grad_q)
    grad_kv = added([key_parts[0]] + key_moved)
    return (grad_q, finished(grad_kv[:, :flat_width]), finished(grad_kv[:, flat_width:]))


def solution(mesh):
    return jax.shard_map(
        shards,
        mesh=mesh,
        in_specs=(
            P("row", "col", None),
            P("row", "col", None),
            P("row", "col", None),
            P("row", "col", None),
            P("row"),
            P("row"),
        ),
        out_specs=(P("row", "col", None), P("row", "col", None), P("row", "col", None)),
        check_vma=False,
    )
```

```python
import math

import jax
import jax.numpy as jnp
from jax import lax
from jax.experimental import pallas as pl
from jax.experimental.layout import Layout, with_layout_constraint
from jax.experimental.pallas import tpu as pltpu
from jax.sharding import PartitionSpec as P

SUMMARIES = 256
XS = 4
FLAG_ROWS = 16

ROW_PAIR = (((1,), (1,)), ((), ()))
LEAD_PAIR = (((0,), (0,)), ((), ()))
PLAIN = (((1,), (0,)), ((), ()))

WHOLE = pl.BlockSpec()
SMEM = pl.BlockSpec(memory_space=pltpu.SMEM)
ROOM = pltpu.CompilerParams(vmem_limit_bytes=24 * 1024 * 1024)


def dot_f32(left, right, dims=PLAIN):
    return lax.dot_general(left, right, dims, preferred_element_type=jnp.float32)


def diagonal(n):
    return lax.broadcasted_iota(jnp.int32, (n, n), 0) == lax.broadcasted_iota(jnp.int32, (n, n), 1)


def across(column):
    return jnp.sum(jnp.where(diagonal(column.shape[0]), column, 0.0), axis=0, keepdims=True)


def upright(row):
    return jnp.sum(jnp.where(diagonal(row.shape[1]), row, 0.0), axis=1, keepdims=True)


def cross_scores(sums_ref, q_ref, g_ref, column, feature, inv_root):
    flat_width = q_ref.shape[1]
    lanes = slice(column * feature, (column + 1) * feature)
    other = slice(flat_width + column * feature, flat_width + (column + 1) * feature)
    scores = dot_f32(sums_ref[:, lanes], q_ref[:, lanes], ROW_PAIR) * inv_root
    dprob = dot_f32(sums_ref[:, other], g_ref[:, lanes], ROW_PAIR)
    return scores, dprob, lanes, other


def cross_statistics(q_blk, g_blk, k_blk, v_blk, row_stats, tokens, feature, inv_root):
    block_keys, flat_width = k_blk.shape
    both_width = 2 * flat_width
    block_rows = q_blk.shape[0]
    group = block_keys // tokens
    columns = both_width // (2 * feature)
    stat_rows = -(-(3 * columns + 1) // 8) * 8
    kinds, rows = 3, row_stats.shape[1]

    def kernel(q_ref, g_ref, k_ref, v_ref, row_ref, sums_ref, stat_ref):
        for half, table_ref in enumerate((k_ref, v_ref)):
            pooled = jnp.sum(
                table_ref[...].astype(jnp.float32).reshape(tokens, group, flat_width), axis=1
            )
            sums_ref[:, half * flat_width : (half + 1) * flat_width] = (pooled / group).astype(
                jnp.bfloat16
            )
        for c in range(columns):
            scores, dprob, _, _ = cross_scores(sums_ref, q_ref, g_ref, c, feature, inv_root)
            peak = jnp.max(scores, axis=0, keepdims=True)
            lifted = jnp.exp(scores - peak)
            stat_ref[c : c + 1, :] = peak
            stat_ref[columns + c : columns + c + 1, :] = jnp.sum(lifted, axis=0, keepdims=True)
            stat_ref[2 * columns + c : 2 * columns + c + 1, :] = jnp.sum(
                lifted * dprob, axis=0, keepdims=True
            )
        stat_ref[3 * columns :, :] = jnp.zeros((stat_rows - 3 * columns, block_rows), jnp.float32)
        for i in range(kinds):
            stat_ref[3 * columns : 3 * columns + 1, i * rows : (i + 1) * rows] = row_ref[
                i : i + 1, :
            ]

    return pl.pallas_call(
        kernel,
        out_shape=(
            jax.ShapeDtypeStruct((tokens, both_width), jnp.bfloat16),
            jax.ShapeDtypeStruct((stat_rows, block_rows), jnp.float32),
        ),
        compiler_params=ROOM,
        name="cross_statistics",
    )(q_blk, g_blk, k_blk, v_blk, row_stats)


def cross_grads(q_blk, g_blk, sums, all_stats, feature, inv_root):
    tokens, both_width = sums.shape
    block_rows = q_blk.shape[0]
    columns = both_width // (2 * feature)

    def kernel(q_ref, g_ref, sums_ref, stat_ref, dl_ref, dsum_ref):
        peaks = stat_ref[:, :columns, :]
        peak = jnp.max(peaks, axis=0)
        weight = jnp.exp(peaks - peak[None])
        total = jnp.sum(weight * stat_ref[:, columns : 2 * columns, :], axis=0)
        delta = jnp.sum(weight * stat_ref[:, 2 * columns : 3 * columns, :], axis=0) / total
        for c in range(columns):
            scores, dprob, lanes, other = cross_scores(sums_ref, q_ref, g_ref, c, feature, inv_root)
            probs = jnp.exp(scores - peak[c : c + 1, :]) / total[c : c + 1, :]
            dl = (inv_root * probs * (dprob - delta[c : c + 1, :])).astype(jnp.bfloat16)
            dl_ref[c * tokens : (c + 1) * tokens, :] = dl
            dsum_ref[:, lanes] = dot_f32(dl, q_ref[:, lanes])
            dsum_ref[:, other] = dot_f32(probs.astype(jnp.bfloat16), g_ref[:, lanes])

    return pl.pallas_call(
        kernel,
        out_shape=(
            jax.ShapeDtypeStruct((columns * tokens, block_rows), jnp.bfloat16),
            jax.ShapeDtypeStruct((tokens, both_width), jnp.float32),
        ),
        compiler_params=ROOM,
        name="cross_grads",
    )(q_blk, g_blk, sums, all_stats)


def block_softmax(logit_scale, logit_sum, own, forward, back, key_flags):
    rows, width = logit_sum.shape

    def kernel(
        logit_ref, own_ref, forward_ref, back_ref, flag_ref, both_ref, stat_ref, held_ref, sem
    ):
        copy = pltpu.make_async_copy(logit_ref, held_ref, sem)
        copy.start()
        dprob = (
            own_ref[...].astype(jnp.float32)
            + forward_ref[...].astype(jnp.float32)
            + back_ref[...].astype(jnp.float32)
        )
        copy.wait()
        logits = jnp.where(flag_ref[...] > 0, held_ref[...] * logit_scale, -1e30)
        peak = jnp.max(logits, axis=1, keepdims=True)
        lifted = jnp.exp(logits - peak)
        total = jnp.sum(lifted, axis=1, keepdims=True)
        weighted = jnp.sum(lifted * dprob, axis=1, keepdims=True)
        delta = weighted / total
        both_ref[:, :width] = lifted.astype(jnp.bfloat16)
        both_ref[:, width:] = (lifted * (dprob - delta)).astype(jnp.bfloat16)
        for i, column in enumerate((peak, total, weighted, delta)):
            stat_ref[i : i + 1, :] = across(column)
        stat_ref[4:8, :] = jnp.zeros((4, rows), jnp.float32)

    return pl.pallas_call(
        kernel,
        out_shape=(
            jax.ShapeDtypeStruct((rows, 2 * width), jnp.bfloat16),
            jax.ShapeDtypeStruct((8, rows), jnp.float32),
        ),
        in_specs=[pl.BlockSpec(memory_space=pltpu.HBM)] + [WHOLE] * 4,
        scratch_shapes=[pltpu.VMEM((rows, width), jnp.float32), pltpu.SemaphoreType.DMA],
        compiler_params=ROOM,
        name="block_softmax",
    )(
        pltpu.with_memory_space_constraint(logit_sum, pltpu.HBM), own, forward, back, key_flags
    )


def query_grads(logit_scale, place, both, scaling, k_blk, cross_dl, sums, chunks):
    block_rows, width = both.shape[0], both.shape[1] // 2
    rows = block_rows // chunks
    flat_width = k_blk.shape[1]
    tokens = sums.shape[0]
    columns = cross_dl.shape[0] // tokens
    feature = flat_width // columns

    def kernel(place_ref, both_ref, scale_ref, k_ref, dl_ref, sums_ref, p_ref, ds_ref, own_ref, other_ref, dq_ref, held_ref, sems):
        core = place_ref[0]
        copies = []
        for i in range(chunks):
            at = pl.ds(i * rows, rows)
            copies.append(pltpu.make_async_copy(both_ref.at[at], held_ref.at[at], sems.at[i]))
            copies[i].start()
        for i in range(chunks):
            at = slice(i * rows, (i + 1) * rows)
            copies[i].wait()
            weight, offset = upright(scale_ref[i, 0:1, :]), upright(scale_ref[i, 1:2, :])
            lifted = held_ref[at, :width].astype(jnp.float32)
            tilted = held_ref[at, width:].astype(jnp.float32)
            p_ref[at, :] = (lifted * weight).astype(jnp.bfloat16)
            ds_ref[at, :] = ((tilted - lifted * offset) * (weight * logit_scale)).astype(
                jnp.bfloat16
            )
        dq_ref[...] = dot_f32(ds_ref[...], k_ref[...])
        for c in range(columns):
            lanes = slice(c * feature, (c + 1) * feature)
            dq_ref[:, lanes] += dot_f32(
                dl_ref[c * tokens : (c + 1) * tokens, :], sums_ref[:, lanes], LEAD_PAIR
            )
        for x in range(chunks // 2):
            to = slice(x * rows, (x + 1) * rows)
            mine = pl.multiple_of((2 * x + core) * rows, rows)
            theirs = pl.multiple_of((2 * x + 1 - core) * rows, rows)
            own_ref[to, :] = dq_ref[pl.ds(mine, rows), :]
            other_ref[to, :] = dq_ref[pl.ds(theirs, rows), :].astype(jnp.bfloat16)

    return pl.pallas_call(
        kernel,
        in_specs=[SMEM, pl.BlockSpec(memory_space=pltpu.HBM)] + [WHOLE] * 4,
        out_shape=(
            jax.ShapeDtypeStruct((block_rows, width), jnp.bfloat16),
            jax.ShapeDtypeStruct((block_rows, width), jnp.bfloat16),
            jax.ShapeDtypeStruct((block_rows // 2, flat_width), jnp.float32),
            jax.ShapeDtypeStruct((block_rows // 2, flat_width), jnp.bfloat16),
        ),
        scratch_shapes=[
            pltpu.VMEM((block_rows, flat_width), jnp.float32),
            pltpu.VMEM((block_rows, 2 * width), jnp.bfloat16),
            pltpu.SemaphoreType.DMA((chunks,)),
        ],
        compiler_params=ROOM,
        name="query_grads",
    )(place, pltpu.with_memory_space_constraint(both, pltpu.HBM), scaling, k_blk, cross_dl, sums)


def key_grads(prob, dlogit, q_blk, g_blk, dsum, pieces):
    width, flat_width = prob.shape[1], q_blk.shape[1]
    tokens = dsum.shape[0]
    group = width // tokens
    piece = width // pieces

    def kernel(p_ref, ds_ref, q_ref, g_ref, dsum_ref, *out_refs):
        for half, (w_ref, t_ref) in enumerate(((ds_ref, q_ref), (p_ref, g_ref))):
            lanes = slice(half * flat_width, (half + 1) * flat_width)
            grads = dot_f32(w_ref[...], t_ref[...], LEAD_PAIR)
            shared = dsum_ref[:, lanes] / group
            grads = grads.reshape(tokens, group, flat_width) + shared[:, None, :]
            grads = grads.reshape(width, flat_width).astype(jnp.bfloat16)
            for s, out_ref in enumerate(out_refs):
                out_ref[:, lanes] = grads[s * piece : (s + 1) * piece]

    return pl.pallas_call(
        kernel,
        out_shape=tuple(
            jax.ShapeDtypeStruct((piece, 2 * flat_width), jnp.bfloat16) for _ in range(pieces)
        ),
        compiler_params=ROOM,
        name="key_grads",
    )(prob, dlogit, q_blk, g_blk, dsum)


def shards(queries, keys, values, out_grad, row_keep, row_lengths):
    rows_dev, cols_dev, feature = queries.shape
    row_axis, zs = lax.axis_size("row"), lax.axis_size("col")
    ys = row_axis // (2 * XS)
    near_size = 2 * XS
    total_rows = rows_dev * row_axis
    total_cols = cols_dev * zs
    group_rows = total_rows // SUMMARIES
    flat_width = cols_dev * feature
    block_rows = near_size * rows_dev
    block_keys = ys * rows_dev
    tokens = block_keys // group_rows
    near = [[y * near_size + i for i in range(near_size)] for y in range(ys)]
    own_x = (lax.axis_index("row") // 2) % XS
    own_core = lax.axis_index("row") % 2
    own_z = lax.axis_index("col")
    place = jnp.stack([own_core, own_z]).astype(jnp.int32)
    logit_scale = 1.0 / math.sqrt(total_cols * feature)
    inv_root = 1.0 / math.sqrt(feature)

    def at(y, x, core):
        return ((y % ys) * XS + x % XS) * 2 + core

    cells = [(y, x, c) for y in range(ys) for x in range(XS) for c in range(2)]

    def shift_y(table, step):
        return lax.ppermute(table, "row", [(at(y, x, c), at(y + step, x, c)) for y, x, c in cells])

    def shift_x(table, step):
        return lax.ppermute(table, "row", [(at(y, x, c), at(y, x + step, c)) for y, x, c in cells])

    def swap_core(table):
        return lax.ppermute(table, "row", [(at(y, x, c), at(y, x, 1 - c)) for y, x, c in cells])

    def shift_z(table, step):
        return lax.ppermute(table, "col", [(z, (z + step) % zs) for z in range(zs)])

    def share(table, axis, groups=None):
        count = lax.axis_size(axis) if groups is None else len(groups[0])
        copies = jnp.broadcast_to(table[None], (count,) + table.shape)
        return lax.all_to_all(
            copies, axis, split_axis=0, concat_axis=0, tiled=True, axis_index_groups=groups
        )

    own_columns = jnp.where(row_keep == 1, row_lengths, 0) - own_z * cols_dev
    cell_keep = jnp.arange(cols_dev, dtype=jnp.int32)[None, :] < own_columns[:, None]
    keep_flat = jnp.broadcast_to(cell_keep[:, :, None], queries.shape).reshape(
        rows_dev, flat_width
    )
    zero = jnp.zeros((), queries.dtype)

    def masked(table):
        flat = jnp.where(keep_flat, table.reshape(rows_dev, flat_width), zero)
        return with_layout_constraint(flat, Layout((0, 1)))

    def wave(first, second, chained):
        along_x = {s: shift_x(first, s) for s in range(1, XS)}
        late = second
        if chained:
            late, along_x[1] = lax.optimization_barrier((second, along_x[1]))
        along_y = {s: shift_y(late if s == ys - 1 else second, s) for s in range(1, ys)}
        return lax.optimization_barrier(
            (
                [first] + [along_x[s] for s in range(1, XS)],
                [second] + [along_y[s] for s in range(1, ys)],
            )
        )

    def in_line(pieces):
        line = jnp.zeros((XS, rows_dev, flat_width), queries.dtype)
        for s, piece in enumerate(pieces):
            line = lax.dynamic_update_slice(line, piece[None], ((own_x - s) % XS, 0, 0))
        return line

    def both_lines(line, other):
        first = jnp.where(own_core == 0, line, other)
        second = jnp.where(own_core == 0, other, line)
        return jnp.stack([first, second], axis=1).reshape(block_rows, flat_width)

    flag_rows = jnp.pad(
        row_keep.astype(jnp.bfloat16)[None, :], ((0, FLAG_ROWS - 1), (0, flat_width - rows_dev))
    )
    query_rows = jnp.concatenate([masked(queries), masked(out_grad)], axis=0)
    key_rows = jnp.concatenate([masked(keys), masked(values), flag_rows], axis=0)
    query_pieces, key_pieces = wave(*lax.optimization_barrier((query_rows, key_rows)), False)
    q_line = in_line([p[:rows_dev] for p in query_pieces])
    g_line = in_line([p[rows_dev:] for p in query_pieces])
    q_blk = both_lines(q_line, swap_core(q_line))
    k_blk = jnp.concatenate([p[:rows_dev] for p in key_pieces], axis=0)
    logit_piece = dot_f32(q_blk, k_blk, ROW_PAIR)
    v_blk = jnp.concatenate([p[rows_dev : 2 * rows_dev] for p in key_pieces], axis=0)
    g_blk = both_lines(g_line, swap_core(g_line))
    g_blk, _ = lax.optimization_barrier((g_blk, logit_piece))
    dprob_piece = dot_f32(g_blk, v_blk, ROW_PAIR).astype(jnp.bfloat16)
    key_flags = jnp.concatenate([p[2 * rows_dev, :rows_dev] for p in key_pieces])[None, :]
    logit_sum = lax.psum_scatter(logit_piece, "col", scatter_dimension=0, tiled=True)

    dprob_chunks = dprob_piece.reshape(zs, block_rows // zs, block_keys)

    def part(step):
        return lax.dynamic_index_in_dim(dprob_chunks, (own_z + step) % zs, axis=0, keepdims=False)

    def passed(step, count):
        moving = part(step * count)
        for left in range(count - 1, -1, -1):
            moving = shift_z(moving, step)
            if left > 0:
                moving = (
                    moving.astype(jnp.float32) + part(step * left).astype(jnp.float32)
                ).astype(jnp.bfloat16)
        return moving

    dprob_forward = passed(1, zs // 2)
    dprob_back = passed(-1, zs - 1 - zs // 2)

    both, stats = block_softmax(
        logit_scale, logit_sum, part(0), dprob_forward, dprob_back, key_flags
    )
    both = lax.all_gather(both, "col", axis=0, tiled=True)

    sums, own_stats = cross_statistics(
        q_blk, g_blk, k_blk, v_blk, stats, tokens, feature, inv_root
    )
    all_stats = share(own_stats, "row", near)
    row_stats = all_stats[:, 3 * cols_dev, : 3 * rows_dev].reshape(near_size, 3, rows_dev)
    peak = jnp.max(row_stats[:, 0], axis=0)
    weight = jnp.exp(row_stats[:, 0] - peak)
    total = jnp.sum(weight * row_stats[:, 1], axis=0)
    delta = jnp.sum(weight * row_stats[:, 2], axis=0) / total
    scaling = share(jnp.stack([jnp.exp(stats[0] - peak) / total, delta - stats[3]]), "col")
    cross_dl, dsum = cross_grads(q_blk, g_blk, sums, all_stats, feature, inv_root)
    both, scaling, cross_dl, dsum = lax.optimization_barrier((both, scaling, cross_dl, dsum))

    prob, dlogit, dq_own, dq_other = query_grads(
        logit_scale, place, both, scaling, k_blk, cross_dl, sums, zs
    )
    dq_swapped = swap_core(dq_other)
    key_parts = key_grads(prob, dlogit, q_blk, g_blk, dsum, ys)
    key_moved = [shift_y(key_parts[s], -s) for s in range(1, ys)]
    line = (dq_own + dq_swapped.astype(jnp.float32)).astype(jnp.bfloat16)
    line = line.reshape(XS, rows_dev, flat_width)
    lines = [[at(y, x, c) for x in range(XS)] for y in range(ys) for c in range(2)]
    line = lax.all_to_all(
        line, "row", split_axis=0, concat_axis=0, tiled=True, axis_index_groups=lines
    )

    def added(parts):
        return sum(p.astype(jnp.float32) for p in parts)

    grad_q = added([line[x] for x in range(XS)])
    def finished(rows):
        return (
            jnp.where(keep_flat, rows, 0.0)
            .astype(jnp.bfloat16)
            .reshape(rows_dev, cols_dev, feature)
        )

    grad_q = finished(grad_q)
    grad_kv = added([key_parts[0]] + key_moved)
    return (grad_q, finished(grad_kv[:, :flat_width]), finished(grad_kv[:, flat_width:]))


def solution(mesh):
    return jax.shard_map(
        shards,
        mesh=mesh,
        in_specs=(
            P("row", "col", None),
            P("row", "col", None),
            P("row", "col", None),
            P("row", "col", None),
            P("row"),
            P("row"),
        ),
        out_specs=(P("row", "col", None), P("row", "col", None), P("row", "col", None)),
        check_vma=False,
    )
```

```python
import math

import jax
import jax.numpy as jnp
from jax import lax
from jax.experimental import pallas as pl
from jax.experimental.layout import Layout, with_layout_constraint
from jax.experimental.pallas import tpu as pltpu
from jax.sharding import PartitionSpec as P

SUMMARIES = 256
XS = 4
FLAG_ROWS = 16

ROW_PAIR = (((1,), (1,)), ((), ()))
LEAD_PAIR = (((0,), (0,)), ((), ()))
PLAIN = (((1,), (0,)), ((), ()))

WHOLE = pl.BlockSpec()
SMEM = pl.BlockSpec(memory_space=pltpu.SMEM)
ROOM = pltpu.CompilerParams(vmem_limit_bytes=24 * 1024 * 1024)


def dot_f32(left, right, dims=PLAIN):
    return lax.dot_general(left, right, dims, preferred_element_type=jnp.float32)


def diagonal(n):
    return lax.broadcasted_iota(jnp.int32, (n, n), 0) == lax.broadcasted_iota(jnp.int32, (n, n), 1)


def across(column):
    return jnp.sum(jnp.where(diagonal(column.shape[0]), column, 0.0), axis=0, keepdims=True)


def upright(row):
    return jnp.sum(jnp.where(diagonal(row.shape[1]), row, 0.0), axis=1, keepdims=True)


def cross_scores(sums_ref, q_ref, g_ref, column, feature, inv_root):
    flat_width = q_ref.shape[1]
    lanes = slice(column * feature, (column + 1) * feature)
    other = slice(flat_width + column * feature, flat_width + (column + 1) * feature)
    scores = dot_f32(sums_ref[:, lanes], q_ref[:, lanes], ROW_PAIR) * inv_root
    dprob = dot_f32(sums_ref[:, other], g_ref[:, lanes], ROW_PAIR)
    return scores, dprob, lanes, other


def cross_statistics(q_blk, g_blk, k_blk, v_blk, row_stats, tokens, feature, inv_root):
    block_keys, flat_width = k_blk.shape
    both_width = 2 * flat_width
    block_rows = q_blk.shape[0]
    group = block_keys // tokens
    columns = both_width // (2 * feature)
    stat_rows = -(-(3 * columns + 1) // 8) * 8
    kinds, rows = 3, row_stats.shape[1]

    def kernel(q_ref, g_ref, k_ref, v_ref, row_ref, sums_ref, stat_ref):
        for half, table_ref in enumerate((k_ref, v_ref)):
            pooled = jnp.sum(
                table_ref[...].astype(jnp.float32).reshape(tokens, group, flat_width), axis=1
            )
            sums_ref[:, half * flat_width : (half + 1) * flat_width] = (pooled / group).astype(
                jnp.bfloat16
            )
        for c in range(columns):
            scores, dprob, _, _ = cross_scores(sums_ref, q_ref, g_ref, c, feature, inv_root)
            peak = jnp.max(scores, axis=0, keepdims=True)
            lifted = jnp.exp(scores - peak)
            stat_ref[c : c + 1, :] = peak
            stat_ref[columns + c : columns + c + 1, :] = jnp.sum(lifted, axis=0, keepdims=True)
            stat_ref[2 * columns + c : 2 * columns + c + 1, :] = jnp.sum(
                lifted * dprob, axis=0, keepdims=True
            )
        stat_ref[3 * columns :, :] = jnp.zeros((stat_rows - 3 * columns, block_rows), jnp.float32)
        for i in range(kinds):
            stat_ref[3 * columns : 3 * columns + 1, i * rows : (i + 1) * rows] = row_ref[
                i : i + 1, :
            ]

    return pl.pallas_call(
        kernel,
        out_shape=(
            jax.ShapeDtypeStruct((tokens, both_width), jnp.bfloat16),
            jax.ShapeDtypeStruct((stat_rows, block_rows), jnp.float32),
        ),
        compiler_params=ROOM,
        name="cross_statistics",
    )(q_blk, g_blk, k_blk, v_blk, row_stats)


def cross_grads(q_blk, g_blk, sums, all_stats, feature, inv_root):
    tokens, both_width = sums.shape
    block_rows = q_blk.shape[0]
    columns = both_width // (2 * feature)

    def kernel(q_ref, g_ref, sums_ref, stat_ref, dl_ref, dsum_ref):
        peaks = stat_ref[:, :columns, :]
        peak = jnp.max(peaks, axis=0)
        weight = jnp.exp(peaks - peak[None])
        total = jnp.sum(weight * stat_ref[:, columns : 2 * columns, :], axis=0)
        delta = jnp.sum(weight * stat_ref[:, 2 * columns : 3 * columns, :], axis=0) / total
        for c in range(columns):
            scores, dprob, lanes, other = cross_scores(sums_ref, q_ref, g_ref, c, feature, inv_root)
            probs = jnp.exp(scores - peak[c : c + 1, :]) / total[c : c + 1, :]
            dl = (inv_root * probs * (dprob - delta[c : c + 1, :])).astype(jnp.bfloat16)
            dl_ref[c * tokens : (c + 1) * tokens, :] = dl
            dsum_ref[:, lanes] = dot_f32(dl, q_ref[:, lanes])
            dsum_ref[:, other] = dot_f32(probs.astype(jnp.bfloat16), g_ref[:, lanes])

    return pl.pallas_call(
        kernel,
        out_shape=(
            jax.ShapeDtypeStruct((columns * tokens, block_rows), jnp.bfloat16),
            jax.ShapeDtypeStruct((tokens, both_width), jnp.float32),
        ),
        compiler_params=ROOM,
        name="cross_grads",
    )(q_blk, g_blk, sums, all_stats)


def block_softmax(logit_scale, logit_sum, own, forward, back, key_flags):
    rows, width = logit_sum.shape

    def kernel(
        logit_ref, own_ref, forward_ref, back_ref, flag_ref, both_ref, stat_ref, held_ref, sem
    ):
        copy = pltpu.make_async_copy(logit_ref, held_ref, sem)
        copy.start()
        dprob = (
            own_ref[...].astype(jnp.float32)
            + forward_ref[...].astype(jnp.float32)
            + back_ref[...].astype(jnp.float32)
        )
        copy.wait()
        logits = jnp.where(flag_ref[...] > 0, held_ref[...] * logit_scale, -1e30)
        peak = jnp.max(logits, axis=1, keepdims=True)
        lifted = jnp.exp(logits - peak)
        total = jnp.sum(lifted, axis=1, keepdims=True)
        weighted = jnp.sum(lifted * dprob, axis=1, keepdims=True)
        delta = weighted / total
        both_ref[:, :width] = lifted.astype(jnp.bfloat16)
        both_ref[:, width:] = (lifted * (dprob - delta)).astype(jnp.bfloat16)
        for i, column in enumerate((peak, total, weighted, delta)):
            stat_ref[i : i + 1, :] = across(column)
        stat_ref[4:8, :] = jnp.zeros((4, rows), jnp.float32)

    return pl.pallas_call(
        kernel,
        out_shape=(
            jax.ShapeDtypeStruct((rows, 2 * width), jnp.bfloat16),
            jax.ShapeDtypeStruct((8, rows), jnp.float32),
        ),
        in_specs=[pl.BlockSpec(memory_space=pltpu.HBM)] + [WHOLE] * 4,
        scratch_shapes=[pltpu.VMEM((rows, width), jnp.float32), pltpu.SemaphoreType.DMA],
        compiler_params=ROOM,
        name="block_softmax",
    )(
        pltpu.with_memory_space_constraint(logit_sum, pltpu.HBM), own, forward, back, key_flags
    )


def query_grads(logit_scale, place, both, scaling, k_blk, cross_dl, sums, chunks):
    block_rows, width = both.shape[0], both.shape[1] // 2
    rows = block_rows // chunks
    flat_width = k_blk.shape[1]
    tokens = sums.shape[0]
    columns = cross_dl.shape[0] // tokens
    feature = flat_width // columns

    def kernel(place_ref, both_ref, scale_ref, k_ref, dl_ref, sums_ref, p_ref, ds_ref, own_ref, other_ref, dq_ref, held_ref, sems):
        core = place_ref[0]
        copies = []
        for i in range(chunks):
            at = pl.ds(i * rows, rows)
            copies.append(pltpu.make_async_copy(both_ref.at[at], held_ref.at[at], sems.at[i]))
            copies[i].start()
        for i in range(chunks):
            at = slice(i * rows, (i + 1) * rows)
            copies[i].wait()
            weight, offset = upright(scale_ref[i, 0:1, :]), upright(scale_ref[i, 1:2, :])
            lifted = held_ref[at, :width].astype(jnp.float32)
            tilted = held_ref[at, width:].astype(jnp.float32)
            p_ref[at, :] = (lifted * weight).astype(jnp.bfloat16)
            ds_ref[at, :] = ((tilted - lifted * offset) * (weight * logit_scale)).astype(
                jnp.bfloat16
            )
        dq_ref[...] = dot_f32(ds_ref[...], k_ref[...])
        for c in range(columns):
            lanes = slice(c * feature, (c + 1) * feature)
            dq_ref[:, lanes] += dot_f32(
                dl_ref[c * tokens : (c + 1) * tokens, :], sums_ref[:, lanes], LEAD_PAIR
            )
        for x in range(chunks // 2):
            to = slice(x * rows, (x + 1) * rows)
            mine = pl.multiple_of((2 * x + core) * rows, rows)
            theirs = pl.multiple_of((2 * x + 1 - core) * rows, rows)
            own_ref[to, :] = dq_ref[pl.ds(mine, rows), :]
            other_ref[to, :] = dq_ref[pl.ds(theirs, rows), :].astype(jnp.bfloat16)

    return pl.pallas_call(
        kernel,
        in_specs=[SMEM, pl.BlockSpec(memory_space=pltpu.HBM)] + [WHOLE] * 4,
        out_shape=(
            jax.ShapeDtypeStruct((block_rows, width), jnp.bfloat16),
            jax.ShapeDtypeStruct((block_rows, width), jnp.bfloat16),
            jax.ShapeDtypeStruct((block_rows // 2, flat_width), jnp.float32),
            jax.ShapeDtypeStruct((block_rows // 2, flat_width), jnp.bfloat16),
        ),
        scratch_shapes=[
            pltpu.VMEM((block_rows, flat_width), jnp.float32),
            pltpu.VMEM((block_rows, 2 * width), jnp.bfloat16),
            pltpu.SemaphoreType.DMA((chunks,)),
        ],
        compiler_params=ROOM,
        name="query_grads",
    )(place, pltpu.with_memory_space_constraint(both, pltpu.HBM), scaling, k_blk, cross_dl, sums)


def key_grads(prob, dlogit, q_blk, g_blk, dsum, pieces):
    width, flat_width = prob.shape[1], q_blk.shape[1]
    tokens = dsum.shape[0]
    group = width // tokens
    piece = width // pieces

    def kernel(p_ref, ds_ref, q_ref, g_ref, dsum_ref, *out_refs):
        for half, (w_ref, t_ref) in enumerate(((ds_ref, q_ref), (p_ref, g_ref))):
            lanes = slice(half * flat_width, (half + 1) * flat_width)
            grads = dot_f32(w_ref[...], t_ref[...], LEAD_PAIR)
            shared = dsum_ref[:, lanes] / group
            grads = grads.reshape(tokens, group, flat_width) + shared[:, None, :]
            grads = grads.reshape(width, flat_width).astype(jnp.bfloat16)
            for s, out_ref in enumerate(out_refs):
                out_ref[:, lanes] = grads[s * piece : (s + 1) * piece]

    return pl.pallas_call(
        kernel,
        out_shape=tuple(
            jax.ShapeDtypeStruct((piece, 2 * flat_width), jnp.bfloat16) for _ in range(pieces)
        ),
        compiler_params=ROOM,
        name="key_grads",
    )(prob, dlogit, q_blk, g_blk, dsum)


def shards(queries, keys, values, out_grad, row_keep, row_lengths):
    rows_dev, cols_dev, feature = queries.shape
    row_axis, zs = lax.axis_size("row"), lax.axis_size("col")
    ys = row_axis // (2 * XS)
    near_size = 2 * XS
    total_rows = rows_dev * row_axis
    total_cols = cols_dev * zs
    group_rows = total_rows // SUMMARIES
    flat_width = cols_dev * feature
    block_rows = near_size * rows_dev
    block_keys = ys * rows_dev
    tokens = block_keys // group_rows
    near = [[y * near_size + i for i in range(near_size)] for y in range(ys)]
    own_x = (lax.axis_index("row") // 2) % XS
    own_core = lax.axis_index("row") % 2
    own_z = lax.axis_index("col")
    place = jnp.stack([own_core, own_z]).astype(jnp.int32)
    logit_scale = 1.0 / math.sqrt(total_cols * feature)
    inv_root = 1.0 / math.sqrt(feature)

    def at(y, x, core):
        return ((y % ys) * XS + x % XS) * 2 + core

    cells = [(y, x, c) for y in range(ys) for x in range(XS) for c in range(2)]

    def shift_y(table, step):
        return lax.ppermute(table, "row", [(at(y, x, c), at(y + step, x, c)) for y, x, c in cells])

    def shift_x(table, step):
        return lax.ppermute(table, "row", [(at(y, x, c), at(y, x + step, c)) for y, x, c in cells])

    def swap_core(table):
        return lax.ppermute(table, "row", [(at(y, x, c), at(y, x, 1 - c)) for y, x, c in cells])

    def shift_z(table, step):
        return lax.ppermute(table, "col", [(z, (z + step) % zs) for z in range(zs)])

    def share(table, axis, groups=None):
        count = lax.axis_size(axis) if groups is None else len(groups[0])
        copies = jnp.broadcast_to(table[None], (count,) + table.shape)
        return lax.all_to_all(
            copies, axis, split_axis=0, concat_axis=0, tiled=True, axis_index_groups=groups
        )

    own_columns = jnp.where(row_keep == 1, row_lengths, 0) - own_z * cols_dev
    cell_keep = jnp.arange(cols_dev, dtype=jnp.int32)[None, :] < own_columns[:, None]
    keep_flat = jnp.broadcast_to(cell_keep[:, :, None], queries.shape).reshape(
        rows_dev, flat_width
    )
    zero = jnp.zeros((), queries.dtype)

    def masked(table):
        flat = jnp.where(keep_flat, table.reshape(rows_dev, flat_width), zero)
        return with_layout_constraint(flat, Layout((0, 1)))

    def wave(first, second, chained):
        along_x = {s: shift_x(first, s) for s in range(1, XS)}
        late = second
        if chained:
            late, along_x[1] = lax.optimization_barrier((second, along_x[1]))
        along_y = {s: shift_y(late if s == ys - 1 else second, s) for s in range(1, ys)}
        return lax.optimization_barrier(
            (
                [first] + [along_x[s] for s in range(1, XS)],
                [second] + [along_y[s] for s in range(1, ys)],
            )
        )

    def in_line(pieces):
        line = jnp.zeros((XS, rows_dev, flat_width), queries.dtype)
        for s, piece in enumerate(pieces):
            line = lax.dynamic_update_slice(line, piece[None], ((own_x - s) % XS, 0, 0))
        return line

    def both_lines(line, other):
        first = jnp.where(own_core == 0, line, other)
        second = jnp.where(own_core == 0, other, line)
        return jnp.stack([first, second], axis=1).reshape(block_rows, flat_width)

    q_pieces, k_pieces = wave(*lax.optimization_barrier((masked(queries), masked(keys))), True)
    q_line = in_line(q_pieces)
    q_other, keep_flat = lax.optimization_barrier((swap_core(q_line), keep_flat))
    q_blk = both_lines(q_line, q_other)
    k_blk = jnp.concatenate(k_pieces, axis=0)
    logit_piece = dot_f32(q_blk, k_blk, ROW_PAIR)
    flag_rows = jnp.pad(
        row_keep.astype(jnp.bfloat16)[None, :], ((0, FLAG_ROWS - 1), (0, flat_width - rows_dev))
    )
    g_pieces, key_pieces = wave(
        masked(out_grad), jnp.concatenate([masked(values), flag_rows], axis=0), False
    )
    v_blk = jnp.concatenate([p[:rows_dev] for p in key_pieces], axis=0)
    g_line = in_line(g_pieces)
    g_blk = both_lines(g_line, swap_core(g_line))
    g_blk, _ = lax.optimization_barrier((g_blk, logit_piece))
    dprob_piece = dot_f32(g_blk, v_blk, ROW_PAIR).astype(jnp.bfloat16)
    key_flags = jnp.concatenate([p[rows_dev, :rows_dev] for p in key_pieces])[None, :]
    logit_sum = lax.psum_scatter(logit_piece, "col", scatter_dimension=0, tiled=True)

    dprob_chunks = dprob_piece.reshape(zs, block_rows // zs, block_keys)

    back_chunks = lax.optimization_barrier(dprob_chunks)

    def part(step):
        chunks = back_chunks if step < 0 else dprob_chunks
        return lax.dynamic_index_in_dim(chunks, (own_z + step) % zs, axis=0, keepdims=False)

    def passed(step, count):
        moving = part(step * count)
        for left in range(count - 1, -1, -1):
            moving = shift_z(moving, step)
            if left > 0:
                moving = (
                    moving.astype(jnp.float32) + part(step * left).astype(jnp.float32)
                ).astype(jnp.bfloat16)
        return moving

    dprob_forward = passed(1, zs // 2)
    dprob_back = passed(-1, zs - 1 - zs // 2)

    both, stats = block_softmax(
        logit_scale, logit_sum, part(0), dprob_forward, dprob_back, key_flags
    )
    both = lax.all_gather(both, "col", axis=0, tiled=True)

    sums, own_stats = cross_statistics(
        q_blk, g_blk, k_blk, v_blk, stats, tokens, feature, inv_root
    )
    all_stats = share(own_stats, "row", near)
    row_stats = all_stats[:, 3 * cols_dev, : 3 * rows_dev].reshape(near_size, 3, rows_dev)
    peak = jnp.max(row_stats[:, 0], axis=0)
    weight = jnp.exp(row_stats[:, 0] - peak)
    total = jnp.sum(weight * row_stats[:, 1], axis=0)
    delta = jnp.sum(weight * row_stats[:, 2], axis=0) / total
    scaling = share(jnp.stack([jnp.exp(stats[0] - peak) / total, delta - stats[3]]), "col")
    cross_dl, dsum = cross_grads(q_blk, g_blk, sums, all_stats, feature, inv_root)
    both, scaling, cross_dl, dsum = lax.optimization_barrier((both, scaling, cross_dl, dsum))

    prob, dlogit, dq_own, dq_other = query_grads(
        logit_scale, place, both, scaling, k_blk, cross_dl, sums, zs
    )
    dq_swapped = swap_core(dq_other)
    key_parts = key_grads(prob, dlogit, q_blk, g_blk, dsum, ys)
    key_moved = [shift_y(key_parts[s], -s) for s in range(1, ys)]
    line = (dq_own + dq_swapped.astype(jnp.float32)).astype(jnp.bfloat16)
    line = line.reshape(XS, rows_dev, flat_width)
    lines = [[at(y, x, c) for x in range(XS)] for y in range(ys) for c in range(2)]
    line = lax.all_to_all(
        line, "row", split_axis=0, concat_axis=0, tiled=True, axis_index_groups=lines
    )

    def added(parts):
        return sum(p.astype(jnp.float32) for p in parts)

    grad_q = added([line[x] for x in range(XS)])
    def finished(rows):
        return (
            jnp.where(keep_flat, rows, 0.0)
            .astype(jnp.bfloat16)
            .reshape(rows_dev, cols_dev, feature)
        )

    grad_q = finished(grad_q)
    grad_kv = added([key_parts[0]] + key_moved)
    return (grad_q, finished(grad_kv[:, :flat_width]), finished(grad_kv[:, flat_width:]))


def solution(mesh):
    return jax.shard_map(
        shards,
        mesh=mesh,
        in_specs=(
            P("row", "col", None),
            P("row", "col", None),
            P("row", "col", None),
            P("row", "col", None),
            P("row"),
            P("row"),
        ),
        out_specs=(P("row", "col", None), P("row", "col", None), P("row", "col", None)),
        check_vma=False,
    )
```
